32 devices in a mesh: section: 2 (over core), experts: 4 (over z), dp: 4 (over y, x).
Axes of the slice: x: 2, y: 2, z: 4, core: 2. Of those that a mesh axis runs over, the one named last changes fastest.
Arguments:
- tokens: bfloat16 [6304, 768], P(('experts', 'dp')), may hold values from -6 to 6
- cotangent: bfloat16 [6304, 768], P(('experts', 'dp')), may hold values from -6 to 6
- norm_gains: float32 [2, 2, 768], P('section'), may hold values from 0.5 to 1.5
- norm_biases: float32 [2, 2, 768], P('section'), may hold values from -1.5 to 1.5
- qkv_weight: bfloat16 [2, 768, 2304], P('section'), may hold values from -4 to 4
- out_weight: bfloat16 [2, 768, 768], P('section'), may hold values from -1.5 to 1.5
- dense_in: bfloat16 [768, 3072], replicated, may hold values from -0.21875 to 0.21875
- dense_out: bfloat16 [3072, 768], replicated, may hold values from -0.109375 to 0.109375
- expert_in: bfloat16 [4, 768, 3072], P('experts', None, 'dp'), may hold values from -0.21875 to 0.21875
- expert_out: bfloat16 [4, 3072, 768], P('experts', 'dp'), may hold values from -0.109375 to 0.109375
- routes: int32 [6304, 2], P(('experts', 'dp')), may hold values from 0 to 3, all different within a row
- gates: float32 [6304, 2], P(('experts', 'dp')), may hold values from 0.1 to 0.6
Outputs:
- acts: bfloat16 [2, 6304, 768], P('section', ('experts', 'dp'))
- act_grads: float32 [2, 6304, 768], P('section', ('experts', 'dp'))
- qkv_grad: float32 [2, 768, 2304], P('section', ('experts', 'dp'))
- out_grad: float32 [2, 768, 768], P('section', ('experts', 'dp'))
- gain_grad: float32 [2, 2, 768], P('section', None, ('experts', 'dp'))
- bias_grad: float32 [2, 2, 768], P('section', None, ('experts', 'dp'))
- dense_in_grad: float32 [768, 3072], P(('experts', 'dp'), 'section')
- dense_out_grad: float32 [3072, 768], P(('experts', 'dp'), 'section')
- expert_in_grad: float32 [4, 768, 3072], P('experts', 'section', 'dp')
- expert_out_grad: float32 [4, 3072, 768], P('experts', 'dp', 'section')
The draws below stay inside these ranges and needn't reach their ends.
Inputs may be any that keep to these rules, and one draw needn't show every extreme that they name: `routes`: each row names two different experts, and every expert is named by some row.
All inputs are finite; a program needn't handle non-finite values.
Results may differ from the reference program's by a relative error of at most 0.015.
The reference program's roundings to bfloat16 on the way count: a program that leaves them out, or rounds other values in their place, can miss the bound.
Values may be sent and summed in bfloat16 or wider, within the bound.
A program may use at most 448 MiB of HBM per device.

```python
import math
import jax
import jax.numpy as jnp
from jax import lax

D = 768
HEADS = 12
HEAD_DIM = 64
FF = 3072
SEQ = 197
ROWS = 197
TOKENS = 6304
EXPERTS = 4
CAP = 98


def draw_qkv_weight(key, part):
    base_key = jax.random.fold_in(jax.random.fold_in(key, 17), 0)
    weights = jax.random.normal(base_key, (2, D, 3 * D), jnp.float32) / math.sqrt(D)
    return jnp.clip(weights, -4.0, 4.0).astype(jnp.bfloat16)


def shard_levels(key, extent, shards, smallest, high):
    level, own = 1.0, jax.random.fold_in(key, 6)
    for axis_at, blocks in shards:
        heights = jnp.exp(jax.random.uniform(jax.random.fold_in(own, axis_at), (blocks,), jnp.float32, smallest / len(shards), high / len(shards)))
        level = level * jnp.repeat(heights, extent[axis_at] // blocks).reshape([-1 if axis == axis_at else 1 for axis in range(len(extent))])
    return level


def distinct(key, rows, amount, top, lift):
    ranking = jax.random.permutation(jax.random.fold_in(key, 1), amount)
    boost = ranking
    for power in range(3):
        boost = boost * boost // amount
    boost = boost * lift // amount
    tickets = jax.random.randint(jax.random.fold_in(key, 2), (rows, amount), 0, 4096) + boost
    sure = jax.random.permutation(jax.random.fold_in(key, 3), rows)[jnp.arange(amount) % rows]
    tickets = jnp.where(jnp.arange(rows)[:, None] == sure[None, :], 1 << 14, tickets)
    merit = tickets * amount + jnp.arange(amount)
    return lax.top_k(merit.astype(jnp.int32), top)[1].astype(jnp.int32)


def gaussian(own_key, shape, width, most, cuts=(), kind=jnp.bfloat16):
    array = width * jax.random.normal(own_key, shape, jnp.float32)
    if cuts:
        array = array * shard_levels(own_key, shape, cuts, -0.22, 0.18)
    return jnp.clip(array, -most, most).astype(kind)


def setup_inputs(seed: int = 0) -> dict:
    arg_keys = jax.random.split(jax.random.key(seed), 13)
    return {
        "tokens": gaussian(arg_keys[0], (TOKENS, D), 1.0, 6.0, ((0, 16),)),
        "cotangent": gaussian(arg_keys[1], (TOKENS, D), 1.0, 6.0, ((0, 16),)),
        "norm_gains": jnp.clip(1.0 + 0.1 * jax.random.normal(arg_keys[2], (2, 2, D), jnp.float32), 0.5, 1.5),
        "norm_biases": gaussian(arg_keys[3], (2, 2, D), 0.3, 1.5, ((0, 2),), jnp.float32),
        "qkv_weight": draw_qkv_weight(jax.random.fold_in(arg_keys[12], 71), 0),
        "out_weight": gaussian(arg_keys[5], (2, D, D), (max(2, 4 * D // SEQ)) ** -0.5, 1.5, ((0, 2),)),
        "dense_in": gaussian(arg_keys[6], (D, FF), D ** -0.5, 0.21875),
        "dense_out": gaussian(arg_keys[7], (FF, D), FF ** -0.5, 0.109375),
        "expert_in": gaussian(arg_keys[8], (EXPERTS, D, FF), D ** -0.5, 0.21875, ((0, 4), (2, 4))),
        "expert_out": gaussian(arg_keys[9], (EXPERTS, FF, D), FF ** -0.5, 0.109375, ((0, 4), (1, 4))),
        "routes": distinct(arg_keys[10], TOKENS, EXPERTS, 2, 8192),
        "gates": jnp.clip(0.1 + 0.5 * jax.random.uniform(arg_keys[11], (TOKENS, 2), jnp.float32) ** shard_levels(arg_keys[11], (TOKENS, 2), ((0, 16),), -0.2, 0.2), 0.1, 0.6),
    }


eps = 1e-06

def layer_norm(values, gain, bias):
    centred = values - lax.optimization_barrier(jnp.mean(values, axis=-1, keepdims=True))
    spread = lax.optimization_barrier(jnp.mean(centred * centred, axis=-1, keepdims=True))
    return centred * lax.rsqrt(spread + eps) * gain + bias

def norm_back(values, gain, bias, cotan):
    _, pull = jax.vjp(layer_norm, values, gain, bias)
    return pull(cotan)

def gelu_back(before, cotan):
    _, pull = jax.vjp(jax.nn.gelu, before)
    return pull(cotan)[0]

def matmul(left, right):
    return jnp.dot(left, right, preferred_element_type=jnp.float32)

def matmul_rows(left, right):
    return jnp.dot(left.T, right, preferred_element_type=jnp.float32)

def matmul_cols(left, right):
    return jnp.dot(left, right.T, preferred_element_type=jnp.float32)

def widen(values):
    return lax.optimization_barrier(values).astype(jnp.float32)

def head_split(mixed):
    return widen(mixed).reshape(-1, SEQ, 3, HEADS, HEAD_DIM)

def score_table(split):
    return jnp.einsum('bqhd,bkhd->bhqk', split[:, :, 0], split[:, :, 1]) * HEAD_DIM ** (-0.5)

def attend(normed, weight_qkv):
    mixed = matmul(normed, weight_qkv).astype(jnp.bfloat16)
    split = head_split(mixed)
    scores = score_table(split)
    top = lax.optimization_barrier(jnp.max(scores, axis=-1, keepdims=True))
    logsum = top + jnp.log(lax.optimization_barrier(jnp.sum(jnp.exp(scores - top), axis=-1, keepdims=True)))
    probs = widen(jnp.exp(scores - logsum).astype(jnp.bfloat16))
    attended = jnp.einsum('bhqk,bkhd->bqhd', probs, split[:, :, 2])
    return (mixed, logsum, attended.reshape(normed.shape[0], D).astype(jnp.bfloat16))

def attend_back(normed, mixed, logsum, attended, grad_hidden, weight_qkv, weight_out):
    grad_cast = grad_hidden.astype(jnp.bfloat16)
    grad_wout = matmul_rows(attended, grad_cast)
    grad_att = matmul_cols(grad_cast, weight_out).astype(jnp.bfloat16)
    split = head_split(mixed)
    probs_full = jnp.exp(score_table(split) - logsum)
    probs = widen(probs_full.astype(jnp.bfloat16))
    grad_heads = widen(grad_att).reshape(-1, SEQ, HEADS, HEAD_DIM)
    grad_probs = jnp.einsum('bqhd,bkhd->bhqk', grad_heads, split[:, :, 2])
    grad_value = jnp.einsum('bhqk,bqhd->bkhd', probs, grad_heads)
    inner = lax.optimization_barrier(jnp.sum(probs_full * grad_probs, axis=-1, keepdims=True))
    grad_scores = widen((probs_full * (grad_probs - inner) * HEAD_DIM ** (-0.5)).astype(jnp.bfloat16))
    grad_query = jnp.einsum('bhqk,bkhd->bqhd', grad_scores, split[:, :, 1])
    grad_key = jnp.einsum('bhqk,bqhd->bkhd', grad_scores, split[:, :, 0])
    grad_mixed = jnp.stack([grad_query, grad_key, grad_value], axis=2).reshape(normed.shape[0], 3 * D).astype(jnp.bfloat16)
    return (matmul_cols(grad_mixed, weight_qkv), matmul_rows(normed, grad_mixed), grad_wout)

def front_half(block_in, gains, biases, weight_qkv, weight_out):
    start = block_in.astype(jnp.float32)
    normed = layer_norm(start, gains[0], biases[0]).astype(jnp.bfloat16)
    mixed, logsum, attended = attend(normed, weight_qkv)
    hidden = start + matmul(attended, weight_out)
    second = layer_norm(hidden, gains[1], biases[1]).astype(jnp.bfloat16)
    return (normed, mixed, logsum, attended, hidden, second)

def front_back(block_in, saved, grad_top, grad_second, gains, biases, weight_qkv, weight_out):
    normed, mixed, logsum, attended, hidden = saved
    grad_mid, gain_two, bias_two = norm_back(hidden, gains[1], biases[1], grad_second)
    grad_hidden = grad_top + grad_mid
    grad_normed, grad_wqkv, grad_wout = attend_back(normed, mixed, logsum, attended, grad_hidden, weight_qkv, weight_out)
    grad_start, gain_one, bias_one = norm_back(block_in.astype(jnp.float32), gains[0], biases[0], grad_normed)
    return (grad_start + grad_hidden, grad_wqkv, grad_wout, jnp.stack([gain_one, gain_two]), jnp.stack([bias_one, bias_two]))

def route(chosen):
    flat = jnp.concatenate([chosen[:, 0], chosen[:, 1]]).astype(jnp.int32)
    table = (flat[:, None] == jnp.arange(EXPERTS, dtype=jnp.int32)[None, :]).astype(jnp.int32)
    place = lax.optimization_barrier(jnp.sum((jnp.cumsum(table, axis=0, dtype=jnp.int32) - table) * table, axis=1, dtype=jnp.int32))
    kept = place < CAP
    slot = jnp.where(kept, flat * CAP + place, EXPERTS * CAP).astype(jnp.int32)
    return (slot, kept)

def place_rows(values, slot):
    return jnp.zeros((EXPERTS * CAP, D), jnp.bfloat16).at[slot].set(values, mode='drop')

def pick_rows(buffer, slot, kept, factor):
    picked = jnp.take(buffer, jnp.where(kept, slot, 0).astype(jnp.int32), axis=0).astype(jnp.float32) * factor[:, None]
    return picked[:ROWS] + picked[ROWS:]

def expert_pass(inputs):
    rows_in, grad_rows, weight_in, weight_back = inputs
    before = matmul(rows_in, weight_in)
    active = jax.nn.gelu(before).astype(jnp.bfloat16)
    returned = matmul(active, weight_back).astype(jnp.bfloat16)
    grad_active = matmul_cols(grad_rows, weight_back)
    grad_back = matmul_rows(active, grad_rows)
    grad_before = gelu_back(before, grad_active).astype(jnp.bfloat16)
    grad_in = matmul_rows(rows_in, grad_before)
    grad_input = matmul_cols(grad_before, weight_in).astype(jnp.bfloat16)
    return (returned, grad_input, grad_in, grad_back)

def reference(tokens, cotangent, norm_gains, norm_biases, qkv_weight, out_weight, dense_in, dense_out, expert_in, expert_out, routes, gates):
    blocks = TOKENS // ROWS
    gain_all = norm_gains.astype(jnp.float32)
    bias_all = norm_biases.astype(jnp.float32)
    token_blocks = tokens.reshape(blocks, ROWS, D)
    grad_blocks = cotangent.reshape(blocks, ROWS, D)
    route_blocks = routes.reshape(blocks, ROWS, 2)
    gate_blocks = gates.reshape(blocks, ROWS, 2)

    def first_forward(block_in):
        outs = front_half(block_in, gain_all[0], bias_all[0], qkv_weight[0], out_weight[0])
        active = jax.nn.gelu(matmul(outs[5], dense_in)).astype(jnp.bfloat16)
        return (outs[4] + matmul(active, dense_out)).astype(jnp.bfloat16)
    middle = lax.map(first_forward, token_blocks)

    def second_front(inputs):
        block_in, chosen, gate_pair, grad_block = inputs
        second = front_half(block_in, gain_all[1], bias_all[1], qkv_weight[1], out_weight[1])[5]
        slot, kept = route(chosen)
        gate_flat = jnp.concatenate([gate_pair[:, 0], gate_pair[:, 1]])
        grad_top = grad_block.astype(jnp.float32)
        grad_sent = (jnp.concatenate([grad_top, grad_top]) * gate_flat[:, None]).astype(jnp.bfloat16)
        return (place_rows(jnp.concatenate([second, second]), slot), place_rows(grad_sent, slot))
    outgoing, grad_outgoing = lax.map(second_front, (middle, route_blocks, gate_blocks, grad_blocks))

    def by_expert(values):
        return jnp.swapaxes(values.reshape(blocks, EXPERTS, CAP, D), 0, 1).reshape(EXPERTS, blocks * CAP, D)

    def by_block(values):
        return jnp.swapaxes(values.reshape(EXPERTS, blocks, CAP, D), 0, 1).reshape(blocks, EXPERTS * CAP, D)
    returned, grad_returned, expert_in_grad, expert_out_grad = lax.map(expert_pass, (by_expert(outgoing), by_expert(grad_outgoing), expert_in, expert_out))

    def second_back(carry, inputs):
        block_in, chosen, gate_pair, grad_block, back_home, grad_home = inputs
        normed, mixed, logsum, attended, hidden, second = front_half(block_in, gain_all[1], bias_all[1], qkv_weight[1], out_weight[1])
        slot, kept = route(chosen)
        gate_flat = jnp.concatenate([gate_pair[:, 0], gate_pair[:, 1]])
        final = hidden + pick_rows(back_home, slot, kept, jnp.where(kept, gate_flat, 0.0))
        grad_second = pick_rows(grad_home, slot, kept, kept.astype(jnp.float32))
        grad_start, grad_wqkv, grad_wout, grad_gain, grad_bias = front_back(block_in, (normed, mixed, logsum, attended, hidden), grad_block.astype(jnp.float32), grad_second, gain_all[1], bias_all[1], qkv_weight[1], out_weight[1])
        carry = (carry[0] + grad_wqkv, carry[1] + grad_wout, carry[2] + grad_gain, carry[3] + grad_bias)
        return (carry, (final.astype(jnp.bfloat16), grad_start))
    shared_zero = (jnp.zeros((D, 3 * D), jnp.float32), jnp.zeros((D, D), jnp.float32), jnp.zeros((2, D), jnp.float32), jnp.zeros((2, D), jnp.float32))
    second_sums, (final, grad_middle) = lax.scan(second_back, shared_zero, (middle, route_blocks, gate_blocks, grad_blocks, by_block(returned), by_block(grad_returned)))

    def first_back(carry, inputs):
        block_in, grad_block = inputs
        normed, mixed, logsum, attended, hidden, second = front_half(block_in, gain_all[0], bias_all[0], qkv_weight[0], out_weight[0])
        before = matmul(second, dense_in)
        active = jax.nn.gelu(before).astype(jnp.bfloat16)
        grad_result = grad_block.astype(jnp.bfloat16)
        grad_back = matmul_rows(active, grad_result)
        grad_before = gelu_back(before, matmul_cols(grad_result, dense_out)).astype(jnp.bfloat16)
        grad_in = matmul_rows(second, grad_before)
        grad_second = matmul_cols(grad_before, dense_in)
        grad_start, grad_wqkv, grad_wout, grad_gain, grad_bias = front_back(block_in, (normed, mixed, logsum, attended, hidden), widen(grad_result), grad_second, gain_all[0], bias_all[0], qkv_weight[0], out_weight[0])
        carry = (carry[0] + grad_wqkv, carry[1] + grad_wout, carry[2] + grad_gain, carry[3] + grad_bias, carry[4] + grad_in, carry[5] + grad_back)
        return (carry, grad_start)
    first_zero = shared_zero + (jnp.zeros((D, FF), jnp.float32), jnp.zeros((FF, D), jnp.float32))
    first_sums, grad_tokens = lax.scan(first_back, first_zero, (token_blocks, grad_middle))
    acts = jnp.stack([middle.reshape(TOKENS, D), final.reshape(TOKENS, D)])
    act_grads = jnp.stack([grad_tokens.reshape(TOKENS, D), grad_middle.reshape(TOKENS, D)])
    qkv_grad = jnp.stack([first_sums[0], second_sums[0]])
    out_grad = jnp.stack([first_sums[1], second_sums[1]])
    gain_grad = jnp.stack([first_sums[2], second_sums[2]])
    bias_grad = jnp.stack([first_sums[3], second_sums[3]])
    return (acts, act_grads, qkv_grad, out_grad, gain_grad, bias_grad, first_sums[4], first_sums[5], expert_in_grad, expert_out_grad)
```

```python
import jax
import jax.numpy as jnp
from jax import lax
from jax.sharding import PartitionSpec as P

HEADS = 12
HEAD_DIM = 64
SEQ = 197


eps = 1e-06


def pair(block):
    return lax.ppermute(block, "section", [(0, 1), (1, 0)])


def layer_norm(values, gain, bias):
    centred = values - jnp.mean(values, axis=-1, keepdims=True)
    spread = jnp.mean(centred * centred, axis=-1, keepdims=True)
    return centred * lax.rsqrt(spread + eps) * gain + bias


def norm_back(values, gain, bias, cotan):
    _, pull = jax.vjp(layer_norm, values, gain, bias)
    return pull(cotan)


def gelu_back(before, cotan):
    _, pull = jax.vjp(jax.nn.gelu, before)
    return pull(cotan)[0]


def matmul(left, right):
    return jnp.dot(left, right, preferred_element_type=jnp.float32)


def matmul_rows(left, right):
    return lax.dot_general(
        left, right, (((0,), (0,)), ((), ())), preferred_element_type=jnp.float32
    )


def matmul_cols(left, right):
    return lax.dot_general(
        left, right, (((1,), (1,)), ((), ())), preferred_element_type=jnp.float32
    )


def head_split(mixed):
    return mixed.reshape(-1, SEQ, 3, HEADS, HEAD_DIM)


def score_table(split):
    return jnp.einsum(
        "bqhd,bkhd->bhqk", split[:, :, 0], split[:, :, 1], preferred_element_type=jnp.float32
    ) * HEAD_DIM ** (-0.5)


def attend(normed, weight_qkv):
    mixed = matmul(normed, weight_qkv).astype(jnp.bfloat16)
    split = head_split(mixed)
    scores = score_table(split)
    top = jnp.max(scores, axis=-1, keepdims=True)
    logsum = top + jnp.log(jnp.sum(jnp.exp(scores - top), axis=-1, keepdims=True))
    probs = jnp.exp(scores - logsum).astype(jnp.bfloat16)
    attended = jnp.einsum(
        "bhqk,bkhd->bqhd", probs, split[:, :, 2], preferred_element_type=jnp.float32
    )
    return (mixed, logsum, attended.reshape(normed.shape[0], -1).astype(jnp.bfloat16))


def attend_back(normed, mixed, logsum, attended, grad_hidden, weight_qkv, weight_out):
    grad_cast = grad_hidden.astype(jnp.bfloat16)
    grad_att = matmul_cols(grad_cast, weight_out).astype(jnp.bfloat16)
    split = head_split(mixed)
    probs_full = jnp.exp(score_table(split) - logsum)
    probs = probs_full.astype(jnp.bfloat16)
    grad_heads = grad_att.reshape(-1, SEQ, HEADS, HEAD_DIM)
    grad_probs = jnp.einsum(
        "bqhd,bkhd->bhqk", grad_heads, split[:, :, 2], preferred_element_type=jnp.float32
    )
    grad_value = jnp.einsum(
        "bhqk,bqhd->bkhd", probs, grad_heads, preferred_element_type=jnp.float32
    )
    inner = jnp.sum(probs_full * grad_probs, axis=-1, keepdims=True)
    grad_scores = (probs_full * (grad_probs - inner) * HEAD_DIM ** (-0.5)).astype(jnp.bfloat16)
    grad_query = jnp.einsum(
        "bhqk,bkhd->bqhd", grad_scores, split[:, :, 1], preferred_element_type=jnp.float32
    )
    grad_key = jnp.einsum(
        "bhqk,bqhd->bkhd", grad_scores, split[:, :, 0], preferred_element_type=jnp.float32
    )
    grad_mixed = (
        jnp.stack([grad_query, grad_key, grad_value], axis=2)
        .reshape(normed.shape[0], -1)
        .astype(jnp.bfloat16)
    )
    return (matmul_cols(grad_mixed, weight_qkv), grad_mixed, grad_cast)


def front_half(block_in, gains, biases, weight_qkv, weight_out):
    start = block_in.astype(jnp.float32)
    normed = layer_norm(start, gains[0], biases[0]).astype(jnp.bfloat16)
    mixed, logsum, attended = attend(normed, weight_qkv)
    hidden = start + matmul(attended, weight_out)
    second = layer_norm(hidden, gains[1], biases[1]).astype(jnp.bfloat16)
    return (normed, mixed, logsum, attended, hidden, second)


def front_back(block_in, saved, grad_top, grad_second, gains, biases, weight_qkv, weight_out):
    normed, mixed, logsum, attended, hidden = saved
    grad_mid, gain_two, bias_two = norm_back(hidden, gains[1], biases[1], grad_second)
    grad_hidden = grad_top + grad_mid
    grad_normed, grad_mixed, grad_cast = attend_back(
        normed, mixed, logsum, attended, grad_hidden, weight_qkv, weight_out
    )
    grad_start, gain_one, bias_one = norm_back(
        block_in.astype(jnp.float32), gains[0], biases[0], grad_normed
    )
    return (
        grad_start + grad_hidden,
        jnp.stack([gain_one, gain_two, bias_one, bias_two]),
        grad_mixed,
        grad_cast,
    )


def rounded(values):
    return lax.reduce_precision(values, exponent_bits=8, mantissa_bits=7).astype(jnp.bfloat16)


def on_device(
    tokens,
    cotangent,
    norm_gains,
    norm_biases,
    qkv_weight,
    out_weight,
    dense_in,
    dense_out,
    expert_in,
    expert_out,
    routes,
    gates,
):
    rows = SEQ
    width = tokens.shape[1]
    experts = lax.axis_size("experts")
    shards = lax.axis_size("dp")
    capacity = 2 * rows // experts
    padded = -(-capacity // 8) * 8
    slots = experts * padded
    section = lax.axis_index("section")
    group = lax.axis_index("experts")
    shard = lax.axis_index("dp")
    first = section == 0

    def ordered(mine, other, axis):
        return jnp.concatenate(
            [jnp.where(first, mine, other), jnp.where(first, other, mine)], axis=axis
        )

    def kept_half(array, axis):
        low, high = jnp.split(array, 2, axis=axis)
        return jnp.where(first, low, high)

    def sent_half(array, axis):
        low, high = jnp.split(array, 2, axis=axis)
        return jnp.where(first, high, low)

    def both(own):
        other = pair(own)
        return (jnp.where(first, own, other), jnp.where(first, other, own))

    def across(array, mask):
        return lax.ppermute(array, "dp", [(i, i ^ mask) for i in range(shards)])

    def shifted(array, step):
        return lax.ppermute(
            array, "experts", [(i, (i + step) % experts) for i in range(experts)]
        )

    def wide(array):
        return array.astype(jnp.float32)

    def shard_sum(block, near, far):
        passed = across(block(3).astype(jnp.bfloat16), near)
        direct = across(block(near).astype(jnp.bfloat16), near)
        turned = across((block(far) + wide(passed)).astype(jnp.bfloat16), far)
        return block(0) + wide(direct) + wide(turned)

    def group_sum(array):
        own = lax.dynamic_index_in_dim(array, group, 0, False)
        total = wide(own)
        for step in range(1, experts):
            target = lax.rem(group + step, experts)
            total = total + wide(
                shifted(lax.dynamic_index_in_dim(array, target, 0, False), step)
            )
        return total

    def everyone_sum(left, right, near, far):
        blocks = left.reshape(experts, shards, -1, left.shape[1])

        def block(mask):
            part = lax.dynamic_index_in_dim(blocks, shard ^ mask, 1, False)
            return matmul(part.reshape(-1, left.shape[1]), right)

        total = shard_sum(block, near, far).astype(jnp.bfloat16)
        return group_sum(total.reshape(experts, -1, right.shape[1]))

    def padded_rows(array):
        return jnp.pad(array, ((0, -array.shape[0] % 256), (0, 0)))

    def joined(own, other):
        return jnp.concatenate([padded_rows(own), padded_rows(other)], axis=0)

    def joined_left(array):
        return joined(array, pair(array)).T

    def joined_right(array):
        return joined(kept_half(array, 1), pair(sent_half(array, 1)))

    qkv_zero, qkv_one = both(qkv_weight[0])
    norms_zero, norms_one = both(jnp.concatenate([norm_gains[0], norm_biases[0]], axis=0))
    out_zero, out_one = both(out_weight[0])

    def own_block(array):
        return lax.dynamic_slice_in_dim(array, section * rows, rows, 0)

    block_in = own_block(tokens)
    grad_top = own_block(cotangent).astype(jnp.float32)
    chosen = own_block(routes)
    gate_pair = own_block(gates)

    flat = jnp.concatenate([chosen[:, 0], chosen[:, 1]])
    order = jnp.arange(2 * rows, dtype=jnp.int32)
    place = jnp.sum(
        ((flat[:, None] == flat[None, :]) & (order[None, :] < order[:, None])).astype(jnp.int32),
        axis=1,
        dtype=jnp.int32,
    )
    step_of = lax.rem(flat - group + experts, experts)
    slot = jnp.where(place < capacity, step_of * padded + place, slots)
    gate_flat = jnp.concatenate([gate_pair[:, 0], gate_pair[:, 1]])
    spread = (jnp.arange(slots, dtype=jnp.int32)[:, None] == slot[None, :]).astype(jnp.bfloat16)
    spread_both = spread[:, :rows] + spread[:, rows:]

    def sent_out(array):
        parts = [array[k * padded : (k + 1) * padded] for k in range(experts)]
        return jnp.concatenate([parts[0]] + [shifted(parts[k], k) for k in range(1, experts)])

    def sent_home(array):
        parts = [array[k * padded : (k + 1) * padded] for k in range(experts)]
        return jnp.concatenate(
            [parts[0]] + [shifted(parts[k], experts - k) for k in range(1, experts)]
        )

    doubled = (jnp.concatenate([grad_top, grad_top]) * gate_flat[:, None]).astype(jnp.bfloat16)
    grad_rows = sent_out(matmul(spread, doubled).astype(jnp.bfloat16))

    piece_in = kept_half(expert_in[0], 1)
    piece_back = kept_half(expert_out[0], 0)
    near_in = jnp.concatenate(
        [piece_in] + [across(piece_in, mask) for mask in range(1, shards)], axis=1
    )
    near_back = jnp.concatenate(
        [piece_back] + [across(piece_back, mask) for mask in range(1, shards)], axis=0
    )
    weights_in = (near_in, pair(near_in))
    weights_back = (near_back, pair(near_back))

    normed0, mixed0, logsum0, attended0, hidden0, second0 = front_half(
        block_in, norms_zero[:2], norms_zero[2:], qkv_zero, out_zero
    )
    before0 = matmul(second0, dense_in)
    active0 = jax.nn.gelu(before0).astype(jnp.bfloat16)
    middle = rounded(hidden0 + matmul(active0, dense_out))

    normed1, mixed1, logsum1, attended1, hidden1, second1 = front_half(
        middle, norms_one[:2], norms_one[2:], qkv_one, out_one
    )
    rows_in = sent_out(matmul(spread_both, second1).astype(jnp.bfloat16))

    before1 = [matmul(rows_in, weight) for weight in weights_in]
    active1 = [jax.nn.gelu(before).astype(jnp.bfloat16) for before in before1]
    grad_before1 = [
        gelu_back(before, matmul_cols(grad_rows, weight)).astype(jnp.bfloat16)
        for before, weight in zip(before1, weights_back)
    ]
    grad_arrived = (
        matmul_cols(grad_before1[0], weights_in[0]) + matmul_cols(grad_before1[1], weights_in[1])
    ).astype(jnp.bfloat16)
    grad_home = sent_home(grad_arrived)
    returned = (
        matmul(active1[0], weights_back[0]) + matmul(active1[1], weights_back[1])
    ).astype(jnp.bfloat16)
    returned_home = sent_home(returned)

    def expert_sums(halves, right):
        landed = [pair(half) for half in halves]
        lefts = [
            jnp.concatenate([halves[0], landed[1]], axis=0),
            jnp.concatenate([halves[1], landed[0]], axis=0),
        ]
        right = jnp.concatenate([kept_half(right, 1), pair(sent_half(right, 1))], axis=0)
        sums = []
        for left, (near, far) in zip(lefts, ((1, 2), (2, 1))):
            size = left.shape[1] // shards

            def block(mask, left=left, size=size):
                return matmul_rows(left[:, mask * size : (mask + 1) * size], right)

            sums.append(shard_sum(block, near, far))
        return ordered(sums[0], sums[1], 0)

    expert_in_sum = expert_sums(grad_before1, rows_in)
    expert_out_sum = expert_sums(active1, grad_rows)

    picked = matmul_rows(spread, returned_home) * gate_flat[:, None]
    final = (hidden1 + (picked[:rows] + picked[rows:])).astype(jnp.bfloat16)
    grad_second1 = matmul_rows(spread_both, grad_home)
    grad_middle, grad_norm1, grad_mixed1, grad_cast1 = front_back(
        middle,
        (normed1, mixed1, logsum1, attended1, hidden1),
        grad_top,
        grad_second1,
        norms_one[:2],
        norms_one[2:],
        qkv_one,
        out_one,
    )

    def shared_sums(normed, attended, grad_mixed, grad_cast):
        normed_left = joined_left(normed)
        right = joined_right(grad_mixed)
        cut = grad_cast.shape[1]
        return jnp.concatenate(
            [
                everyone_sum(normed_left, right[:, :cut], 1, 2),
                everyone_sum(normed_left, right[:, cut:], 2, 1),
                everyone_sum(joined_left(attended), joined_right(grad_cast), 2, 1),
            ],
            axis=1,
        ).astype(jnp.bfloat16)

    shared1 = shared_sums(normed1, attended1, grad_mixed1, grad_cast1)

    grad_result = rounded(grad_middle)
    dense_out_sum = everyone_sum(joined_left(active0), joined_right(grad_result), 1, 2)
    grad_before0 = gelu_back(before0, matmul_cols(grad_result, dense_out)).astype(jnp.bfloat16)
    dense_in_sum = everyone_sum(joined_left(second0), joined_right(grad_before0), 2, 1)
    grad_tokens, grad_norm0, grad_mixed0, grad_cast0 = front_back(
        block_in,
        (normed0, mixed0, logsum0, attended0, hidden0),
        grad_result.astype(jnp.float32),
        matmul_cols(grad_before0, dense_in),
        norms_zero[:2],
        norms_zero[2:],
        qkv_zero,
        out_zero,
    )
    shared0 = shared_sums(normed0, attended0, grad_mixed0, grad_cast0)

    norm_pair = jnp.where(first, grad_norm0, grad_norm1) + pair(
        jnp.where(first, grad_norm1, grad_norm0)
    )
    norm_parts = jnp.swapaxes(norm_pair.reshape(4, experts, shards, -1), 0, 2)
    for mask in (1, 2):
        kept = lax.bitwise_and(shard, mask) // mask
        halves = norm_parts.reshape(-1, 2, *norm_parts.shape[1:]) if mask == 1 else norm_parts[None]
        norm_parts = lax.dynamic_index_in_dim(halves, kept, 1, False) + across(
            lax.dynamic_index_in_dim(halves, 1 - kept, 1, False), mask
        )
    norm_sum = group_sum(norm_parts[0])

    own_shared = jnp.where(first, shared0, shared1)
    other_shared = pair(jnp.where(first, shared1, shared0))
    cut = qkv_weight.shape[2] // 2
    qkv_sum = ordered(own_shared[:, :cut], other_shared[:, :cut], 1).astype(jnp.float32)
    out_sum = ordered(own_shared[:, cut:], other_shared[:, cut:], 1).astype(jnp.float32)
    acts = ordered(
        jnp.where(first, middle, final), pair(jnp.where(first, final, middle)), 0
    )
    act_grads = ordered(
        jnp.where(first, grad_tokens, grad_middle),
        pair(jnp.where(first, grad_middle, grad_tokens)),
        0,
    )
    return (
        acts[None],
        act_grads[None],
        qkv_sum[None],
        out_sum[None],
        norm_sum[:2][None],
        norm_sum[2:][None],
        dense_in_sum,
        dense_out_sum,
        expert_in_sum.T[None],
        expert_out_sum[None],
    )


def solution(mesh):
    placed = (
        P(("experts", "dp"), None),
        P(("experts", "dp"), None),
        P("section", None, None),
        P("section", None, None),
        P("section", None, None),
        P("section", None, None),
        P(),
        P(),
        P("experts", None, "dp"),
        P("experts", "dp", None),
        P(("experts", "dp"), None),
        P(("experts", "dp"), None),
    )
    return jax.shard_map(
        on_device,
        mesh=mesh,
        in_specs=placed,
        out_specs=(
            P("section", ("experts", "dp"), None),
            P("section", ("experts", "dp"), None),
            P("section", ("experts", "dp"), None),
            P("section", ("experts", "dp"), None),
            P("section", None, ("experts", "dp")),
            P("section", None, ("experts", "dp")),
            P(("experts", "dp"), "section"),
            P(("experts", "dp"), "section"),
            P("experts", "section", "dp"),
            P("experts", "dp", "section"),
        ),
        check_vma=False,
    )
```

```python
import functools

import jax
import jax.numpy as jnp
from jax import lax
from jax.experimental import pallas as pl
from jax.experimental.pallas import tpu as pltpu
from jax.sharding import PartitionSpec as P

HEADS = 12
HEAD_DIM = 64
SEQ = 197


eps = 1e-06


def pair(block):
    return lax.ppermute(block, "section", [(0, 1), (1, 0)])


def layer_norm(values, gain, bias):
    centred = values - jnp.mean(values, axis=-1, keepdims=True)
    spread = jnp.mean(centred * centred, axis=-1, keepdims=True)
    return centred * lax.rsqrt(spread + eps) * gain + bias


def norm_back(values, gain, bias, cotan):
    _, pull = jax.vjp(layer_norm, values, gain, bias)
    return pull(cotan)


def gelu_back(before, cotan):
    _, pull = jax.vjp(jax.nn.gelu, before)
    return pull(cotan)[0]


def matmul(left, right):
    return jnp.dot(left, right, preferred_element_type=jnp.float32)


def matmul_rows(left, right):
    return lax.dot_general(
        left, right, (((0,), (0,)), ((), ())), preferred_element_type=jnp.float32
    )


def matmul_cols(left, right):
    return lax.dot_general(
        left, right, (((1,), (1,)), ((), ())), preferred_element_type=jnp.float32
    )


def head_split(mixed):
    return mixed.reshape(-1, SEQ, 3, HEADS, HEAD_DIM)


def score_table(split):
    return jnp.einsum(
        "bqhd,bkhd->bhqk", split[:, :, 0], split[:, :, 1], preferred_element_type=jnp.float32
    ) * HEAD_DIM ** (-0.5)


def attend(normed, weight_qkv):
    mixed = matmul(normed, weight_qkv).astype(jnp.bfloat16)
    split = head_split(mixed)
    scores = score_table(split)
    top = jnp.max(scores, axis=-1, keepdims=True)
    logsum = top + jnp.log(jnp.sum(jnp.exp(scores - top), axis=-1, keepdims=True))
    probs = jnp.exp(scores - logsum).astype(jnp.bfloat16)
    attended = jnp.einsum(
        "bhqk,bkhd->bqhd", probs, split[:, :, 2], preferred_element_type=jnp.float32
    )
    return (mixed, logsum, attended.reshape(normed.shape[0], -1).astype(jnp.bfloat16))


def attend_back(normed, mixed, logsum, attended, grad_hidden, weight_qkv, weight_out):
    grad_cast = grad_hidden.astype(jnp.bfloat16)
    grad_att = matmul_cols(grad_cast, weight_out).astype(jnp.bfloat16)
    split = head_split(mixed)
    probs_full = jnp.exp(score_table(split) - logsum)
    probs = probs_full.astype(jnp.bfloat16)
    grad_heads = grad_att.reshape(-1, SEQ, HEADS, HEAD_DIM)
    grad_probs = jnp.einsum(
        "bqhd,bkhd->bhqk", grad_heads, split[:, :, 2], preferred_element_type=jnp.float32
    )
    grad_value = jnp.einsum(
        "bhqk,bqhd->bkhd", probs, grad_heads, preferred_element_type=jnp.float32
    )
    inner = jnp.sum(probs_full * grad_probs, axis=-1, keepdims=True)
    grad_scores = (probs_full * (grad_probs - inner) * HEAD_DIM ** (-0.5)).astype(jnp.bfloat16)
    grad_query = jnp.einsum(
        "bhqk,bkhd->bqhd", grad_scores, split[:, :, 1], preferred_element_type=jnp.float32
    )
    grad_key = jnp.einsum(
        "bhqk,bqhd->bkhd", grad_scores, split[:, :, 0], preferred_element_type=jnp.float32
    )
    grad_mixed = (
        jnp.stack([grad_query, grad_key, grad_value], axis=2)
        .reshape(normed.shape[0], -1)
        .astype(jnp.bfloat16)
    )
    return (matmul_cols(grad_mixed, weight_qkv), grad_mixed, grad_cast)


def front_half(block_in, gains, biases, weight_qkv, weight_out):
    start = block_in.astype(jnp.float32)
    normed = layer_norm(start, gains[0], biases[0]).astype(jnp.bfloat16)
    mixed, logsum, attended = attend(normed, weight_qkv)
    hidden = start + matmul(attended, weight_out)
    second = layer_norm(hidden, gains[1], biases[1]).astype(jnp.bfloat16)
    return (normed, mixed, logsum, attended, hidden, second)


def front_back(block_in, saved, grad_top, grad_second, gains, biases, weight_qkv, weight_out):
    normed, mixed, logsum, attended, hidden = saved
    grad_mid, gain_two, bias_two = norm_back(hidden, gains[1], biases[1], grad_second)
    grad_hidden = grad_top + grad_mid
    grad_normed, grad_mixed, grad_cast = attend_back(
        normed, mixed, logsum, attended, grad_hidden, weight_qkv, weight_out
    )
    grad_start, gain_one, bias_one = norm_back(
        block_in.astype(jnp.float32), gains[0], biases[0], grad_normed
    )
    return (
        grad_start + grad_hidden,
        jnp.stack([gain_one, gain_two, bias_one, bias_two]),
        grad_mixed,
        grad_cast,
    )


def rounded(values):
    return lax.reduce_precision(values, exponent_bits=8, mantissa_bits=7).astype(jnp.bfloat16)


TILE = 384
MESH = pl.DeviceIdType.MESH


def tail_kernel(
    experts,
    places,
    lag,
    *refs,
):
    count = 1 + max(place[0] for place in places)
    inputs = refs[:count]
    norm_in, sums, norm_out = refs[count : count + 3]
    (
        near_in,
        far_own,
        last_own,
        far_out,
        far_in,
        group_out,
        group_in,
        norm_near,
        norm_mid,
        norm_far,
        own_sems,
        near_send,
        near_recv,
        far_send,
        far_recv,
        group_send,
        group_recv,
        norm_send,
        norm_recv,
        norm_group_send,
        norm_group_recv,
    ) = refs[count + 3 :]
    shard = lax.axis_index("dp")
    group = lax.axis_index("experts")
    low = shard % 2
    high = shard // 2
    peers = {0: shard, 1: shard + 1 - 2 * low, 2: shard + 2 - 4 * high, 3: 3 - shard}
    groups = [(group + step) % experts for step in range(experts)]
    tiles = len(places)
    batch = 4

    barrier = pltpu.get_barrier_semaphore()
    for mask in (1, 2, 3):
        pl.semaphore_signal(barrier, 1, device_id={"dp": peers[mask]}, device_id_type=MESH)
    for step in range(1, experts):
        pl.semaphore_signal(barrier, 1, device_id={"experts": groups[step]}, device_id_type=MESH)

    def block(tile, mask):
        which, index, columns = places[tile]
        if index is None:
            return inputs[which].at[:, peers[mask], :, pl.ds(columns, TILE)]
        return inputs[which].at[:, peers[mask], index, :, :]

    def order(tile):
        return (1, 2) if tile % 2 == 0 else (2, 1)

    def own_copy(tile, part):
        mask = (order(tile)[1], 0)[part]
        target = (far_own, last_own)[part]
        return pltpu.make_async_copy(
            block(tile, mask), target.at[tile], own_sems.at[2 * tile + part]
        )

    def near_copy(tile, part):
        near = order(tile)[0]
        return pltpu.make_async_remote_copy(
            block(tile, (3, near)[part]),
            near_in.at[tile, part],
            near_send.at[2 * tile + part],
            near_recv.at[2 * tile + part],
            device_id={"dp": peers[near]},
            device_id_type=MESH,
        )

    def far_copy(tile):
        return pltpu.make_async_remote_copy(
            far_out.at[tile],
            far_in.at[tile],
            far_send.at[tile],
            far_recv.at[tile],
            device_id={"dp": peers[order(tile)[1]]},
            device_id_type=MESH,
        )

    def group_copy(chunk, step):
        span = pl.ds(chunk * batch, batch)
        return pltpu.make_async_remote_copy(
            group_out.at[groups[step], span],
            group_in.at[step - 1, span],
            group_send.at[chunk * (experts - 1) + step - 1],
            group_recv.at[chunk * (experts - 1) + step - 1],
            device_id={"experts": groups[step]},
            device_id_type=MESH,
        )

    def norm_copy(mask):
        return pltpu.make_async_remote_copy(
            norm_in.at[peers[mask]],
            norm_near.at[mask - 1],
            norm_send.at[mask - 1],
            norm_recv.at[mask - 1],
            device_id={"dp": peers[mask]},
            device_id_type=MESH,
        )

    def norm_group_copy(step):
        return pltpu.make_async_remote_copy(
            norm_mid.at[groups[step]],
            norm_far.at[step - 1],
            norm_group_send.at[step - 1],
            norm_group_recv.at[step - 1],
            device_id={"experts": groups[step]},
            device_id_type=MESH,
        )

    def wide(value):
        return value.astype(jnp.float32)

    pl.semaphore_wait(barrier, 3 + experts - 1)

    def start(tile):
        near_copy(tile, 0).start()
        near_copy(tile, 1).start()
        own_copy(tile, 0).start()
        own_copy(tile, 1).start()

    def turn(tile):
        own_copy(tile, 0).wait()
        near_copy(tile, 0).wait_recv()

        @pl.loop(0, experts)
        def _(at):
            far_out[tile, at] = (wide(far_own[tile, at]) + wide(near_in[tile, 0, at])).astype(
                jnp.bfloat16
            )

        far_copy(tile).start()

    def finish(tile):
        own_copy(tile, 1).wait()
        near_copy(tile, 1).wait_recv()
        far_copy(tile).wait_recv()

        @pl.loop(0, experts)
        def _(at):
            group_out[at, tile] = (
                wide(last_own[tile, at]) + wide(near_in[tile, 1, at]) + wide(far_in[tile, at])
            ).astype(jnp.bfloat16)

        if tile % batch == batch - 1:
            for step in range(1, experts):
                group_copy(tile // batch, step).start()

    for step in range(tiles + 2 * lag):
        if step < tiles:
            start(step)
        if step == 2:
            for mask in (1, 2, 3):
                norm_copy(mask).start()
        if 0 <= step - lag < tiles:
            turn(step - lag)
        if 0 <= step - 2 * lag < tiles:
            finish(step - 2 * lag)
        if step == tiles // 2:
            for mask in (1, 2, 3):
                norm_copy(mask).wait()
            norm_mid[...] = (norm_in[shard] + norm_near[0]) + (norm_near[1] + norm_near[2])
            for other in range(1, experts):
                norm_group_copy(other).start()

    norm_total = norm_mid[group]
    for step in range(1, experts):
        norm_group_copy(step).wait()
        norm_total = norm_total + norm_far[step - 1]
    norm_out[...] = norm_total

    for chunk in range(tiles // batch):
        for step in range(1, experts):
            group_copy(chunk, step).wait_recv()

        @pl.loop(chunk * batch, chunk * batch + batch)
        def _(tile):
            total = wide(group_out[group, tile])
            for step in range(1, experts):
                total = total + wide(group_in[step - 1, tile])
            sums[tile] = total

    for tile in range(tiles):
        near_copy(tile, 0).wait_send()
        near_copy(tile, 1).wait_send()
        far_copy(tile).wait_send()
    for chunk in range(tiles // batch):
        for step in range(1, experts):
            group_copy(chunk, step).wait_send()


def tail_sums(experts, shards, dense_out, dense_in, qkv, out, norms):
    size = dense_in.shape[0] // (experts * shards)
    folds = dense_out.shape[0] // dense_in.shape[0]
    inputs = [dense_out.reshape(experts, shards, folds, size, -1)] + [
        array.reshape(experts, shards, size, -1) for array in (dense_in, qkv, out)
    ]
    places = [(0, index, 0) for index in range(folds)]
    for which in (1, 2, 3):
        places += [(which, None, at) for at in range(0, inputs[which].shape[-1], TILE)]
    tiles = len(places)
    full = (tiles, experts, size, TILE)
    dma = pltpu.SemaphoreType.DMA
    half = jnp.bfloat16
    sums, norm = pl.pallas_call(
        functools.partial(tail_kernel, experts, places, 2),
        out_shape=(
            jax.ShapeDtypeStruct((tiles, size, TILE), jnp.float32),
            jax.ShapeDtypeStruct(norms.shape[2:], jnp.float32),
        ),
        in_specs=[pl.BlockSpec(memory_space=pl.ANY)] * 4
        + [pl.BlockSpec(memory_space=pltpu.VMEM)],
        out_specs=(
            pl.BlockSpec(memory_space=pltpu.VMEM),
            pl.BlockSpec(memory_space=pltpu.VMEM),
        ),
        scratch_shapes=[
            pltpu.VMEM((tiles, 2) + full[1:], half),
            pltpu.VMEM(full, half),
            pltpu.VMEM(full, half),
            pltpu.VMEM(full, half),
            pltpu.VMEM(full, half),
            pltpu.VMEM((experts, tiles, size, TILE), half),
            pltpu.VMEM((experts - 1, tiles, size, TILE), half),
            pltpu.VMEM((shards - 1,) + norms.shape[1:], jnp.float32),
            pltpu.VMEM(norms.shape[1:], jnp.float32),
            pltpu.VMEM((experts - 1,) + norms.shape[2:], jnp.float32),
            dma((2 * tiles,)),
            dma((2 * tiles,)),
            dma((2 * tiles,)),
            dma((tiles,)),
            dma((tiles,)),
            dma((tiles // 4 * (experts - 1),)),
            dma((tiles // 4 * (experts - 1),)),
            dma((shards - 1,)),
            dma((shards - 1,)),
            dma((experts - 1,)),
            dma((experts - 1,)),
        ],
        compiler_params=pltpu.CompilerParams(
            collective_id=0, has_side_effects=True, vmem_limit_bytes=40 * 2**20
        ),
        cost_estimate=pl.CostEstimate(
            flops=10**7, bytes_accessed=10**7, transcendentals=0
        ),
    )(*inputs, norms)
    spans = [0]
    for which in range(4):
        spans.append(spans[-1] + sum(place[0] == which for place in places))
    dense_out_sum = sums[: spans[1]].reshape(folds * size, TILE)
    rest = [
        jnp.swapaxes(sums[spans[i] : spans[i + 1]], 0, 1).reshape(size, -1) for i in (1, 2, 3)
    ]
    return [dense_out_sum] + rest + [norm]


def on_device(
    tokens,
    cotangent,
    norm_gains,
    norm_biases,
    qkv_weight,
    out_weight,
    dense_in,
    dense_out,
    expert_in,
    expert_out,
    routes,
    gates,
):
    rows = SEQ
    width = tokens.shape[1]
    experts = lax.axis_size("experts")
    shards = lax.axis_size("dp")
    capacity = 2 * rows // experts
    padded = -(-capacity // 8) * 8
    slots = experts * padded
    section = lax.axis_index("section")
    group = lax.axis_index("experts")
    shard = lax.axis_index("dp")
    first = section == 0

    def ordered(mine, other, axis):
        return jnp.concatenate(
            [jnp.where(first, mine, other), jnp.where(first, other, mine)], axis=axis
        )

    def kept_half(array, axis):
        low, high = jnp.split(array, 2, axis=axis)
        return jnp.where(first, low, high)

    def sent_half(array, axis):
        low, high = jnp.split(array, 2, axis=axis)
        return jnp.where(first, high, low)

    def both(own):
        other = pair(own)
        return (jnp.where(first, own, other), jnp.where(first, other, own))

    def across(array, mask):
        return lax.ppermute(array, "dp", [(i, i ^ mask) for i in range(shards)])

    def shifted(array, step):
        return lax.ppermute(
            array, "experts", [(i, (i + step) % experts) for i in range(experts)]
        )

    def wide(array):
        return array.astype(jnp.float32)

    def shard_sum(block, near, far):
        passed = across(block(3).astype(jnp.bfloat16), near)
        direct = across(block(near).astype(jnp.bfloat16), near)
        turned = across((block(far) + wide(passed)).astype(jnp.bfloat16), far)
        return block(0) + wide(direct) + wide(turned)

    def group_sum(array):
        own = lax.dynamic_index_in_dim(array, group, 0, False)
        total = wide(own)
        for step in range(1, experts):
            target = lax.rem(group + step, experts)
            total = total + wide(
                shifted(lax.dynamic_index_in_dim(array, target, 0, False), step)
            )
        return total

    def everyone_sum(left, right, near, far):
        blocks = left.reshape(experts, shards, -1, left.shape[1])

        def block(mask):
            part = lax.dynamic_index_in_dim(blocks, shard ^ mask, 1, False)
            return matmul(part.reshape(-1, left.shape[1]), right)

        total = shard_sum(block, near, far).astype(jnp.bfloat16)
        return group_sum(total.reshape(experts, -1, right.shape[1]))

    def padded_rows(array):
        return jnp.pad(array, ((0, -array.shape[0] % 256), (0, 0)))

    def joined(own, other):
        return jnp.concatenate([padded_rows(own), padded_rows(other)], axis=0)

    def joined_right(array):
        return joined(kept_half(array, 1), pair(sent_half(array, 1)))

    qkv_zero, qkv_one = both(qkv_weight[0])
    norms_zero, norms_one = both(jnp.concatenate([norm_gains[0], norm_biases[0]], axis=0))
    out_zero, out_one = both(out_weight[0])

    def own_block(array):
        return lax.dynamic_slice_in_dim(array, section * rows, rows, 0)

    block_in = own_block(tokens)
    grad_top = own_block(cotangent).astype(jnp.float32)
    chosen = own_block(routes)
    gate_pair = own_block(gates)

    flat = jnp.concatenate([chosen[:, 0], chosen[:, 1]])
    order = jnp.arange(2 * rows, dtype=jnp.int32)
    place = jnp.sum(
        ((flat[:, None] == flat[None, :]) & (order[None, :] < order[:, None])).astype(jnp.int32),
        axis=1,
        dtype=jnp.int32,
    )
    step_of = lax.rem(flat - group + experts, experts)
    slot = jnp.where(place < capacity, step_of * padded + place, slots)
    gate_flat = jnp.concatenate([gate_pair[:, 0], gate_pair[:, 1]])
    spread = (jnp.arange(slots, dtype=jnp.int32)[:, None] == slot[None, :]).astype(jnp.bfloat16)
    spread_both = spread[:, :rows] + spread[:, rows:]

    def sent_out(array):
        parts = [array[k * padded : (k + 1) * padded] for k in range(experts)]
        return jnp.concatenate([parts[0]] + [shifted(parts[k], k) for k in range(1, experts)])

    def sent_home(array):
        parts = [array[k * padded : (k + 1) * padded] for k in range(experts)]
        return jnp.concatenate(
            [parts[0]] + [shifted(parts[k], experts - k) for k in range(1, experts)]
        )

    doubled = (jnp.concatenate([grad_top, grad_top]) * gate_flat[:, None]).astype(jnp.bfloat16)
    grad_rows = sent_out(matmul(spread, doubled).astype(jnp.bfloat16))

    piece_in = kept_half(expert_in[0], 1)
    piece_back = kept_half(expert_out[0], 0)
    near_in = lax.all_gather(piece_in, "dp", axis=1, tiled=True)
    near_back = lax.all_gather(piece_back, "dp", axis=0, tiled=True)

    normed0, mixed0, logsum0, attended0, hidden0, second0 = front_half(
        block_in, norms_zero[:2], norms_zero[2:], qkv_zero, out_zero
    )
    before0 = matmul(second0, dense_in)
    active0 = jax.nn.gelu(before0).astype(jnp.bfloat16)
    middle = rounded(hidden0 + matmul(active0, dense_out))

    normed1, mixed1, logsum1, attended1, hidden1, second1 = front_half(
        middle, norms_one[:2], norms_one[2:], qkv_one, out_one
    )
    rows_in = sent_out(matmul(spread_both, second1).astype(jnp.bfloat16))

    near_in, near_back, mixed1 = lax.optimization_barrier((near_in, near_back, mixed1))
    weights_in = (near_in, pair(near_in))
    weights_back = (near_back, pair(near_back))
    before1 = [matmul(rows_in, weight) for weight in weights_in]
    active1 = [jax.nn.gelu(before).astype(jnp.bfloat16) for before in before1]
    grad_before1 = [
        gelu_back(before, matmul_cols(grad_rows, weight)).astype(jnp.bfloat16)
        for before, weight in zip(before1, weights_back)
    ]
    grad_arrived = (
        matmul_cols(grad_before1[0], weights_in[0]) + matmul_cols(grad_before1[1], weights_in[1])
    ).astype(jnp.bfloat16)
    grad_home = sent_home(grad_arrived)
    returned = (
        matmul(active1[0], weights_back[0]) + matmul(active1[1], weights_back[1])
    ).astype(jnp.bfloat16)
    returned_home = sent_home(returned)

    def expert_parts(halves, right):
        landed = [pair(half) for half in halves]
        lefts = [
            jnp.concatenate([halves[0], landed[1]], axis=0),
            jnp.concatenate([halves[1], landed[0]], axis=0),
        ]
        right = jnp.concatenate([kept_half(right, 1), pair(sent_half(right, 1))], axis=0)
        return [matmul_rows(left, right).astype(jnp.bfloat16) for left in lefts]

    expert_in_parts = expert_parts(grad_before1, rows_in)
    expert_out_parts = expert_parts(active1, grad_rows)
    expert_halves = [
        lax.psum_scatter(
            jnp.concatenate([one, two], axis=1), "dp", scatter_dimension=0, tiled=True
        )
        for one, two in zip(expert_in_parts, expert_out_parts)
    ]
    expert_sum = ordered(expert_halves[0], expert_halves[1], 0).astype(jnp.float32)
    expert_in_sum, expert_out_sum = jnp.split(expert_sum, 2, axis=1)

    picked = matmul_rows(spread, returned_home) * gate_flat[:, None]
    final = (hidden1 + (picked[:rows] + picked[rows:])).astype(jnp.bfloat16)
    grad_second1 = matmul_rows(spread_both, grad_home)
    grad_middle, grad_norm1, grad_mixed1, grad_cast1 = front_back(
        middle,
        (normed1, mixed1, logsum1, attended1, hidden1),
        grad_top,
        grad_second1,
        norms_one[:2],
        norms_one[2:],
        qkv_one,
        out_one,
    )

    grad_result = rounded(grad_middle)
    grad_before0 = gelu_back(before0, matmul_cols(grad_result, dense_out)).astype(jnp.bfloat16)
    grad_tokens, grad_norm0, grad_mixed0, grad_cast0 = front_back(
        block_in,
        (normed0, mixed0, logsum0, attended0, hidden0),
        grad_result.astype(jnp.float32),
        matmul_cols(grad_before0, dense_in),
        norms_zero[:2],
        norms_zero[2:],
        qkv_zero,
        out_zero,
    )
    def section_pair(zero, one):
        return joined(jnp.where(first, zero, one), pair(jnp.where(first, one, zero)))

    normed = section_pair(normed0, normed1)
    attended = section_pair(attended0, attended1)
    grad_mixed = section_pair(grad_mixed0, grad_mixed1)
    grad_cast = section_pair(grad_cast0, grad_cast1)
    active = joined(active0, pair(active0))
    second = joined(second0, pair(second0))
    grad_out_half = joined_right(grad_result)
    grad_in_half = joined_right(grad_before0)
    norm_pair = jnp.where(first, grad_norm0, grad_norm1) + pair(
        jnp.where(first, grad_norm1, grad_norm0)
    )
    pairs = (
        (active, grad_out_half),
        (second, grad_in_half),
        (normed, grad_mixed),
        (attended, grad_cast),
    )
    if experts == 4 and shards == 4:
        norm_parts = jnp.transpose(norm_pair.reshape(4, experts, shards, -1), (2, 1, 0, 3))
        size = norm_parts.shape[-1]
        norm_parts = jnp.pad(norm_parts, ((0, 0), (0, 0), (0, 4), (0, 128 - size)))
        dense_out_sum, dense_in_sum, qkv_sum, out_sum, norm_sum = tail_sums(
            experts,
            shards,
            *[matmul_rows(left, right).astype(jnp.bfloat16) for left, right in pairs],
            norm_parts,
        )
        norm_sum = norm_sum[:4, :size]
    else:
        dense_out_sum, dense_in_sum, qkv_sum, out_sum = [
            everyone_sum(left.T, right, *turn)
            for (left, right), turn in zip(pairs, ((1, 2), (2, 1), (1, 2), (2, 1)))
        ]
        norm_sum = lax.psum_scatter(
            norm_pair.T, ("experts", "dp"), scatter_dimension=0, tiled=True
        ).T

    acts = ordered(
        jnp.where(first, middle, final), pair(jnp.where(first, final, middle)), 0
    )
    act_grads = ordered(
        jnp.where(first, grad_tokens, grad_middle),
        pair(jnp.where(first, grad_middle, grad_tokens)),
        0,
    )
    return (
        acts[None],
        act_grads[None],
        qkv_sum[None],
        out_sum[None],
        norm_sum[:2][None],
        norm_sum[2:][None],
        dense_in_sum,
        dense_out_sum,
        expert_in_sum.T[None],
        expert_out_sum[None],
    )


def solution(mesh):
    placed = (
        P(("experts", "dp"), None),
        P(("experts", "dp"), None),
        P("section", None, None),
        P("section", None, None),
        P("section", None, None),
        P("section", None, None),
        P(),
        P(),
        P("experts", None, "dp"),
        P("experts", "dp", None),
        P(("experts", "dp"), None),
        P(("experts", "dp"), None),
    )
    return jax.shard_map(
        on_device,
        mesh=mesh,
        in_specs=placed,
        out_specs=(
            P("section", ("experts", "dp"), None),
            P("section", ("experts", "dp"), None),
            P("section", ("experts", "dp"), None),
            P("section", ("experts", "dp"), None),
            P("section", None, ("experts", "dp")),
            P("section", None, ("experts", "dp")),
            P(("experts", "dp"), "section"),
            P(("experts", "dp"), "section"),
            P("experts", "section", "dp"),
            P("experts", "dp", "section"),
        ),
        check_vma=False,
    )
```

```python
import functools

import jax
import jax.numpy as jnp
from jax import lax
from jax.experimental import pallas as pl
from jax.experimental.pallas import tpu as pltpu
from jax.sharding import PartitionSpec as P

HEADS = 12
HEAD_DIM = 64
SEQ = 197


eps = 1e-06


def pair(block):
    return lax.ppermute(block, "section", [(0, 1), (1, 0)])


def layer_norm(values, gain, bias):
    centred = values - jnp.mean(values, axis=-1, keepdims=True)
    spread = jnp.mean(centred * centred, axis=-1, keepdims=True)
    return centred * lax.rsqrt(spread + eps) * gain + bias


def norm_back(values, gain, bias, cotan):
    _, pull = jax.vjp(layer_norm, values, gain, bias)
    return pull(cotan)


def gelu_back(before, cotan):
    _, pull = jax.vjp(jax.nn.gelu, before)
    return pull(cotan)[0]


def matmul(left, right):
    return jnp.dot(left, right, preferred_element_type=jnp.float32)


def matmul_rows(left, right):
    return lax.dot_general(
        left, right, (((0,), (0,)), ((), ())), preferred_element_type=jnp.float32
    )


def matmul_cols(left, right):
    return lax.dot_general(
        left, right, (((1,), (1,)), ((), ())), preferred_element_type=jnp.float32
    )


def head_split(mixed):
    return mixed.reshape(-1, SEQ, 3, HEADS, HEAD_DIM)


def score_table(split):
    return jnp.einsum(
        "bqhd,bkhd->bhqk", split[:, :, 0], split[:, :, 1], preferred_element_type=jnp.float32
    ) * HEAD_DIM ** (-0.5)


def attend(normed, weight_qkv):
    mixed = matmul(normed, weight_qkv).astype(jnp.bfloat16)
    split = head_split(mixed)
    scores = score_table(split)
    top = jnp.max(scores, axis=-1, keepdims=True)
    logsum = top + jnp.log(jnp.sum(jnp.exp(scores - top), axis=-1, keepdims=True))
    probs = jnp.exp(scores - logsum).astype(jnp.bfloat16)
    attended = jnp.einsum(
        "bhqk,bkhd->bqhd", probs, split[:, :, 2], preferred_element_type=jnp.float32
    )
    return (mixed, logsum, attended.reshape(normed.shape[0], -1).astype(jnp.bfloat16))


def attend_back(normed, mixed, logsum, attended, grad_hidden, weight_qkv, weight_out):
    grad_cast = grad_hidden.astype(jnp.bfloat16)
    grad_att = matmul_cols(grad_cast, weight_out).astype(jnp.bfloat16)
    split = head_split(mixed)
    probs_full = jnp.exp(score_table(split) - logsum)
    probs = probs_full.astype(jnp.bfloat16)
    grad_heads = grad_att.reshape(-1, SEQ, HEADS, HEAD_DIM)
    grad_probs = jnp.einsum(
        "bqhd,bkhd->bhqk", grad_heads, split[:, :, 2], preferred_element_type=jnp.float32
    )
    grad_value = jnp.einsum(
        "bhqk,bqhd->bkhd", probs, grad_heads, preferred_element_type=jnp.float32
    )
    inner = jnp.sum(probs_full * grad_probs, axis=-1, keepdims=True)
    grad_scores = (probs_full * (grad_probs - inner) * HEAD_DIM ** (-0.5)).astype(jnp.bfloat16)
    grad_query = jnp.einsum(
        "bhqk,bkhd->bqhd", grad_scores, split[:, :, 1], preferred_element_type=jnp.float32
    )
    grad_key = jnp.einsum(
        "bhqk,bqhd->bkhd", grad_scores, split[:, :, 0], preferred_element_type=jnp.float32
    )
    grad_mixed = (
        jnp.stack([grad_query, grad_key, grad_value], axis=2)
        .reshape(normed.shape[0], -1)
        .astype(jnp.bfloat16)
    )
    return (matmul_cols(grad_mixed, weight_qkv), grad_mixed, grad_cast)


def front_half(block_in, gains, biases, weight_qkv, weight_out):
    start = block_in.astype(jnp.float32)
    normed = layer_norm(start, gains[0], biases[0]).astype(jnp.bfloat16)
    mixed, logsum, attended = attend(normed, weight_qkv)
    hidden = start + matmul(attended, weight_out)
    second = layer_norm(hidden, gains[1], biases[1]).astype(jnp.bfloat16)
    return (normed, mixed, logsum, attended, hidden, second)


def front_back(block_in, saved, grad_top, grad_second, gains, biases, weight_qkv, weight_out):
    normed, mixed, logsum, attended, hidden = saved
    grad_mid, gain_two, bias_two = norm_back(hidden, gains[1], biases[1], grad_second)
    grad_hidden = grad_top + grad_mid
    grad_normed, grad_mixed, grad_cast = attend_back(
        normed, mixed, logsum, attended, grad_hidden, weight_qkv, weight_out
    )
    grad_start, gain_one, bias_one = norm_back(
        block_in.astype(jnp.float32), gains[0], biases[0], grad_normed
    )
    return (
        grad_start + grad_hidden,
        jnp.stack([gain_one, gain_two, bias_one, bias_two]),
        grad_mixed,
        grad_cast,
    )


def rounded(values):
    return lax.reduce_precision(values, exponent_bits=8, mantissa_bits=7).astype(jnp.bfloat16)


TILE = 384
MESH = pl.DeviceIdType.MESH


def tail_kernel(
    experts,
    places,
    lag,
    *refs,
):
    count = 5
    inputs = refs[:count]
    mixed_in, grad_att_in, left, weight, block_in, gain, grad_hidden, norm_in = refs[
        count : count + 8
    ]
    dense_out_sum, dense_in_sum, qkv_sum, out_sum, norm_out, grad_own, grad_other = refs[
        count + 8 : count + 15
    ]
    (
        near_in,
        far_own,
        last_own,
        far_out,
        far_in,
        group_out,
        group_in,
        norm_near,
        norm_mid,
        norm_far,
        own_sems,
        near_send,
        near_recv,
        far_send,
        far_recv,
        group_send,
        group_recv,
        norm_send,
        norm_recv,
        norm_group_send,
        norm_group_recv,
        swap_out,
        swap_in,
        swap_send,
        swap_recv,
        right,
        grad_mixed,
        late,
        norm_own,
        norm_pair,
        pair_send,
        pair_recv,
        mixed,
        grad_att,
        grad_normed,
    ) = refs[count + 15 :]
    shard = lax.axis_index("dp")
    group = lax.axis_index("experts")
    section = lax.axis_index("section")
    low = shard % 2
    high = shard // 2
    peers = {0: shard, 1: shard + 1 - 2 * low, 2: shard + 2 - 4 * high, 3: 3 - shard}
    groups = [(group + step) % experts for step in range(experts)]
    tiles = len(places)
    batch = 4

    barrier = pltpu.get_barrier_semaphore()
    for mask in (1, 2, 3):
        pl.semaphore_signal(barrier, 1, device_id={"dp": peers[mask]}, device_id_type=MESH)
    for step in range(1, experts):
        pl.semaphore_signal(barrier, 1, device_id={"experts": groups[step]}, device_id_type=MESH)

    pl.semaphore_signal(barrier, 1, device_id={"section": 1 - section}, device_id_type=MESH)

    def block(tile, mask):
        which, index, columns = places[tile]
        if which == count:
            return late.at[index, :, peers[mask], :, :]
        if index is None:
            return inputs[which].at[:, peers[mask], :, pl.ds(columns, TILE)]
        return inputs[which].at[:, peers[mask], index, :, :]

    def order(tile):
        return (1, 2) if tile % 2 == 0 else (2, 1)

    def own_copy(tile, part):
        mask = (order(tile)[1], 0)[part]
        target = (far_own, last_own)[part]
        return pltpu.make_async_copy(
            block(tile, mask), target.at[tile], own_sems.at[2 * tile + part]
        )

    def near_copy(tile, part):
        near = order(tile)[0]
        return pltpu.make_async_remote_copy(
            block(tile, (3, near)[part]),
            near_in.at[tile, part],
            near_send.at[2 * tile + part],
            near_recv.at[2 * tile + part],
            device_id={"dp": peers[near]},
            device_id_type=MESH,
        )

    def far_copy(tile):
        return pltpu.make_async_remote_copy(
            far_out.at[tile],
            far_in.at[tile],
            far_send.at[tile],
            far_recv.at[tile],
            device_id={"dp": peers[order(tile)[1]]},
            device_id_type=MESH,
        )

    def group_copy(chunk, step):
        span = pl.ds(chunk * batch, batch)
        return pltpu.make_async_remote_copy(
            group_out.at[groups[step], span],
            group_in.at[step - 1, span],
            group_send.at[chunk * (experts - 1) + step - 1],
            group_recv.at[chunk * (experts - 1) + step - 1],
            device_id={"experts": groups[step]},
            device_id_type=MESH,
        )

    def norm_copy(mask):
        return pltpu.make_async_remote_copy(
            norm_own,
            norm_near.at[mask - 1],
            norm_send.at[mask - 1],
            norm_recv.at[mask - 1],
            device_id={"dp": peers[mask]},
            device_id_type=MESH,
        )

    def norm_group_copy(step):
        return pltpu.make_async_remote_copy(
            norm_mid,
            norm_far.at[step - 1],
            norm_group_send.at[step - 1],
            norm_group_recv.at[step - 1],
            device_id={"experts": groups[step]},
            device_id_type=MESH,
        )

    def wide(value):
        return value.astype(jnp.float32)

    pl.semaphore_wait(barrier, 4 + experts - 1)

    def start(tile):
        near_copy(tile, 0).start()
        near_copy(tile, 1).start()
        own_copy(tile, 0).start()
        own_copy(tile, 1).start()

    def turn(tile):
        own_copy(tile, 0).wait()
        near_copy(tile, 0).wait_recv()

        @pl.loop(0, experts)
        def _(at):
            far_out[tile, at] = (wide(far_own[tile, at]) + wide(near_in[tile, 0, at])).astype(
                jnp.bfloat16
            )

        far_copy(tile).start()

    def finish(tile):
        own_copy(tile, 1).wait()
        near_copy(tile, 1).wait_recv()
        far_copy(tile).wait_recv()

        @pl.loop(0, experts)
        def _(at):
            group_out[at, tile] = (
                wide(last_own[tile, at]) + wide(near_in[tile, 1, at]) + wide(far_in[tile, at])
            ).astype(jnp.bfloat16)

        if tile % batch == batch - 1:
            for step in range(1, experts):
                group_copy(tile // batch, step).start()

    def pair_copy(index, source, target):
        return pltpu.make_async_remote_copy(
            source,
            target,
            pair_send.at[index],
            pair_recv.at[index],
            device_id={"section": 1 - section},
            device_id_type=MESH,
        )

    late_tiles = [tile for tile in range(tiles) if places[tile][0] == count]
    for tile in range(4):
        start(tile)

    mixed[...] = jnp.zeros_like(mixed)
    grad_att[...] = jnp.zeros_like(grad_att)
    mixed[0:SEQ] = mixed_in[...]
    grad_att[0:SEQ] = grad_att_in[...]
    width = grad_att.shape[1]
    spaced = grad_att.shape[0]
    scale = HEAD_DIM ** (-0.5)
    valid = lax.broadcasted_iota(jnp.int32, (spaced, spaced), 1) < SEQ

    def dot(one, other, dims):
        return lax.dot_general(one, other, ((dims[:1], dims[1:]), ((), ())), preferred_element_type=jnp.float32)

    def head_pair(at):
        def columns(part):
            return pl.ds(pl.multiple_of(part * width + at * 2 * HEAD_DIM, 2 * HEAD_DIM), 2 * HEAD_DIM)

        queries, keys, values = [mixed[:, columns(part)] for part in range(3)]
        grads = grad_att[:, columns(0)]
        made = []
        for half in range(2):
            span = slice(half * HEAD_DIM, (half + 1) * HEAD_DIM)
            query, key, value, grad = queries[:, span], keys[:, span], values[:, span], grads[:, span]
            scores = dot(query, key, (1, 1)) * scale
            top = jnp.max(jnp.where(valid, scores, -jnp.inf), axis=1, keepdims=True)
            raised = jnp.where(valid, jnp.exp(scores - top), 0.0)
            full = raised / jnp.sum(raised, axis=1, keepdims=True)
            probs = full.astype(jnp.bfloat16)
            grad_probs = dot(grad, value, (1, 1))
            inner = jnp.sum(full * grad_probs, axis=1, keepdims=True)
            grad_scores = (full * (grad_probs - inner) * scale).astype(jnp.bfloat16)
            made.append(
                (
                    dot(grad_scores, key, (1, 0)),
                    dot(grad_scores, query, (0, 0)),
                    dot(probs, grad, (0, 0)),
                )
            )
        for part in range(3):
            grad_mixed[:, columns(part)] = jnp.concatenate(
                [made[0][part], made[1][part]], axis=1
            ).astype(jnp.bfloat16)

    pairs = HEADS // 2
    pl.loop(0, pairs // 3)(head_pair)
    turn(0)
    turn(1)
    start(4)
    start(5)
    pl.loop(pairs // 3, 2 * pairs // 3)(head_pair)
    turn(2)
    turn(3)
    start(6)
    start(7)
    finish(0)
    finish(1)
    pl.loop(2 * pairs // 3, pairs)(head_pair)
    turn(4)
    turn(5)
    start(8)
    start(9)
    finish(2)
    finish(3)

    cut = grad_mixed.shape[1] // 2
    kept = pl.ds(pl.multiple_of(section * cut, 128), cut)
    sent = pl.ds(pl.multiple_of((1 - section) * cut, 128), cut)
    mixed_copy = pair_copy(0, grad_mixed.at[:, sent], right.at[1])
    mixed_copy.start()
    right[0] = grad_mixed[:, kept]

    rows_at = 256

    @pl.loop(0, width // rows_at)
    def _(at):
        span = pl.ds(pl.multiple_of(at * rows_at, rows_at), rows_at)
        grad_normed[:, span] = dot(grad_mixed[...], weight[span, :], (1, 1))

    start(10)
    start(11)
    mixed_copy.wait()
    parts = left.shape[2] // TILE

    @pl.loop(0, parts)
    def _(at):
        rows = pl.ds(pl.multiple_of(at * TILE, TILE), TILE)
        for index in range(len(late_tiles)):
            span = slice(index * TILE, (index + 1) * TILE)
            product = dot(left[0, :, rows], right[0, :, span], (0, 0)) + dot(
                left[1, :, rows], right[1, :, span], (0, 0)
            )
            product = product.astype(jnp.bfloat16).reshape((experts // parts,) + late.shape[2:])
            for inner in range(experts // parts):
                late[index, at * (experts // parts) + inner] = product[inner]

    turn(6)
    turn(7)
    finish(4)
    finish(5)
    start(12)
    start(13)

    start_values = wide(block_in[...])
    centred = start_values - jnp.mean(start_values, axis=1, keepdims=True)
    root = lax.rsqrt(jnp.mean(centred * centred, axis=1, keepdims=True) + eps)
    unit = centred * root
    cotan = grad_normed[0:SEQ]
    norm_pair[0, 0:1, :] = jnp.sum(cotan * unit, axis=0, keepdims=True)
    norm_pair[0, 1:2, :] = jnp.sum(cotan, axis=0, keepdims=True)
    norm_copy_pair = pair_copy(1, norm_pair.at[0], norm_pair.at[1])
    norm_copy_pair.start()
    scaled = cotan * gain[0:1, :]
    grad_own[0:SEQ] = grad_hidden[...] + root * (
        scaled
        - jnp.mean(scaled, axis=1, keepdims=True)
        - unit * jnp.mean(scaled * unit, axis=1, keepdims=True)
    )
    grad_copy = pair_copy(2, grad_own, grad_other)
    grad_copy.start()
    norm_copy_pair.wait()
    chosen = jnp.where(section == 0, 1.0, 0.0)
    norm_own[...] = norm_in[...]
    norm_own[0:1, :] = norm_in[0:1, :] + chosen * (norm_pair[0, 0:1, :] + norm_pair[1, 0:1, :])
    norm_own[2:3, :] = norm_in[2:3, :] + chosen * (norm_pair[0, 1:2, :] + norm_pair[1, 1:2, :])
    for mask in (1, 2, 3):
        norm_copy(mask).start()

    start(14)
    start(15)
    for step in range(8, tiles + lag):
        if step < tiles:
            turn(step)
        if step == 12:
            for mask in (1, 2, 3):
                norm_copy(mask).wait()
            norm_mid[...] = (norm_own[...] + norm_near[0]) + (norm_near[1] + norm_near[2])
            for other in range(1, experts):
                norm_group_copy(other).start()
        finish(step - lag)

    grad_copy.wait()
    norm_total = norm_mid[...]
    for step in range(1, experts):
        norm_group_copy(step).wait()
        norm_total = norm_total + norm_far[step - 1]
    norm_out[...] = norm_total

    def total_of(tile):
        total = wide(group_out[group, tile])
        for step in range(1, experts):
            total = total + wide(group_in[step - 1, tile])
        return total

    size = dense_in_sum.shape[0]
    for chunk in range(tiles // batch):
        for step in range(1, experts):
            group_copy(chunk, step).wait_recv()
        for at in range(batch):
            total = total_of(chunk * batch + at)
            if chunk == 0:
                dense_out_sum[at * size : (at + 1) * size] = total
            elif chunk == 1:
                dense_in_sum[:, at * TILE : (at + 1) * TILE] = total
            else:
                swap_out[chunk - 2, at] = total

    swap = pltpu.make_async_remote_copy(
        swap_out.at[section],
        swap_in,
        swap_send,
        swap_recv,
        device_id={"section": 1 - section},
        device_id_type=MESH,
    )
    swap.start()

    def place(half, parts):
        cut = qkv_sum.shape[1] // 2
        for at in range(batch - 1):
            start_at = pl.multiple_of(half * cut + at * TILE, 128)
            qkv_sum[:, pl.ds(start_at, TILE)] = parts[at]
        out_sum[:, pl.ds(pl.multiple_of(half * TILE, 128), TILE)] = parts[batch - 1]

    place(section, swap_out[1 - section])
    swap.wait()
    place(1 - section, swap_in[...])

    for tile in range(tiles):
        near_copy(tile, 0).wait_send()
        near_copy(tile, 1).wait_send()
        far_copy(tile).wait_send()
    for chunk in range(tiles // batch):
        for step in range(1, experts):
            group_copy(chunk, step).wait_send()


def tail_sums(experts, shards, dense_out, rest, mixed, grad_att, left, weight, block_in, gain, grad_hidden, norms):
    size = rest[0].shape[0] // (experts * shards)
    folds = dense_out.shape[0] // rest[0].shape[0]
    inputs = [dense_out.reshape(experts, shards, folds, size, -1)] + [
        array.reshape(experts, shards, size, -1) for array in rest
    ]
    places = [(0, index, 0) for index in range(folds)]
    places += [(1, None, at) for at in range(0, 4 * TILE, TILE)]
    places += [(2, None, at) for at in range(0, 3 * TILE, TILE)] + [(3, None, 0)]
    places += [(len(inputs), index, 0) for index in range(3)] + [(4, None, 0)]
    tiles = len(places)
    assert inputs[0].shape[2] == 4 and [array.shape[-1] // TILE for array in inputs] == [1, 4, 3, 1, 1]
    width = grad_att.shape[1]
    spaced = left.shape[1]
    full = (tiles, experts, size, TILE)
    dma = pltpu.SemaphoreType.DMA
    half = jnp.bfloat16
    return pl.pallas_call(
        functools.partial(tail_kernel, experts, places, 2),
        out_shape=(
            jax.ShapeDtypeStruct((folds * size, TILE), jnp.float32),
            jax.ShapeDtypeStruct((size, 4 * TILE), jnp.float32),
            jax.ShapeDtypeStruct((size, 6 * TILE), jnp.float32),
            jax.ShapeDtypeStruct((size, 2 * TILE), jnp.float32),
            jax.ShapeDtypeStruct(norms.shape, jnp.float32),
            jax.ShapeDtypeStruct(block_in.shape, jnp.float32),
            jax.ShapeDtypeStruct(block_in.shape, jnp.float32),
        ),
        in_specs=[pl.BlockSpec(memory_space=pl.ANY)] * len(inputs)
        + [pl.BlockSpec(memory_space=pltpu.VMEM)] * 8,
        out_specs=(pl.BlockSpec(memory_space=pltpu.VMEM),) * 7,
        scratch_shapes=[
            pltpu.VMEM((tiles, 2) + full[1:], half),
            pltpu.VMEM(full, half),
            pltpu.VMEM(full, half),
            pltpu.VMEM(full, half),
            pltpu.VMEM(full, half),
            pltpu.VMEM((experts, tiles, size, TILE), half),
            pltpu.VMEM((experts - 1, tiles, size, TILE), half),
            pltpu.VMEM((shards - 1,) + norms.shape, jnp.float32),
            pltpu.VMEM(norms.shape, jnp.float32),
            pltpu.VMEM((experts - 1,) + norms.shape, jnp.float32),
            dma((2 * tiles,)),
            dma((2 * tiles,)),
            dma((2 * tiles,)),
            dma((tiles,)),
            dma((tiles,)),
            dma((tiles // 4 * (experts - 1),)),
            dma((tiles // 4 * (experts - 1),)),
            dma((shards - 1,)),
            dma((shards - 1,)),
            dma((experts - 1,)),
            dma((experts - 1,)),
            pltpu.VMEM((2, 4, size, TILE), jnp.float32),
            pltpu.VMEM((4, size, TILE), jnp.float32),
            dma,
            dma,
            pltpu.VMEM((2, spaced, mixed.shape[1] // 2), half),
            pltpu.VMEM((spaced, mixed.shape[1]), half),
            pltpu.VMEM((3, experts, shards, size, TILE), half),
            pltpu.VMEM(norms.shape, jnp.float32),
            pltpu.VMEM((2,) + norms.shape, jnp.float32),
            dma((3,)),
            dma((3,)),
            pltpu.VMEM((spaced, mixed.shape[1]), half),
            pltpu.VMEM((spaced, width), half),
            pltpu.VMEM((spaced, width), jnp.float32),
        ],
        compiler_params=pltpu.CompilerParams(
            collective_id=0, has_side_effects=True, vmem_limit_bytes=56 * 2**20
        ),
        cost_estimate=pl.CostEstimate(
            flops=10**7, bytes_accessed=10**7, transcendentals=0
        ),
    )(*inputs, mixed, grad_att, left, weight, block_in, gain, grad_hidden, norms)


def on_device(
    tokens,
    cotangent,
    norm_gains,
    norm_biases,
    qkv_weight,
    out_weight,
    dense_in,
    dense_out,
    expert_in,
    expert_out,
    routes,
    gates,
):
    rows = SEQ
    width = tokens.shape[1]
    experts = lax.axis_size("experts")
    shards = lax.axis_size("dp")
    capacity = 2 * rows // experts
    padded = -(-capacity // 8) * 8
    slots = experts * padded
    section = lax.axis_index("section")
    group = lax.axis_index("experts")
    shard = lax.axis_index("dp")
    first = section == 0

    def ordered(mine, other, axis):
        return jnp.concatenate(
            [jnp.where(first, mine, other), jnp.where(first, other, mine)], axis=axis
        )

    def kept_half(array, axis):
        low, high = jnp.split(array, 2, axis=axis)
        return jnp.where(first, low, high)

    def sent_half(array, axis):
        low, high = jnp.split(array, 2, axis=axis)
        return jnp.where(first, high, low)

    def both(own):
        other = pair(own)
        return (jnp.where(first, own, other), jnp.where(first, other, own))

    def across(array, mask):
        return lax.ppermute(array, "dp", [(i, i ^ mask) for i in range(shards)])

    def shifted(array, step):
        return lax.ppermute(
            array, "experts", [(i, (i + step) % experts) for i in range(experts)]
        )

    def wide(array):
        return array.astype(jnp.float32)

    def shard_sum(block, near, far):
        passed = across(block(3).astype(jnp.bfloat16), near)
        direct = across(block(near).astype(jnp.bfloat16), near)
        turned = across((block(far) + wide(passed)).astype(jnp.bfloat16), far)
        return block(0) + wide(direct) + wide(turned)

    def group_sum(array):
        own = lax.dynamic_index_in_dim(array, group, 0, False)
        total = wide(own)
        for step in range(1, experts):
            target = lax.rem(group + step, experts)
            total = total + wide(
                shifted(lax.dynamic_index_in_dim(array, target, 0, False), step)
            )
        return total

    def everyone_sum(left, right, near, far):
        blocks = left.reshape(experts, shards, -1, left.shape[1])

        def block(mask):
            part = lax.dynamic_index_in_dim(blocks, shard ^ mask, 1, False)
            return matmul(part.reshape(-1, left.shape[1]), right)

        total = shard_sum(block, near, far).astype(jnp.bfloat16)
        return group_sum(total.reshape(experts, -1, right.shape[1]))

    def padded_rows(array):
        return jnp.pad(array, ((0, -array.shape[0] % 256), (0, 0)))

    def joined(own, other):
        return jnp.concatenate([padded_rows(own), padded_rows(other)], axis=0)

    kernel_fits = experts == 4 and shards == 4

    def partial_grad(both_sides):
        left, right = both_sides
        left = joined(left, pair(left))
        right = joined(kept_half(right, 1), pair(sent_half(right, 1)))
        if kernel_fits:
            return matmul_rows(left, right).astype(jnp.bfloat16)
        return (left.T, right)

    qkv_zero, qkv_one = both(qkv_weight[0])
    norms_zero, norms_one = both(jnp.concatenate([norm_gains[0], norm_biases[0]], axis=0))
    out_zero, out_one = both(out_weight[0])

    def own_block(array):
        return lax.dynamic_slice_in_dim(array, section * rows, rows, 0)

    block_in = own_block(tokens)
    grad_top = own_block(cotangent).astype(jnp.float32)
    chosen = own_block(routes)
    gate_pair = own_block(gates)

    flat = jnp.concatenate([chosen[:, 0], chosen[:, 1]])
    order = jnp.arange(2 * rows, dtype=jnp.int32)
    place = jnp.sum(
        ((flat[:, None] == flat[None, :]) & (order[None, :] < order[:, None])).astype(jnp.int32),
        axis=1,
        dtype=jnp.int32,
    )
    step_of = lax.rem(flat - group + experts, experts)
    slot = jnp.where(place < capacity, step_of * padded + place, slots)
    gate_flat = jnp.concatenate([gate_pair[:, 0], gate_pair[:, 1]])
    spread = (jnp.arange(slots, dtype=jnp.int32)[:, None] == slot[None, :]).astype(jnp.bfloat16)
    spread_both = spread[:, :rows] + spread[:, rows:]

    def sent_out(array):
        parts = [array[k * padded : (k + 1) * padded] for k in range(experts)]
        return jnp.concatenate([parts[0]] + [shifted(parts[k], k) for k in range(1, experts)])

    def sent_home(array):
        parts = [array[k * padded : (k + 1) * padded] for k in range(experts)]
        return jnp.concatenate(
            [parts[0]] + [shifted(parts[k], experts - k) for k in range(1, experts)]
        )

    doubled = (jnp.concatenate([grad_top, grad_top]) * gate_flat[:, None]).astype(jnp.bfloat16)
    grad_rows = sent_out(matmul(spread, doubled).astype(jnp.bfloat16))

    piece_in = kept_half(expert_in[0], 1)
    piece_back = kept_half(expert_out[0], 0)
    near_in = lax.all_gather(piece_in, "dp", axis=1, tiled=True)
    near_back = lax.all_gather(piece_back, "dp", axis=0, tiled=True)

    normed0, mixed0, logsum0, attended0, hidden0, second0 = front_half(
        block_in, norms_zero[:2], norms_zero[2:], qkv_zero, out_zero
    )
    before0 = matmul(second0, dense_in)
    active0 = jax.nn.gelu(before0).astype(jnp.bfloat16)
    middle = rounded(hidden0 + matmul(active0, dense_out))

    normed1, mixed1, logsum1, attended1, hidden1, second1 = front_half(
        middle, norms_one[:2], norms_one[2:], qkv_one, out_one
    )
    rows_in = sent_out(matmul(spread_both, second1).astype(jnp.bfloat16))

    near_in, near_back, rows_in = lax.optimization_barrier((near_in, near_back, rows_in))
    weights_in = (near_in, pair(near_in))
    weights_back = (near_back, pair(near_back))
    before1 = [matmul(rows_in, weight) for weight in weights_in]
    active1 = [jax.nn.gelu(before).astype(jnp.bfloat16) for before in before1]
    grad_before1 = [
        gelu_back(before, matmul_cols(grad_rows, weight)).astype(jnp.bfloat16)
        for before, weight in zip(before1, weights_back)
    ]
    grad_arrived = (
        matmul_cols(grad_before1[0], weights_in[0]) + matmul_cols(grad_before1[1], weights_in[1])
    ).astype(jnp.bfloat16)
    grad_home = sent_home(grad_arrived)
    returned = (
        matmul(active1[0], weights_back[0]) + matmul(active1[1], weights_back[1])
    ).astype(jnp.bfloat16)
    returned_home = sent_home(returned)

    def expert_parts(halves, right):
        landed = [pair(half) for half in halves]
        lefts = [
            jnp.concatenate([halves[0], landed[1]], axis=0),
            jnp.concatenate([halves[1], landed[0]], axis=0),
        ]
        right = jnp.concatenate([kept_half(right, 1), pair(sent_half(right, 1))], axis=0)
        return [matmul_rows(left, right).astype(jnp.bfloat16) for left in lefts]

    expert_in_parts = expert_parts(grad_before1, rows_in)
    expert_out_parts = expert_parts(active1, grad_rows)
    expert_stack = jnp.concatenate(expert_in_parts + expert_out_parts, axis=1)
    grad_home, expert_stack = lax.optimization_barrier((grad_home, expert_stack))
    expert_shard = lax.psum_scatter(expert_stack, "dp", scatter_dimension=0, tiled=True)
    parts = jnp.split(expert_shard, 4, axis=1)
    expert_in_sum = ordered(parts[0], parts[1], 0).astype(jnp.float32)
    expert_out_sum = ordered(parts[2], parts[3], 0).astype(jnp.float32)

    picked = matmul_rows(spread, returned_home) * gate_flat[:, None]
    final = (hidden1 + (picked[:rows] + picked[rows:])).astype(jnp.bfloat16)
    grad_second1 = matmul_rows(spread_both, grad_home)
    grad_middle, grad_norm1, grad_mixed1, grad_cast1 = front_back(
        middle,
        (normed1, mixed1, logsum1, attended1, hidden1),
        grad_top,
        grad_second1,
        norms_one[:2],
        norms_one[2:],
        qkv_one,
        out_one,
    )

    grad_result = rounded(grad_middle)
    grad_before0 = gelu_back(before0, matmul_cols(grad_result, dense_out)).astype(jnp.bfloat16)
    dense_out_part = partial_grad((active0, grad_result))
    dense_in_part = partial_grad((second0, grad_before0))
    qkv_part1 = partial_grad((normed1, grad_mixed1))
    out_part1 = partial_grad((attended1, grad_cast1))
    grad_second0 = matmul_cols(grad_before0, dense_in)
    saved0 = (normed0, mixed0, logsum0, attended0, hidden0)
    if not kernel_fits:
        grad_tokens, grad_norm0, grad_mixed0, grad_cast0 = front_back(
            block_in,
            saved0,
            grad_result.astype(jnp.float32),
            grad_second0,
            norms_zero[:2],
            norms_zero[2:],
            qkv_zero,
            out_zero,
        )
        qkv_part0 = partial_grad((normed0, grad_mixed0))
    else:
        grad_mid0, gain_two0, bias_two0 = norm_back(
            hidden0, norms_zero[1], norms_zero[3], grad_second0
        )
        grad_hidden0 = grad_result.astype(jnp.float32) + grad_mid0
        grad_cast0 = grad_hidden0.astype(jnp.bfloat16)
        grad_att0 = matmul_cols(grad_cast0, out_zero).astype(jnp.bfloat16)
        nothing = jnp.zeros_like(gain_two0)
        grad_norm0 = jnp.stack([nothing, gain_two0, nothing, bias_two0])
    out_part0 = partial_grad((attended0, grad_cast0))
    norm_pair = jnp.where(first, grad_norm0, grad_norm1) + pair(
        jnp.where(first, grad_norm1, grad_norm0)
    )
    rest = [dense_in_part, qkv_part1, out_part1]
    if kernel_fits:
        eight = jnp.zeros((8, width), jnp.float32)
        dense_out_sum, dense_in_sum, qkv_sum, out_sum, norm_sum, grad_tokens, grad_landed = tail_sums(
            experts,
            shards,
            dense_out_part,
            rest + [out_part0],
            mixed0,
            grad_att0,
            joined(normed0, pair(normed0)).reshape(2, -1, width),
            qkv_zero,
            block_in,
            eight.at[0].set(norms_zero[0]),
            grad_hidden0,
            eight.at[:4].set(norm_pair),
        )
        size = width // (experts * shards)
        norm_sum = lax.dynamic_slice(norm_sum[:4], (0, (group * shards + shard) * size), (4, size))
        middle_landed = pair(grad_middle)
        act_grads = jnp.concatenate(
            [
                jnp.where(first, grad_tokens, middle_landed),
                jnp.where(first, grad_landed, grad_middle),
            ]
        )
    else:
        dense_out_sum = everyone_sum(*dense_out_part, 1, 2)
        dense_in_sum, qkv_one, out_one, qkv_zero, out_zero = [
            everyone_sum(*part, 2, 1).astype(jnp.bfloat16)
            for part in rest + [qkv_part0, out_part0]
        ]
        own_shared, other_shared = [
            jnp.where(first, *halves)
            for halves in (
                (
                    jnp.concatenate([qkv_zero, out_zero], axis=1),
                    jnp.concatenate([qkv_one, out_one], axis=1),
                ),
                (
                    jnp.concatenate([qkv_one, out_one], axis=1),
                    jnp.concatenate([qkv_zero, out_zero], axis=1),
                ),
            )
        ]
        other_shared = pair(other_shared)
        cut = qkv_zero.shape[1]
        qkv_sum = ordered(own_shared[:, :cut], other_shared[:, :cut], 1).astype(jnp.float32)
        out_sum = ordered(own_shared[:, cut:], other_shared[:, cut:], 1).astype(jnp.float32)
        dense_in_sum = dense_in_sum.astype(jnp.float32)
        norm_sum = lax.psum_scatter(
            norm_pair.T, ("experts", "dp"), scatter_dimension=0, tiled=True
        ).T
        act_grads = ordered(
            jnp.where(first, grad_tokens, grad_middle),
            pair(jnp.where(first, grad_middle, grad_tokens)),
            0,
        )

    acts = ordered(
        jnp.where(first, middle, final), pair(jnp.where(first, final, middle)), 0
    )
    return (
        acts[None],
        act_grads[None],
        qkv_sum[None],
        out_sum[None],
        norm_sum[:2][None],
        norm_sum[2:][None],
        dense_in_sum,
        dense_out_sum,
        expert_in_sum.T[None],
        expert_out_sum[None],
    )


def solution(mesh):
    placed = (
        P(("experts", "dp"), None),
        P(("experts", "dp"), None),
        P("section", None, None),
        P("section", None, None),
        P("section", None, None),
        P("section", None, None),
        P(),
        P(),
        P("experts", None, "dp"),
        P("experts", "dp", None),
        P(("experts", "dp"), None),
        P(("experts", "dp"), None),
    )
    return jax.shard_map(
        on_device,
        mesh=mesh,
        in_specs=placed,
        out_specs=(
            P("section", ("experts", "dp"), None),
            P("section", ("experts", "dp"), None),
            P("section", ("experts", "dp"), None),
            P("section", ("experts", "dp"), None),
            P("section", None, ("experts", "dp")),
            P("section", None, ("experts", "dp")),
            P(("experts", "dp"), "section"),
            P(("experts", "dp"), "section"),
            P("experts", "section", "dp"),
            P("experts", "dp", "section"),
        ),
        check_vma=False,
    )
```

```python
import functools

import jax
import jax.numpy as jnp
from jax import lax
from jax.experimental import pallas as pl
from jax.experimental.pallas import tpu as pltpu
from jax.sharding import PartitionSpec as P

HEADS = 12
HEAD_DIM = 64
SEQ = 197


eps = 1e-06


def pair(block):
    return lax.ppermute(block, "section", [(0, 1), (1, 0)])


def layer_norm(values, gain, bias):
    centred = values - jnp.mean(values, axis=-1, keepdims=True)
    spread = jnp.mean(centred * centred, axis=-1, keepdims=True)
    return centred * lax.rsqrt(spread + eps) * gain + bias


def norm_back(values, gain, bias, cotan):
    _, pull = jax.vjp(layer_norm, values, gain, bias)
    return pull(cotan)


def gelu_back(before, cotan):
    _, pull = jax.vjp(jax.nn.gelu, before)
    return pull(cotan)[0]


def matmul(left, right):
    return jnp.dot(left, right, preferred_element_type=jnp.float32)


def matmul_rows(left, right):
    return lax.dot_general(
        left, right, (((0,), (0,)), ((), ())), preferred_element_type=jnp.float32
    )


def matmul_cols(left, right):
    return lax.dot_general(
        left, right, (((1,), (1,)), ((), ())), preferred_element_type=jnp.float32
    )


def head_split(mixed):
    return mixed.reshape(-1, SEQ, 3, HEADS, HEAD_DIM)


def score_table(split):
    return jnp.einsum(
        "bqhd,bkhd->bhqk", split[:, :, 0], split[:, :, 1], preferred_element_type=jnp.float32
    ) * HEAD_DIM ** (-0.5)


def attend(normed, weight_qkv):
    mixed = matmul(normed, weight_qkv).astype(jnp.bfloat16)
    split = head_split(mixed)
    scores = score_table(split)
    top = jnp.max(scores, axis=-1, keepdims=True)
    logsum = top + jnp.log(jnp.sum(jnp.exp(scores - top), axis=-1, keepdims=True))
    probs = jnp.exp(scores - logsum).astype(jnp.bfloat16)
    attended = jnp.einsum(
        "bhqk,bkhd->bqhd", probs, split[:, :, 2], preferred_element_type=jnp.float32
    )
    return (mixed, logsum, attended.reshape(normed.shape[0], -1).astype(jnp.bfloat16))


def attend_back(normed, mixed, logsum, attended, grad_hidden, weight_qkv, weight_out):
    grad_cast = grad_hidden.astype(jnp.bfloat16)
    grad_att = matmul_cols(grad_cast, weight_out).astype(jnp.bfloat16)
    split = head_split(mixed)
    probs_full = jnp.exp(score_table(split) - logsum)
    probs = probs_full.astype(jnp.bfloat16)
    grad_heads = grad_att.reshape(-1, SEQ, HEADS, HEAD_DIM)
    grad_probs = jnp.einsum(
        "bqhd,bkhd->bhqk", grad_heads, split[:, :, 2], preferred_element_type=jnp.float32
    )
    grad_value = jnp.einsum(
        "bhqk,bqhd->bkhd", probs, grad_heads, preferred_element_type=jnp.float32
    )
    inner = jnp.sum(probs_full * grad_probs, axis=-1, keepdims=True)
    grad_scores = (probs_full * (grad_probs - inner) * HEAD_DIM ** (-0.5)).astype(jnp.bfloat16)
    grad_query = jnp.einsum(
        "bhqk,bkhd->bqhd", grad_scores, split[:, :, 1], preferred_element_type=jnp.float32
    )
    grad_key = jnp.einsum(
        "bhqk,bqhd->bkhd", grad_scores, split[:, :, 0], preferred_element_type=jnp.float32
    )
    grad_mixed = (
        jnp.stack([grad_query, grad_key, grad_value], axis=2)
        .reshape(normed.shape[0], -1)
        .astype(jnp.bfloat16)
    )
    return (matmul_cols(grad_mixed, weight_qkv), grad_mixed, grad_cast)


def front_half(block_in, gains, biases, weight_qkv, weight_out):
    start = block_in.astype(jnp.float32)
    normed = layer_norm(start, gains[0], biases[0]).astype(jnp.bfloat16)
    mixed, logsum, attended = attend(normed, weight_qkv)
    hidden = start + matmul(attended, weight_out)
    second = layer_norm(hidden, gains[1], biases[1]).astype(jnp.bfloat16)
    return (normed, mixed, logsum, attended, hidden, second)


def front_back(block_in, saved, grad_top, grad_second, gains, biases, weight_qkv, weight_out):
    normed, mixed, logsum, attended, hidden = saved
    grad_mid, gain_two, bias_two = norm_back(hidden, gains[1], biases[1], grad_second)
    grad_hidden = grad_top + grad_mid
    grad_normed, grad_mixed, grad_cast = attend_back(
        normed, mixed, logsum, attended, grad_hidden, weight_qkv, weight_out
    )
    grad_start, gain_one, bias_one = norm_back(
        block_in.astype(jnp.float32), gains[0], biases[0], grad_normed
    )
    return (
        grad_start + grad_hidden,
        jnp.stack([gain_one, gain_two, bias_one, bias_two]),
        grad_mixed,
        grad_cast,
    )


def rounded(values):
    return lax.reduce_precision(values, exponent_bits=8, mantissa_bits=7).astype(jnp.bfloat16)


TILE = 384
MESH = pl.DeviceIdType.MESH


def group_chunks(tiles):
    return [(at, 1) for at in range(tiles)]


def tail_kernel(
    experts,
    places,
    *refs,
):
    lefts, rights = [refs[0:6], refs[6:12]], [refs[12:17], refs[17:22]]
    count = 22
    mixed_in, grad_att_in, weight, block_in, gain, grad_hidden, norm_in = refs[count : count + 7]
    dense_out_sum, dense_in_sum, qkv_sum, out_sum, norm_out, grad_own, grad_other = refs[
        count + 7 : count + 14
    ]
    (
        near_in,
        far_out,
        far_in,
        group_out,
        group_in,
        norm_near,
        norm_mid,
        norm_far,
        near_send,
        near_recv,
        far_send,
        far_recv,
        group_send,
        group_recv,
        norm_send,
        norm_recv,
        norm_group_send,
        norm_group_recv,
        swap_out,
        swap_in,
        swap_send,
        swap_recv,
        right_own,
        grad_mixed,
        late,
        norm_own,
        norm_pair,
        pair_send,
        pair_recv,
        mixed,
        grad_att,
        grad_normed,
    ) = refs[count + 14 :]
    shard = lax.axis_index("dp")
    group = lax.axis_index("experts")
    section = lax.axis_index("section")
    low = shard % 2
    high = shard // 2
    peers = {0: shard, 1: shard + 1 - 2 * low, 2: shard + 2 - 4 * high, 3: 3 - shard}
    groups = [(group + step) % experts for step in range(experts)]
    tiles = len(places)
    batch = 4
    chunks = group_chunks(tiles)

    barrier = pltpu.get_barrier_semaphore()
    for mask in (1, 2, 3):
        pl.semaphore_signal(barrier, 1, device_id={"dp": peers[mask]}, device_id_type=MESH)
    for step in range(1, experts):
        pl.semaphore_signal(barrier, 1, device_id={"experts": groups[step]}, device_id_type=MESH)

    pl.semaphore_signal(barrier, 1, device_id={"section": 1 - section}, device_id_type=MESH)

    def block(tile, mask):
        return late.at[tile, :, peers[mask], :, :]

    def order(tile):
        return (1, 2) if tile % 2 == 0 else (2, 1)

    def near_copy(tile, part):
        near = order(tile)[0]
        return pltpu.make_async_remote_copy(
            block(tile, (3, near)[part]),
            near_in.at[tile, part],
            near_send.at[2 * tile + part],
            near_recv.at[2 * tile + part],
            device_id={"dp": peers[near]},
            device_id_type=MESH,
        )

    def far_copy(tile):
        return pltpu.make_async_remote_copy(
            far_out.at[tile],
            far_in.at[tile],
            far_send.at[tile],
            far_recv.at[tile],
            device_id={"dp": peers[order(tile)[1]]},
            device_id_type=MESH,
        )

    def group_copy(chunk, step):
        span = pl.ds(*chunks[chunk])
        return pltpu.make_async_remote_copy(
            group_out.at[groups[step], span],
            group_in.at[step - 1, span],
            group_send.at[chunk * (experts - 1) + step - 1],
            group_recv.at[chunk * (experts - 1) + step - 1],
            device_id={"experts": groups[step]},
            device_id_type=MESH,
        )

    def norm_copy(mask):
        return pltpu.make_async_remote_copy(
            norm_own,
            norm_near.at[mask - 1],
            norm_send.at[mask - 1],
            norm_recv.at[mask - 1],
            device_id={"dp": peers[mask]},
            device_id_type=MESH,
        )

    def norm_group_copy(step):
        return pltpu.make_async_remote_copy(
            norm_mid,
            norm_far.at[step - 1],
            norm_group_send.at[step - 1],
            norm_group_recv.at[step - 1],
            device_id={"experts": groups[step]},
            device_id_type=MESH,
        )

    def wide(value):
        return value.astype(jnp.float32)

    pl.semaphore_wait(barrier, 4 + experts - 1)

    def start(tile):
        near_copy(tile, 0).start()
        near_copy(tile, 1).start()

    def turn(tile):
        near_copy(tile, 0).wait_recv()
        far = peers[order(tile)[1]]

        @pl.loop(0, experts)
        def _(at):
            far_out[tile, at] = (wide(late[tile, at, far]) + wide(near_in[tile, 0, at])).astype(
                jnp.bfloat16
            )

        far_copy(tile).start()

    def finish(tile):
        near_copy(tile, 1).wait_recv()
        far_copy(tile).wait_recv()

        @pl.loop(0, experts)
        def _(at):
            group_out[at, tile] = (
                wide(late[tile, at, shard]) + wide(near_in[tile, 1, at]) + wide(far_in[tile, at])
            ).astype(jnp.bfloat16)

        for chunk, (begin, count) in enumerate(chunks):
            if tile == begin + count - 1:
                for step in range(1, experts):
                    group_copy(chunk, step).start()

    def pair_copy(index, source, target):
        return pltpu.make_async_remote_copy(
            source,
            target,
            pair_send.at[index],
            pair_recv.at[index],
            device_id={"section": 1 - section},
            device_id_type=MESH,
        )

    width = grad_att.shape[1]
    spaced = grad_att.shape[0]
    scale = HEAD_DIM ** (-0.5)
    valid = lax.broadcasted_iota(jnp.int32, (spaced, spaced), 1) < SEQ

    def dot(one, other, dims):
        return lax.dot_general(one, other, ((dims[:1], dims[1:]), ((), ())), preferred_element_type=jnp.float32)

    parts = width // TILE
    each = experts // parts

    def make(tile):
        which, span = places[tile]

        def right(side):
            columns = slice(span, span + TILE)
            if which < 5:
                return rights[side][which][:, columns]
            return right_own[side * spaced : side * spaced + SEQ, columns]

        @pl.loop(0, parts)
        def _(at):
            rows = pl.ds(pl.multiple_of(at * TILE, TILE), TILE)
            product = dot(lefts[0][which][:, rows], right(0), (0, 0)) + dot(
                lefts[1][which][:, rows], right(1), (0, 0)
            )
            product = product.astype(jnp.bfloat16).reshape((each,) + late.shape[2:])
            for inner in range(each):
                late[tile, at * each + inner] = product[inner]

    def make_folded():
        shards = late.shape[2]
        step = TILE // (batch * late.shape[3])

        @pl.loop(0, experts * shards // step)
        def _(at):
            rows = pl.ds(pl.multiple_of(at * TILE, TILE), TILE)
            product = dot(lefts[0][1][:, rows], rights[0][1][...], (0, 0)) + dot(
                lefts[1][1][:, rows], rights[1][1][...], (0, 0)
            )
            product = product.astype(jnp.bfloat16).reshape((step, batch) + late.shape[3:])
            place = at * step
            for inner in range(step):
                for fold in range(batch):
                    late[batch + fold, place // shards, place % shards + inner] = product[
                        inner, fold
                    ]

    done = []

    def pump(amount):
        for _ in range(amount):
            step = len(done)
            done.append(step)
            if step == batch:
                make_folded()
            if step < tiles:
                if places[step][0] != 1:
                    make(step)
                start(step)
            if 0 <= step - 2 < tiles:
                turn(step - 2)
            if 0 <= step - 3 < tiles:
                finish(step - 3)

    pump(2)
    mixed[...] = jnp.zeros_like(mixed)
    grad_att[...] = jnp.zeros_like(grad_att)
    mixed[0:SEQ] = mixed_in[...]
    grad_att[0:SEQ] = grad_att_in[...]

    def head_pair(at):
        def columns(part):
            return pl.ds(pl.multiple_of(part * width + at * 2 * HEAD_DIM, 2 * HEAD_DIM), 2 * HEAD_DIM)

        queries, keys, values = [mixed[:, columns(part)] for part in range(3)]
        grads = grad_att[:, columns(0)]
        made = []
        for half in range(2):
            span = slice(half * HEAD_DIM, (half + 1) * HEAD_DIM)
            query, key, value, grad = queries[:, span], keys[:, span], values[:, span], grads[:, span]
            scores = dot(query, key, (1, 1)) * scale
            top = jnp.max(jnp.where(valid, scores, -jnp.inf), axis=1, keepdims=True)
            raised = jnp.where(valid, jnp.exp(scores - top), 0.0)
            full = raised / jnp.sum(raised, axis=1, keepdims=True)
            probs = full.astype(jnp.bfloat16)
            grad_probs = dot(grad, value, (1, 1))
            inner = jnp.sum(full * grad_probs, axis=1, keepdims=True)
            grad_scores = (full * (grad_probs - inner) * scale).astype(jnp.bfloat16)
            made.append(
                (
                    dot(grad_scores, key, (1, 0)),
                    dot(grad_scores, query, (0, 0)),
                    dot(probs, grad, (0, 0)),
                )
            )
        for part in range(3):
            grad_mixed[:, columns(part)] = jnp.concatenate(
                [made[0][part], made[1][part]], axis=1
            ).astype(jnp.bfloat16)

    pairs = HEADS // 2
    for third in range(3):
        pl.loop(third * pairs // 3, (third + 1) * pairs // 3)(head_pair)
        pump(2)

    cut = grad_mixed.shape[1] // 2
    kept = pl.ds(pl.multiple_of(section * cut, 128), cut)
    sent = pl.ds(pl.multiple_of((1 - section) * cut, 128), cut)
    mixed_copy = pair_copy(0, grad_mixed.at[:, sent], right_own.at[pl.ds(spaced, spaced)])
    mixed_copy.start()
    right_own[0:spaced] = grad_mixed[:, kept]

    rows_at = 256

    pump(1)

    @pl.loop(0, width // rows_at)
    def _(at):
        span = pl.ds(pl.multiple_of(at * rows_at, rows_at), rows_at)
        grad_normed[:, span] = dot(grad_mixed[...], weight[span, :], (1, 1))

    pump(1)
    mixed_copy.wait()
    pump(1)
    start_values = wide(block_in[...])
    centred = start_values - jnp.mean(start_values, axis=1, keepdims=True)
    root = lax.rsqrt(jnp.mean(centred * centred, axis=1, keepdims=True) + eps)
    unit = centred * root
    cotan = grad_normed[0:SEQ]
    norm_pair[0, 0:1, :] = jnp.sum(cotan * unit, axis=0, keepdims=True)
    norm_pair[0, 1:2, :] = jnp.sum(cotan, axis=0, keepdims=True)
    norm_copy_pair = pair_copy(1, norm_pair.at[0], norm_pair.at[1])
    norm_copy_pair.start()
    scaled = cotan * gain[0:1, :]
    grad_own[0:SEQ] = grad_hidden[...] + root * (
        scaled
        - jnp.mean(scaled, axis=1, keepdims=True)
        - unit * jnp.mean(scaled * unit, axis=1, keepdims=True)
    )
    grad_copy = pair_copy(2, grad_own, grad_other)
    grad_copy.start()
    norm_copy_pair.wait()
    chosen = jnp.where(section == 0, 1.0, 0.0)
    norm_own[...] = norm_in[...]
    norm_own[0:1, :] = norm_in[0:1, :] + chosen * (norm_pair[0, 0:1, :] + norm_pair[1, 0:1, :])
    norm_own[2:3, :] = norm_in[2:3, :] + chosen * (norm_pair[0, 1:2, :] + norm_pair[1, 1:2, :])
    for mask in (1, 2, 3):
        norm_copy(mask).start()

    pump(4)
    for mask in (1, 2, 3):
        norm_copy(mask).wait()
    norm_mid[...] = (norm_own[...] + norm_near[0]) + (norm_near[1] + norm_near[2])
    for other in range(1, experts):
        norm_group_copy(other).start()
    pump(tiles + 3 - len(done))

    grad_copy.wait()
    norm_total = norm_mid[...]
    for step in range(1, experts):
        norm_group_copy(step).wait()
        norm_total = norm_total + norm_far[step - 1]
    norm_out[...] = norm_total

    def total_of(tile):
        total = wide(group_out[group, tile])
        for step in range(1, experts):
            total = total + wide(group_in[step - 1, tile])
        return total

    size = dense_in_sum.shape[0]
    for chunk, (begin, length) in enumerate(chunks):
        for step in range(1, experts):
            group_copy(chunk, step).wait_recv()
        for tile in range(begin, begin + length):
            total = total_of(tile)
            which, at = tile // batch, tile % batch
            if which == 1:
                dense_out_sum[at * size : (at + 1) * size] = total
            elif which == 0:
                dense_in_sum[:, at * TILE : (at + 1) * TILE] = total
            else:
                swap_out[which - 2, at] = total

    swap = pltpu.make_async_remote_copy(
        swap_out.at[section],
        swap_in,
        swap_send,
        swap_recv,
        device_id={"section": 1 - section},
        device_id_type=MESH,
    )
    swap.start()

    def place(half, parts):
        cut = qkv_sum.shape[1] // 2
        for at in range(batch - 1):
            start_at = pl.multiple_of(half * cut + at * TILE, 128)
            qkv_sum[:, pl.ds(start_at, TILE)] = parts[at + 1]
        out_sum[:, pl.ds(pl.multiple_of(half * TILE, 128), TILE)] = parts[0]

    place(section, swap_out[1 - section])
    swap.wait()
    place(1 - section, swap_in[...])

    for tile in range(tiles):
        near_copy(tile, 0).wait_send()
        near_copy(tile, 1).wait_send()
        far_copy(tile).wait_send()
    for chunk in range(len(chunks)):
        for step in range(1, experts):
            group_copy(chunk, step).wait_send()


def tail_sums(experts, shards, sides, left, mixed, grad_att, weight, block_in, gain, grad_hidden, norms):
    width = grad_att.shape[1]
    size = width // (experts * shards)
    places = [(0, at * TILE) for at in range(4)] + [(1, 0)] * 4
    places += [(3, 0)] + [(2, at * TILE) for at in range(3)]
    places += [(4, 0)] + [(5, at * TILE) for at in range(3)]
    tiles = len(places)
    lefts = [side[0] for side in sides] + [left]
    rights = [side[1] for side in sides]
    inputs = [array[side] for arrays in (lefts, rights) for side in (0, 1) for array in arrays]
    assert [array[0].shape[1] // TILE for array in rights] == [4, 1, 3, 1, 1]
    spaced = -(-mixed.shape[0] // 256) * 256
    folds = 4
    full = (tiles, experts, size, TILE)
    dma = pltpu.SemaphoreType.DMA
    half = jnp.bfloat16
    return pl.pallas_call(
        functools.partial(tail_kernel, experts, places),
        out_shape=(
            jax.ShapeDtypeStruct((folds * size, TILE), jnp.float32),
            jax.ShapeDtypeStruct((size, 4 * TILE), jnp.float32),
            jax.ShapeDtypeStruct((size, 6 * TILE), jnp.float32),
            jax.ShapeDtypeStruct((size, 2 * TILE), jnp.float32),
            jax.ShapeDtypeStruct(norms.shape, jnp.float32),
            jax.ShapeDtypeStruct(block_in.shape, jnp.float32),
            jax.ShapeDtypeStruct(block_in.shape, jnp.float32),
        ),
        in_specs=[pl.BlockSpec(memory_space=pltpu.VMEM)] * (len(inputs) + 7),
        out_specs=(pl.BlockSpec(memory_space=pltpu.VMEM),) * 7,
        scratch_shapes=[
            pltpu.VMEM((tiles, 2) + full[1:], half),
            pltpu.VMEM(full, half),
            pltpu.VMEM(full, half),
            pltpu.VMEM((experts, tiles, size, TILE), half),
            pltpu.VMEM((experts - 1, tiles, size, TILE), half),
            pltpu.VMEM((shards - 1,) + norms.shape, jnp.float32),
            pltpu.VMEM(norms.shape, jnp.float32),
            pltpu.VMEM((experts - 1,) + norms.shape, jnp.float32),
            dma((2 * tiles,)),
            dma((2 * tiles,)),
            dma((tiles,)),
            dma((tiles,)),
            dma((len(group_chunks(tiles)) * (experts - 1),)),
            dma((len(group_chunks(tiles)) * (experts - 1),)),
            dma((shards - 1,)),
            dma((shards - 1,)),
            dma((experts - 1,)),
            dma((experts - 1,)),
            pltpu.VMEM((2, 4, size, TILE), jnp.float32),
            pltpu.VMEM((4, size, TILE), jnp.float32),
            dma,
            dma,
            pltpu.VMEM((2 * spaced, mixed.shape[1] // 2), half),
            pltpu.VMEM((spaced, mixed.shape[1]), half),
            pltpu.VMEM((tiles, experts, shards, size, TILE), half),
            pltpu.VMEM(norms.shape, jnp.float32),
            pltpu.VMEM((2,) + norms.shape, jnp.float32),
            dma((3,)),
            dma((3,)),
            pltpu.VMEM((spaced, mixed.shape[1]), half),
            pltpu.VMEM((spaced, width), half),
            pltpu.VMEM((spaced, width), jnp.float32),
        ],
        compiler_params=pltpu.CompilerParams(
            collective_id=0, has_side_effects=True, vmem_limit_bytes=58 * 2**20
        ),
        cost_estimate=pl.CostEstimate(
            flops=10**7, bytes_accessed=10**7, transcendentals=0
        ),
    )(*inputs, mixed, grad_att, weight, block_in, gain, grad_hidden, norms)


def on_device(
    tokens,
    cotangent,
    norm_gains,
    norm_biases,
    qkv_weight,
    out_weight,
    dense_in,
    dense_out,
    expert_in,
    expert_out,
    routes,
    gates,
):
    rows = SEQ
    width = tokens.shape[1]
    experts = lax.axis_size("experts")
    shards = lax.axis_size("dp")
    capacity = 2 * rows // experts
    padded = -(-capacity // 8) * 8
    slots = experts * padded
    section = lax.axis_index("section")
    group = lax.axis_index("experts")
    shard = lax.axis_index("dp")
    first = section == 0

    def ordered(mine, other, axis):
        return jnp.concatenate(
            [jnp.where(first, mine, other), jnp.where(first, other, mine)], axis=axis
        )

    def kept_half(array, axis):
        low, high = jnp.split(array, 2, axis=axis)
        return jnp.where(first, low, high)

    def sent_half(array, axis):
        low, high = jnp.split(array, 2, axis=axis)
        return jnp.where(first, high, low)

    def both(own):
        other = pair(own)
        return (jnp.where(first, own, other), jnp.where(first, other, own))

    def across(array, mask):
        return lax.ppermute(array, "dp", [(i, i ^ mask) for i in range(shards)])

    def shifted(array, step):
        return lax.ppermute(
            array, "experts", [(i, (i + step) % experts) for i in range(experts)]
        )

    def wide(array):
        return array.astype(jnp.float32)

    def shard_sum(block, near, far):
        passed = across(block(3).astype(jnp.bfloat16), near)
        direct = across(block(near).astype(jnp.bfloat16), near)
        turned = across((block(far) + wide(passed)).astype(jnp.bfloat16), far)
        return block(0) + wide(direct) + wide(turned)

    def group_sum(array):
        own = lax.dynamic_index_in_dim(array, group, 0, False)
        total = wide(own)
        for step in range(1, experts):
            target = lax.rem(group + step, experts)
            total = total + wide(
                shifted(lax.dynamic_index_in_dim(array, target, 0, False), step)
            )
        return total

    def everyone_sum(left, right, near, far):
        blocks = left.reshape(experts, shards, -1, left.shape[1])

        def block(mask):
            part = lax.dynamic_index_in_dim(blocks, shard ^ mask, 1, False)
            return matmul(part.reshape(-1, left.shape[1]), right)

        total = shard_sum(block, near, far).astype(jnp.bfloat16)
        return group_sum(total.reshape(experts, -1, right.shape[1]))

    def padded_rows(array):
        return jnp.pad(array, ((0, -array.shape[0] % 256), (0, 0)))

    def joined(own, other):
        return jnp.concatenate([padded_rows(own), padded_rows(other)], axis=0)

    kernel_fits = experts == 4 and shards == 4

    def partial_grad(both_sides):
        left, right = both_sides
        if kernel_fits:
            return ((left, pair(left)), (kept_half(right, 1), pair(sent_half(right, 1))))
        left = joined(left, pair(left))
        right = joined(kept_half(right, 1), pair(sent_half(right, 1)))
        return (left.T, right)

    qkv_zero, qkv_one = both(qkv_weight[0])
    norms_zero, norms_one = both(jnp.concatenate([norm_gains[0], norm_biases[0]], axis=0))
    out_zero, out_one = both(out_weight[0])

    def own_block(array):
        return lax.dynamic_slice_in_dim(array, section * rows, rows, 0)

    block_in = own_block(tokens)
    grad_top = own_block(cotangent).astype(jnp.float32)
    chosen = own_block(routes)
    gate_pair = own_block(gates)

    flat = jnp.concatenate([chosen[:, 0], chosen[:, 1]])
    order = jnp.arange(2 * rows, dtype=jnp.int32)
    place = jnp.sum(
        ((flat[:, None] == flat[None, :]) & (order[None, :] < order[:, None])).astype(jnp.int32),
        axis=1,
        dtype=jnp.int32,
    )
    step_of = lax.rem(flat - group + experts, experts)
    slot = jnp.where(place < capacity, step_of * padded + place, slots)
    gate_flat = jnp.concatenate([gate_pair[:, 0], gate_pair[:, 1]])
    spread = (jnp.arange(slots, dtype=jnp.int32)[:, None] == slot[None, :]).astype(jnp.bfloat16)
    spread_both = spread[:, :rows] + spread[:, rows:]

    def sent_out(array):
        parts = [array[k * padded : (k + 1) * padded] for k in range(experts)]
        return jnp.concatenate([parts[0]] + [shifted(parts[k], k) for k in range(1, experts)])

    def sent_home(array):
        parts = [array[k * padded : (k + 1) * padded] for k in range(experts)]
        return jnp.concatenate(
            [parts[0]] + [shifted(parts[k], experts - k) for k in range(1, experts)]
        )

    doubled = (jnp.concatenate([grad_top, grad_top]) * gate_flat[:, None]).astype(jnp.bfloat16)
    grad_outgoing = matmul(spread, doubled).astype(jnp.bfloat16)

    piece_in = kept_half(expert_in[0], 1)
    piece_back = kept_half(expert_out[0], 0)
    near = lax.all_gather(jnp.concatenate([piece_in.T, piece_back], axis=0), "dp", axis=0)

    normed0, mixed0, logsum0, attended0, hidden0, second0 = front_half(
        block_in, norms_zero[:2], norms_zero[2:], qkv_zero, out_zero
    )
    grad_outgoing, second0 = lax.optimization_barrier((grad_outgoing, second0))
    grad_rows = sent_out(grad_outgoing)
    before0 = matmul(second0, dense_in)
    active0 = jax.nn.gelu(before0).astype(jnp.bfloat16)
    middle = rounded(hidden0 + matmul(active0, dense_out))

    normed1, mixed1, logsum1, attended1, hidden1, second1 = front_half(
        middle, norms_one[:2], norms_one[2:], qkv_one, out_one
    )
    second1, grad_rows = lax.optimization_barrier((second1, grad_rows))
    rows_in = sent_out(matmul(spread_both, second1).astype(jnp.bfloat16))

    near, rows_in = lax.optimization_barrier((near, rows_in))
    gathered = (near, pair(near))
    hidden_share = piece_back.shape[0]
    weights_in = [both[:, :hidden_share].reshape(-1, width) for both in gathered]
    weights_back = [both[:, hidden_share:].reshape(-1, width) for both in gathered]
    before1 = [matmul_cols(rows_in, weight) for weight in weights_in]
    active1 = [jax.nn.gelu(before).astype(jnp.bfloat16) for before in before1]
    grad_before1 = [
        gelu_back(before, matmul_cols(grad_rows, weight)).astype(jnp.bfloat16)
        for before, weight in zip(before1, weights_back)
    ]
    grad_arrived = (
        matmul(grad_before1[0], weights_in[0]) + matmul(grad_before1[1], weights_in[1])
    ).astype(jnp.bfloat16)
    grad_home = sent_home(grad_arrived)
    returned = (
        matmul(active1[0], weights_back[0]) + matmul(active1[1], weights_back[1])
    ).astype(jnp.bfloat16)
    returned_home = sent_home(returned)

    def expert_parts(halves, right):
        landed = [pair(half) for half in halves]
        lefts = [
            jnp.concatenate([halves[0], landed[1]], axis=0),
            jnp.concatenate([halves[1], landed[0]], axis=0),
        ]
        right = jnp.concatenate([kept_half(right, 1), pair(sent_half(right, 1))], axis=0)
        return [matmul_rows(left, right).astype(jnp.bfloat16) for left in lefts]

    expert_in_parts = expert_parts(grad_before1, rows_in)
    expert_out_parts = expert_parts(active1, grad_rows)
    expert_stack = jnp.concatenate(expert_in_parts + expert_out_parts, axis=1)
    grad_home, expert_stack = lax.optimization_barrier((grad_home, expert_stack))
    expert_shard = lax.psum_scatter(expert_stack, "dp", scatter_dimension=0, tiled=True)
    parts = jnp.split(expert_shard, 4, axis=1)
    expert_in_sum = ordered(parts[0], parts[1], 0).astype(jnp.float32)
    expert_out_sum = ordered(parts[2], parts[3], 0).astype(jnp.float32)

    picked = matmul_rows(spread, returned_home) * gate_flat[:, None]
    final = (hidden1 + (picked[:rows] + picked[rows:])).astype(jnp.bfloat16)
    grad_second1 = matmul_rows(spread_both, grad_home)
    grad_middle, grad_norm1, grad_mixed1, grad_cast1 = front_back(
        middle,
        (normed1, mixed1, logsum1, attended1, hidden1),
        grad_top,
        grad_second1,
        norms_one[:2],
        norms_one[2:],
        qkv_one,
        out_one,
    )

    grad_result = rounded(grad_middle)
    grad_before0 = gelu_back(before0, matmul_cols(grad_result, dense_out)).astype(jnp.bfloat16)
    dense_out_part = partial_grad((active0, grad_result))
    dense_in_part = partial_grad((second0, grad_before0))
    qkv_part1 = partial_grad((normed1, grad_mixed1))
    out_part1 = partial_grad((attended1, grad_cast1))
    grad_second0 = matmul_cols(grad_before0, dense_in)
    saved0 = (normed0, mixed0, logsum0, attended0, hidden0)
    if not kernel_fits:
        grad_tokens, grad_norm0, grad_mixed0, grad_cast0 = front_back(
            block_in,
            saved0,
            grad_result.astype(jnp.float32),
            grad_second0,
            norms_zero[:2],
            norms_zero[2:],
            qkv_zero,
            out_zero,
        )
        qkv_part0 = partial_grad((normed0, grad_mixed0))
    else:
        grad_mid0, gain_two0, bias_two0 = norm_back(
            hidden0, norms_zero[1], norms_zero[3], grad_second0
        )
        grad_hidden0 = grad_result.astype(jnp.float32) + grad_mid0
        grad_cast0 = grad_hidden0.astype(jnp.bfloat16)
        grad_att0 = matmul_cols(grad_cast0, out_zero).astype(jnp.bfloat16)
        nothing = jnp.zeros_like(gain_two0)
        grad_norm0 = jnp.stack([nothing, gain_two0, nothing, bias_two0])
    out_part0 = partial_grad((attended0, grad_cast0))
    norm_pair = jnp.where(first, grad_norm0, grad_norm1) + pair(
        jnp.where(first, grad_norm1, grad_norm0)
    )
    rest = [dense_in_part, qkv_part1, out_part1]
    if kernel_fits:
        eight = jnp.zeros((8, width), jnp.float32)
        dense_out_sum, dense_in_sum, qkv_sum, out_sum, norm_sum, grad_tokens, grad_landed = tail_sums(
            experts,
            shards,
            [dense_in_part, dense_out_part, qkv_part1, out_part1, out_part0],
            (normed0, pair(normed0)),
            mixed0,
            grad_att0,
            qkv_zero,
            block_in,
            eight.at[0].set(norms_zero[0]),
            grad_hidden0,
            eight.at[:4].set(norm_pair),
        )
        size = width // (experts * shards)
        norm_sum = lax.dynamic_slice(norm_sum[:4], (0, (group * shards + shard) * size), (4, size))
        middle_landed = pair(grad_middle)
        act_grads = jnp.concatenate(
            [
                jnp.where(first, grad_tokens, middle_landed),
                jnp.where(first, grad_landed, grad_middle),
            ]
        )
    else:
        dense_out_sum = everyone_sum(*dense_out_part, 1, 2)
        dense_in_sum, qkv_one, out_one, qkv_zero, out_zero = [
            everyone_sum(*part, 2, 1).astype(jnp.bfloat16)
            for part in rest + [qkv_part0, out_part0]
        ]
        own_shared, other_shared = [
            jnp.where(first, *halves)
            for halves in (
                (
                    jnp.concatenate([qkv_zero, out_zero], axis=1),
                    jnp.concatenate([qkv_one, out_one], axis=1),
                ),
                (
                    jnp.concatenate([qkv_one, out_one], axis=1),
                    jnp.concatenate([qkv_zero, out_zero], axis=1),
                ),
            )
        ]
        other_shared = pair(other_shared)
        cut = qkv_zero.shape[1]
        qkv_sum = ordered(own_shared[:, :cut], other_shared[:, :cut], 1).astype(jnp.float32)
        out_sum = ordered(own_shared[:, cut:], other_shared[:, cut:], 1).astype(jnp.float32)
        dense_in_sum = dense_in_sum.astype(jnp.float32)
        norm_sum = lax.psum_scatter(
            norm_pair.T, ("experts", "dp"), scatter_dimension=0, tiled=True
        ).T
        act_grads = ordered(
            jnp.where(first, grad_tokens, grad_middle),
            pair(jnp.where(first, grad_middle, grad_tokens)),
            0,
        )

    acts = ordered(
        jnp.where(first, middle, final), pair(jnp.where(first, final, middle)), 0
    )
    return (
        acts[None],
        act_grads[None],
        qkv_sum[None],
        out_sum[None],
        norm_sum[:2][None],
        norm_sum[2:][None],
        dense_in_sum,
        dense_out_sum,
        expert_in_sum.T[None],
        expert_out_sum[None],
    )


def solution(mesh):
    placed = (
        P(("experts", "dp"), None),
        P(("experts", "dp"), None),
        P("section", None, None),
        P("section", None, None),
        P("section", None, None),
        P("section", None, None),
        P(),
        P(),
        P("experts", None, "dp"),
        P("experts", "dp", None),
        P(("experts", "dp"), None),
        P(("experts", "dp"), None),
    )
    return jax.shard_map(
        on_device,
        mesh=mesh,
        in_specs=placed,
        out_specs=(
            P("section", ("experts", "dp"), None),
            P("section", ("experts", "dp"), None),
            P("section", ("experts", "dp"), None),
            P("section", ("experts", "dp"), None),
            P("section", None, ("experts", "dp")),
            P("section", None, ("experts", "dp")),
            P(("experts", "dp"), "section"),
            P(("experts", "dp"), "section"),
            P("experts", "section", "dp"),
            P("experts", "dp", "section"),
        ),
        check_vma=False,
    )
```

```python
import functools

import jax
import jax.numpy as jnp
from jax import lax
from jax.experimental import pallas as pl
from jax.experimental.layout import Layout, with_layout_constraint
from jax.experimental.pallas import tpu as pltpu
from jax.sharding import PartitionSpec as P

HEADS = 12
HEAD_DIM = 64
SEQ = 197


eps = 1e-06


def pair(block):
    return lax.ppermute(block, "section", [(0, 1), (1, 0)])


def layer_norm(values, gain, bias):
    centred = values - jnp.mean(values, axis=-1, keepdims=True)
    spread = jnp.mean(centred * centred, axis=-1, keepdims=True)
    return centred * lax.rsqrt(spread + eps) * gain + bias


def norm_back(values, gain, bias, cotan):
    _, pull = jax.vjp(layer_norm, values, gain, bias)
    return pull(cotan)


def gelu_back(before, cotan):
    _, pull = jax.vjp(jax.nn.gelu, before)
    return pull(cotan)[0]


def matmul(left, right):
    return jnp.dot(left, right, preferred_element_type=jnp.float32)


def matmul_rows(left, right):
    return lax.dot_general(
        left, right, (((0,), (0,)), ((), ())), preferred_element_type=jnp.float32
    )


def matmul_cols(left, right):
    return lax.dot_general(
        left, right, (((1,), (1,)), ((), ())), preferred_element_type=jnp.float32
    )


def head_split(mixed):
    return mixed.reshape(-1, SEQ, 3, HEADS, HEAD_DIM)


def score_table(split):
    return jnp.einsum(
        "bqhd,bkhd->bhqk", split[:, :, 0], split[:, :, 1], preferred_element_type=jnp.float32
    ) * HEAD_DIM ** (-0.5)


def attend(normed, weight_qkv):
    mixed = matmul(normed, weight_qkv).astype(jnp.bfloat16)
    split = head_split(mixed)
    scores = score_table(split)
    top = jnp.max(scores, axis=-1, keepdims=True)
    logsum = top + jnp.log(jnp.sum(jnp.exp(scores - top), axis=-1, keepdims=True))
    probs = jnp.exp(scores - logsum).astype(jnp.bfloat16)
    attended = jnp.einsum(
        "bhqk,bkhd->bqhd", probs, split[:, :, 2], preferred_element_type=jnp.float32
    )
    return (mixed, logsum, attended.reshape(normed.shape[0], -1).astype(jnp.bfloat16))


def attend_back(normed, mixed, logsum, attended, grad_hidden, weight_qkv, weight_out):
    grad_cast = grad_hidden.astype(jnp.bfloat16)
    grad_att = matmul_cols(grad_cast, weight_out).astype(jnp.bfloat16)
    split = head_split(mixed)
    probs_full = jnp.exp(score_table(split) - logsum)
    probs = probs_full.astype(jnp.bfloat16)
    grad_heads = grad_att.reshape(-1, SEQ, HEADS, HEAD_DIM)
    grad_probs = jnp.einsum(
        "bqhd,bkhd->bhqk", grad_heads, split[:, :, 2], preferred_element_type=jnp.float32
    )
    grad_value = jnp.einsum(
        "bhqk,bqhd->bkhd", probs, grad_heads, preferred_element_type=jnp.float32
    )
    inner = jnp.sum(probs_full * grad_probs, axis=-1, keepdims=True)
    grad_scores = (probs_full * (grad_probs - inner) * HEAD_DIM ** (-0.5)).astype(jnp.bfloat16)
    grad_query = jnp.einsum(
        "bhqk,bkhd->bqhd", grad_scores, split[:, :, 1], preferred_element_type=jnp.float32
    )
    grad_key = jnp.einsum(
        "bhqk,bqhd->bkhd", grad_scores, split[:, :, 0], preferred_element_type=jnp.float32
    )
    grad_mixed = (
        jnp.stack([grad_query, grad_key, grad_value], axis=2)
        .reshape(normed.shape[0], -1)
        .astype(jnp.bfloat16)
    )
    return (matmul_cols(grad_mixed, weight_qkv), grad_mixed, grad_cast)


def front_half(block_in, gains, biases, weight_qkv, weight_out):
    start = block_in.astype(jnp.float32)
    normed = layer_norm(start, gains[0], biases[0]).astype(jnp.bfloat16)
    mixed, logsum, attended = attend(normed, weight_qkv)
    hidden = start + matmul(attended, weight_out)
    second = layer_norm(hidden, gains[1], biases[1]).astype(jnp.bfloat16)
    return (normed, mixed, logsum, attended, hidden, second)


def front_back(block_in, saved, grad_top, grad_second, gains, biases, weight_qkv, weight_out):
    normed, mixed, logsum, attended, hidden = saved
    grad_mid, gain_two, bias_two = norm_back(hidden, gains[1], biases[1], grad_second)
    grad_hidden = grad_top + grad_mid
    grad_normed, grad_mixed, grad_cast = attend_back(
        normed, mixed, logsum, attended, grad_hidden, weight_qkv, weight_out
    )
    grad_start, gain_one, bias_one = norm_back(
        block_in.astype(jnp.float32), gains[0], biases[0], grad_normed
    )
    return (
        grad_start + grad_hidden,
        jnp.stack([gain_one, gain_two, bias_one, bias_two]),
        grad_mixed,
        grad_cast,
    )


def rounded(values):
    return lax.reduce_precision(values, exponent_bits=8, mantissa_bits=7).astype(jnp.bfloat16)


TILE = 384
MESH = pl.DeviceIdType.MESH


def group_chunks(tiles):
    return [(at, 1) for at in range(tiles)]


def tail_kernel(
    experts,
    places,
    *refs,
):
    lefts, rights = [refs[0:6], refs[6:12]], [refs[12:17], refs[17:22]]
    count = 22
    mixed_in, grad_att_in, weight, block_in, gain, grad_hidden, norm_in = refs[count : count + 7]
    dense_out_sum, dense_in_sum, qkv_sum, out_sum, norm_out, grad_own, grad_other = refs[
        count + 7 : count + 14
    ]
    (
        near_in,
        far_out,
        far_in,
        group_out,
        group_in,
        norm_near,
        norm_mid,
        norm_far,
        near_send,
        near_recv,
        far_send,
        far_recv,
        group_send,
        group_recv,
        norm_send,
        norm_recv,
        norm_group_send,
        norm_group_recv,
        swap_out,
        swap_in,
        swap_send,
        swap_recv,
        right_own,
        grad_mixed,
        late,
        norm_own,
        norm_pair,
        pair_send,
        pair_recv,
        mixed,
        grad_att,
        grad_normed,
    ) = refs[count + 14 :]
    shard = lax.axis_index("dp")
    group = lax.axis_index("experts")
    section = lax.axis_index("section")
    low = shard % 2
    high = shard // 2
    peers = {0: shard, 1: shard + 1 - 2 * low, 2: shard + 2 - 4 * high, 3: 3 - shard}
    groups = [(group + step) % experts for step in range(experts)]
    tiles = len(places)
    batch = 4
    chunks = group_chunks(tiles)

    barrier = pltpu.get_barrier_semaphore()
    for mask in (1, 2, 3):
        pl.semaphore_signal(barrier, 1, device_id={"dp": peers[mask]}, device_id_type=MESH)
    for step in range(1, experts):
        pl.semaphore_signal(barrier, 1, device_id={"experts": groups[step]}, device_id_type=MESH)

    pl.semaphore_signal(barrier, 1, device_id={"section": 1 - section}, device_id_type=MESH)

    def block(tile, mask):
        return late.at[tile, :, peers[mask], :, :]

    def order(tile):
        return (1, 2) if tile % 2 == 0 else (2, 1)

    def near_copy(tile, part):
        near = order(tile)[0]
        return pltpu.make_async_remote_copy(
            block(tile, (3, near)[part]),
            near_in.at[tile, part],
            near_send.at[2 * tile + part],
            near_recv.at[2 * tile + part],
            device_id={"dp": peers[near]},
            device_id_type=MESH,
        )

    def far_copy(tile):
        return pltpu.make_async_remote_copy(
            far_out.at[tile],
            far_in.at[tile],
            far_send.at[tile],
            far_recv.at[tile],
            device_id={"dp": peers[order(tile)[1]]},
            device_id_type=MESH,
        )

    def group_copy(chunk, step):
        span = pl.ds(*chunks[chunk])
        return pltpu.make_async_remote_copy(
            group_out.at[groups[step], span],
            group_in.at[step - 1, span],
            group_send.at[chunk * (experts - 1) + step - 1],
            group_recv.at[chunk * (experts - 1) + step - 1],
            device_id={"experts": groups[step]},
            device_id_type=MESH,
        )

    def norm_copy(mask):
        return pltpu.make_async_remote_copy(
            norm_own,
            norm_near.at[mask - 1],
            norm_send.at[mask - 1],
            norm_recv.at[mask - 1],
            device_id={"dp": peers[mask]},
            device_id_type=MESH,
        )

    def norm_group_copy(step):
        return pltpu.make_async_remote_copy(
            norm_mid,
            norm_far.at[step - 1],
            norm_group_send.at[step - 1],
            norm_group_recv.at[step - 1],
            device_id={"experts": groups[step]},
            device_id_type=MESH,
        )

    def wide(value):
        return value.astype(jnp.float32)

    pl.semaphore_wait(barrier, 4 + experts - 1)

    def start(tile):
        near_copy(tile, 0).start()
        near_copy(tile, 1).start()

    def turn(tile):
        near_copy(tile, 0).wait_recv()
        far = peers[order(tile)[1]]

        @pl.loop(0, experts)
        def _(at):
            far_out[tile, at] = (wide(late[tile, at, far]) + wide(near_in[tile, 0, at])).astype(
                jnp.bfloat16
            )

        far_copy(tile).start()

    def finish(tile):
        near_copy(tile, 1).wait_recv()
        far_copy(tile).wait_recv()

        @pl.loop(0, experts)
        def _(at):
            group_out[at, tile] = (
                wide(late[tile, at, shard]) + wide(near_in[tile, 1, at]) + wide(far_in[tile, at])
            ).astype(jnp.bfloat16)

        for chunk, (begin, count) in enumerate(chunks):
            if tile == begin + count - 1:
                for step in range(1, experts):
                    group_copy(chunk, step).start()

    def pair_copy(index, source, target):
        return pltpu.make_async_remote_copy(
            source,
            target,
            pair_send.at[index],
            pair_recv.at[index],
            device_id={"section": 1 - section},
            device_id_type=MESH,
        )

    width = grad_att.shape[1]
    spaced = grad_att.shape[0]
    scale = HEAD_DIM ** (-0.5)
    valid = lax.broadcasted_iota(jnp.int32, (spaced, spaced), 1) < SEQ

    def dot(one, other, dims):
        return lax.dot_general(one, other, ((dims[:1], dims[1:]), ((), ())), preferred_element_type=jnp.float32)

    parts = width // TILE
    each = experts // parts

    def make(tile):
        which, span = places[tile]

        def right(side):
            columns = slice(span, span + TILE)
            if which < 5:
                return rights[side][which][:, columns]
            return right_own[side * spaced : side * spaced + SEQ, columns]

        @pl.loop(0, parts)
        def _(at):
            rows = pl.ds(pl.multiple_of(at * TILE, TILE), TILE)
            product = dot(lefts[0][which][:, rows], right(0), (0, 0)) + dot(
                lefts[1][which][:, rows], right(1), (0, 0)
            )
            product = product.astype(jnp.bfloat16).reshape((each,) + late.shape[2:])
            for inner in range(each):
                late[tile, at * each + inner] = product[inner]

    def make_folded():
        shards = late.shape[2]
        step = TILE // (batch * late.shape[3])

        @pl.loop(0, experts * shards // step)
        def _(at):
            rows = pl.ds(pl.multiple_of(at * TILE, TILE), TILE)
            product = dot(lefts[0][1][:, rows], rights[0][1][...], (0, 0)) + dot(
                lefts[1][1][:, rows], rights[1][1][...], (0, 0)
            )
            product = product.astype(jnp.bfloat16).reshape((step, batch) + late.shape[3:])
            place = at * step
            for inner in range(step):
                for fold in range(batch):
                    late[batch + fold, place // shards, place % shards + inner] = product[
                        inner, fold
                    ]

    done = []

    def pump(amount):
        for _ in range(amount):
            step = len(done)
            done.append(step)
            if step == batch:
                make_folded()
            if step < tiles:
                if places[step][0] != 1:
                    make(step)
                start(step)
            if 0 <= step - 2 < tiles:
                turn(step - 2)
            if 0 <= step - 3 < tiles:
                finish(step - 3)

    pump(2)
    mixed[...] = jnp.zeros_like(mixed)
    grad_att[...] = jnp.zeros_like(grad_att)
    mixed[0:SEQ] = mixed_in[...]
    grad_att[0:SEQ] = grad_att_in[...]

    def head_pair(at):
        def columns(part):
            return pl.ds(pl.multiple_of(part * width + at * 2 * HEAD_DIM, 2 * HEAD_DIM), 2 * HEAD_DIM)

        queries, keys, values = [mixed[:, columns(part)] for part in range(3)]
        grads = grad_att[:, columns(0)]
        made = []
        for half in range(2):
            span = slice(half * HEAD_DIM, (half + 1) * HEAD_DIM)
            query, key, value, grad = queries[:, span], keys[:, span], values[:, span], grads[:, span]
            scores = dot(query, key, (1, 1)) * scale
            top = jnp.max(jnp.where(valid, scores, -jnp.inf), axis=1, keepdims=True)
            raised = jnp.where(valid, jnp.exp(scores - top), 0.0)
            full = raised / jnp.sum(raised, axis=1, keepdims=True)
            probs = full.astype(jnp.bfloat16)
            grad_probs = dot(grad, value, (1, 1))
            inner = jnp.sum(full * grad_probs, axis=1, keepdims=True)
            grad_scores = (full * (grad_probs - inner) * scale).astype(jnp.bfloat16)
            made.append(
                (
                    dot(grad_scores, key, (1, 0)),
                    dot(grad_scores, query, (0, 0)),
                    dot(probs, grad, (0, 0)),
                )
            )
        for part in range(3):
            grad_mixed[:, columns(part)] = jnp.concatenate(
                [made[0][part], made[1][part]], axis=1
            ).astype(jnp.bfloat16)

    pairs = HEADS // 2
    for third in range(3):
        pl.loop(third * pairs // 3, (third + 1) * pairs // 3)(head_pair)
        pump(2)

    cut = grad_mixed.shape[1] // 2
    kept = pl.ds(pl.multiple_of(section * cut, 128), cut)
    sent = pl.ds(pl.multiple_of((1 - section) * cut, 128), cut)
    mixed_copy = pair_copy(0, grad_mixed.at[:, sent], right_own.at[pl.ds(spaced, spaced)])
    mixed_copy.start()
    right_own[0:spaced] = grad_mixed[:, kept]

    rows_at = 256

    pump(1)

    @pl.loop(0, width // rows_at)
    def _(at):
        span = pl.ds(pl.multiple_of(at * rows_at, rows_at), rows_at)
        grad_normed[:, span] = dot(grad_mixed[...], weight[span, :], (1, 1))

    pump(1)
    mixed_copy.wait()
    pump(1)
    start_values = wide(block_in[...])
    centred = start_values - jnp.mean(start_values, axis=1, keepdims=True)
    root = lax.rsqrt(jnp.mean(centred * centred, axis=1, keepdims=True) + eps)
    unit = centred * root
    cotan = grad_normed[0:SEQ]
    norm_pair[0, 0:1, :] = jnp.sum(cotan * unit, axis=0, keepdims=True)
    norm_pair[0, 1:2, :] = jnp.sum(cotan, axis=0, keepdims=True)
    norm_copy_pair = pair_copy(1, norm_pair.at[0], norm_pair.at[1])
    norm_copy_pair.start()
    scaled = cotan * gain[0:1, :]
    grad_own[0:SEQ] = grad_hidden[...] + root * (
        scaled
        - jnp.mean(scaled, axis=1, keepdims=True)
        - unit * jnp.mean(scaled * unit, axis=1, keepdims=True)
    )
    grad_copy = pair_copy(2, grad_own, grad_other)
    grad_copy.start()
    norm_copy_pair.wait()
    chosen = jnp.where(section == 0, 1.0, 0.0)
    norm_own[...] = norm_in[...]
    norm_own[0:1, :] = norm_in[0:1, :] + chosen * (norm_pair[0, 0:1, :] + norm_pair[1, 0:1, :])
    norm_own[2:3, :] = norm_in[2:3, :] + chosen * (norm_pair[0, 1:2, :] + norm_pair[1, 1:2, :])
    for mask in (1, 2, 3):
        norm_copy(mask).start()

    pump(4)
    for mask in (1, 2, 3):
        norm_copy(mask).wait()
    norm_mid[...] = (norm_own[...] + norm_near[0]) + (norm_near[1] + norm_near[2])
    for other in range(1, experts):
        norm_group_copy(other).start()
    pump(tiles + 3 - len(done))

    grad_copy.wait()
    norm_total = norm_mid[...]
    for step in range(1, experts):
        norm_group_copy(step).wait()
        norm_total = norm_total + norm_far[step - 1]
    norm_out[...] = norm_total

    def total_of(tile):
        total = wide(group_out[group, tile])
        for step in range(1, experts):
            total = total + wide(group_in[step - 1, tile])
        return total

    size = dense_in_sum.shape[0]
    for chunk, (begin, length) in enumerate(chunks):
        for step in range(1, experts):
            group_copy(chunk, step).wait_recv()
        for tile in range(begin, begin + length):
            total = total_of(tile)
            which, at = tile // batch, tile % batch
            if which == 1:
                dense_out_sum[at * size : (at + 1) * size] = total
            elif which == 0:
                dense_in_sum[:, at * TILE : (at + 1) * TILE] = total
            else:
                swap_out[which - 2, at] = total

    swap = pltpu.make_async_remote_copy(
        swap_out.at[section],
        swap_in,
        swap_send,
        swap_recv,
        device_id={"section": 1 - section},
        device_id_type=MESH,
    )
    swap.start()

    def place(half, parts):
        cut = qkv_sum.shape[1] // 2
        for at in range(batch - 1):
            start_at = pl.multiple_of(half * cut + at * TILE, 128)
            qkv_sum[:, pl.ds(start_at, TILE)] = parts[at + 1]
        out_sum[:, pl.ds(pl.multiple_of(half * TILE, 128), TILE)] = parts[0]

    place(section, swap_out[1 - section])
    swap.wait()
    place(1 - section, swap_in[...])

    for tile in range(tiles):
        near_copy(tile, 0).wait_send()
        near_copy(tile, 1).wait_send()
        far_copy(tile).wait_send()
    for chunk in range(len(chunks)):
        for step in range(1, experts):
            group_copy(chunk, step).wait_send()


def tail_sums(experts, shards, sides, left, mixed, grad_att, weight, block_in, gain, grad_hidden, norms):
    width = grad_att.shape[1]
    size = width // (experts * shards)
    places = [(0, at * TILE) for at in range(4)] + [(1, 0)] * 4
    places += [(3, 0)] + [(2, at * TILE) for at in range(3)]
    places += [(4, 0)] + [(5, at * TILE) for at in range(3)]
    tiles = len(places)
    lefts = [side[0] for side in sides] + [left]
    rights = [side[1] for side in sides]
    inputs = [array[side] for arrays in (lefts, rights) for side in (0, 1) for array in arrays]
    assert [array[0].shape[1] // TILE for array in rights] == [4, 1, 3, 1, 1]
    spaced = -(-mixed.shape[0] // 256) * 256
    folds = 4
    full = (tiles, experts, size, TILE)
    dma = pltpu.SemaphoreType.DMA
    half = jnp.bfloat16
    return pl.pallas_call(
        functools.partial(tail_kernel, experts, places),
        out_shape=(
            jax.ShapeDtypeStruct((folds * size, TILE), jnp.float32),
            jax.ShapeDtypeStruct((size, 4 * TILE), jnp.float32),
            jax.ShapeDtypeStruct((size, 6 * TILE), jnp.float32),
            jax.ShapeDtypeStruct((size, 2 * TILE), jnp.float32),
            jax.ShapeDtypeStruct(norms.shape, jnp.float32),
            jax.ShapeDtypeStruct(block_in.shape, jnp.float32),
            jax.ShapeDtypeStruct(block_in.shape, jnp.float32),
        ),
        in_specs=[pl.BlockSpec(memory_space=pltpu.VMEM)] * (len(inputs) + 7),
        out_specs=(pl.BlockSpec(memory_space=pltpu.VMEM),) * 7,
        scratch_shapes=[
            pltpu.VMEM((tiles, 2) + full[1:], half),
            pltpu.VMEM(full, half),
            pltpu.VMEM(full, half),
            pltpu.VMEM((experts, tiles, size, TILE), half),
            pltpu.VMEM((experts - 1, tiles, size, TILE), half),
            pltpu.VMEM((shards - 1,) + norms.shape, jnp.float32),
            pltpu.VMEM(norms.shape, jnp.float32),
            pltpu.VMEM((experts - 1,) + norms.shape, jnp.float32),
            dma((2 * tiles,)),
            dma((2 * tiles,)),
            dma((tiles,)),
            dma((tiles,)),
            dma((len(group_chunks(tiles)) * (experts - 1),)),
            dma((len(group_chunks(tiles)) * (experts - 1),)),
            dma((shards - 1,)),
            dma((shards - 1,)),
            dma((experts - 1,)),
            dma((experts - 1,)),
            pltpu.VMEM((2, 4, size, TILE), jnp.float32),
            pltpu.VMEM((4, size, TILE), jnp.float32),
            dma,
            dma,
            pltpu.VMEM((2 * spaced, mixed.shape[1] // 2), half),
            pltpu.VMEM((spaced, mixed.shape[1]), half),
            pltpu.VMEM((tiles, experts, shards, size, TILE), half),
            pltpu.VMEM(norms.shape, jnp.float32),
            pltpu.VMEM((2,) + norms.shape, jnp.float32),
            dma((3,)),
            dma((3,)),
            pltpu.VMEM((spaced, mixed.shape[1]), half),
            pltpu.VMEM((spaced, width), half),
            pltpu.VMEM((spaced, width), jnp.float32),
        ],
        compiler_params=pltpu.CompilerParams(
            collective_id=0, has_side_effects=True, vmem_limit_bytes=58 * 2**20
        ),
        cost_estimate=pl.CostEstimate(
            flops=10**7, bytes_accessed=10**7, transcendentals=0
        ),
    )(*inputs, mixed, grad_att, weight, block_in, gain, grad_hidden, norms)


def on_device(
    tokens,
    cotangent,
    norm_gains,
    norm_biases,
    qkv_weight,
    out_weight,
    dense_in,
    dense_out,
    expert_in,
    expert_out,
    routes,
    gates,
):
    rows = SEQ
    width = tokens.shape[1]
    experts = lax.axis_size("experts")
    shards = lax.axis_size("dp")
    capacity = 2 * rows // experts
    padded = -(-capacity // 8) * 8
    slots = experts * padded
    section = lax.axis_index("section")
    group = lax.axis_index("experts")
    shard = lax.axis_index("dp")
    first = section == 0

    def ordered(mine, other, axis):
        return jnp.concatenate(
            [jnp.where(first, mine, other), jnp.where(first, other, mine)], axis=axis
        )

    def kept_half(array, axis):
        low, high = jnp.split(array, 2, axis=axis)
        return jnp.where(first, low, high)

    def sent_half(array, axis):
        low, high = jnp.split(array, 2, axis=axis)
        return jnp.where(first, high, low)

    def both(own):
        other = pair(own)
        return (jnp.where(first, own, other), jnp.where(first, other, own))

    def across(array, mask):
        return lax.ppermute(array, "dp", [(i, i ^ mask) for i in range(shards)])

    def shifted(array, step):
        return lax.ppermute(
            array, "experts", [(i, (i + step) % experts) for i in range(experts)]
        )

    def wide(array):
        return array.astype(jnp.float32)

    def shard_sum(block, near, far):
        passed = across(block(3).astype(jnp.bfloat16), near)
        direct = across(block(near).astype(jnp.bfloat16), near)
        turned = across((block(far) + wide(passed)).astype(jnp.bfloat16), far)
        return block(0) + wide(direct) + wide(turned)

    def group_sum(array):
        own = lax.dynamic_index_in_dim(array, group, 0, False)
        total = wide(own)
        for step in range(1, experts):
            target = lax.rem(group + step, experts)
            total = total + wide(
                shifted(lax.dynamic_index_in_dim(array, target, 0, False), step)
            )
        return total

    def everyone_sum(left, right, near, far):
        blocks = left.reshape(experts, shards, -1, left.shape[1])

        def block(mask):
            part = lax.dynamic_index_in_dim(blocks, shard ^ mask, 1, False)
            return matmul(part.reshape(-1, left.shape[1]), right)

        total = shard_sum(block, near, far).astype(jnp.bfloat16)
        return group_sum(total.reshape(experts, -1, right.shape[1]))

    def padded_rows(array):
        return jnp.pad(array, ((0, -array.shape[0] % 256), (0, 0)))

    def joined(own, other):
        return jnp.concatenate([padded_rows(own), padded_rows(other)], axis=0)

    kernel_fits = experts == 4 and shards == 4

    def partial_grad(both_sides):
        left, right = both_sides
        if kernel_fits:
            return ((left, pair(left)), (kept_half(right, 1), pair(sent_half(right, 1))))
        left = joined(left, pair(left))
        right = joined(kept_half(right, 1), pair(sent_half(right, 1)))
        return (left.T, right)

    qkv_zero, qkv_one = both(qkv_weight[0])
    norms_zero, norms_one = both(jnp.concatenate([norm_gains[0], norm_biases[0]], axis=0))
    out_zero, out_one = both(out_weight[0])

    def own_block(array):
        return lax.dynamic_slice_in_dim(array, section * rows, rows, 0)

    block_in = own_block(tokens)
    grad_top = own_block(cotangent).astype(jnp.float32)
    chosen = own_block(routes)
    gate_pair = own_block(gates)

    flat = jnp.concatenate([chosen[:, 0], chosen[:, 1]])
    order = jnp.arange(2 * rows, dtype=jnp.int32)
    place = jnp.sum(
        ((flat[:, None] == flat[None, :]) & (order[None, :] < order[:, None])).astype(jnp.int32),
        axis=1,
        dtype=jnp.int32,
    )
    step_of = lax.rem(flat - group + experts, experts)
    slot = jnp.where(place < capacity, step_of * padded + place, slots)
    gate_flat = jnp.concatenate([gate_pair[:, 0], gate_pair[:, 1]])
    spread = (jnp.arange(slots, dtype=jnp.int32)[:, None] == slot[None, :]).astype(jnp.bfloat16)
    spread_both = spread[:, :rows] + spread[:, rows:]

    def sent_out(array):
        parts = [array[k * padded : (k + 1) * padded] for k in range(experts)]
        return jnp.concatenate([parts[0]] + [shifted(parts[k], k) for k in range(1, experts)])

    def sent_home(array):
        parts = [array[k * padded : (k + 1) * padded] for k in range(experts)]
        return jnp.concatenate(
            [parts[0]] + [shifted(parts[k], experts - k) for k in range(1, experts)]
        )

    doubled = (jnp.concatenate([grad_top, grad_top]) * gate_flat[:, None]).astype(jnp.bfloat16)
    grad_outgoing = matmul(spread, doubled).astype(jnp.bfloat16)

    piece_in = kept_half(expert_in[0], 1)
    piece_back = kept_half(expert_out[0], 0)
    near = lax.all_gather(jnp.concatenate([piece_in.T, piece_back], axis=0), "dp", axis=0)

    normed0, mixed0, logsum0, attended0, hidden0, second0 = front_half(
        block_in, norms_zero[:2], norms_zero[2:], qkv_zero, out_zero
    )
    grad_outgoing, second0 = lax.optimization_barrier((grad_outgoing, second0))
    grad_pieces = [grad_outgoing[k * padded : (k + 1) * padded] for k in range(experts)]
    grad_pieces = grad_pieces[:1] + [shifted(grad_pieces[k], k) for k in range(1, experts)]
    before0 = matmul(second0, dense_in)
    active0 = jax.nn.gelu(before0).astype(jnp.bfloat16)
    middle = rounded(hidden0 + matmul(active0, dense_out))
    middle, grad_pieces[1] = lax.optimization_barrier((middle, grad_pieces[1]))

    normed1, mixed1, logsum1, attended1, hidden1, second1 = front_half(
        middle, norms_one[:2], norms_one[2:], qkv_one, out_one
    )
    second1, grad_pieces = lax.optimization_barrier((second1, grad_pieces))
    grad_rows = jnp.concatenate(grad_pieces)
    rows_in = sent_out(matmul(spread_both, second1).astype(jnp.bfloat16))

    near, rows_in = lax.optimization_barrier((near, rows_in))
    gathered = (near, pair(near))
    hidden_share = piece_back.shape[0]
    weights_in = [both[:, :hidden_share].reshape(-1, width) for both in gathered]
    weights_back = [both[:, hidden_share:].reshape(-1, width) for both in gathered]
    before1 = [matmul_cols(rows_in, weight) for weight in weights_in]
    active1 = [jax.nn.gelu(before).astype(jnp.bfloat16) for before in before1]
    grad_before1 = [
        gelu_back(before, matmul_cols(grad_rows, weight)).astype(jnp.bfloat16)
        for before, weight in zip(before1, weights_back)
    ]
    grad_arrived = (
        matmul(grad_before1[0], weights_in[0]) + matmul(grad_before1[1], weights_in[1])
    ).astype(jnp.bfloat16)
    grad_home = sent_home(grad_arrived)
    returned = (
        matmul(active1[0], weights_back[0]) + matmul(active1[1], weights_back[1])
    ).astype(jnp.bfloat16)
    returned_home = sent_home(returned)

    def expert_parts(halves, right):
        landed = [pair(half) for half in halves]
        lefts = [
            jnp.concatenate([halves[0], landed[1]], axis=0),
            jnp.concatenate([halves[1], landed[0]], axis=0),
        ]
        right = jnp.concatenate([kept_half(right, 1), pair(sent_half(right, 1))], axis=0)
        return [
            with_layout_constraint(
                matmul_rows(left, right).astype(jnp.bfloat16), Layout(major_to_minor=(0, 1))
            )
            for left in lefts
        ]

    expert_in_parts = expert_parts(grad_before1, rows_in)
    expert_out_parts = expert_parts(active1, grad_rows)
    expert_stack = jnp.concatenate(expert_in_parts + expert_out_parts, axis=1)
    grad_home, expert_stack = lax.optimization_barrier((grad_home, expert_stack))
    expert_shard = lax.psum_scatter(expert_stack, "dp", scatter_dimension=0, tiled=True)
    parts = jnp.split(expert_shard, 4, axis=1)
    expert_in_sum = ordered(parts[0], parts[1], 0).astype(jnp.float32)
    expert_out_sum = ordered(parts[2], parts[3], 0).astype(jnp.float32)

    picked = matmul_rows(spread, returned_home) * gate_flat[:, None]
    final = (hidden1 + (picked[:rows] + picked[rows:])).astype(jnp.bfloat16)
    grad_second1 = matmul_rows(spread_both, grad_home)
    grad_middle, grad_norm1, grad_mixed1, grad_cast1 = front_back(
        middle,
        (normed1, mixed1, logsum1, attended1, hidden1),
        grad_top,
        grad_second1,
        norms_one[:2],
        norms_one[2:],
        qkv_one,
        out_one,
    )

    grad_result = rounded(grad_middle)
    grad_before0 = gelu_back(before0, matmul_cols(grad_result, dense_out)).astype(jnp.bfloat16)
    dense_out_part = partial_grad((active0, grad_result))
    dense_in_part = partial_grad((second0, grad_before0))
    qkv_part1 = partial_grad((normed1, grad_mixed1))
    out_part1 = partial_grad((attended1, grad_cast1))
    grad_second0 = matmul_cols(grad_before0, dense_in)
    saved0 = (normed0, mixed0, logsum0, attended0, hidden0)
    if not kernel_fits:
        grad_tokens, grad_norm0, grad_mixed0, grad_cast0 = front_back(
            block_in,
            saved0,
            grad_result.astype(jnp.float32),
            grad_second0,
            norms_zero[:2],
            norms_zero[2:],
            qkv_zero,
            out_zero,
        )
        qkv_part0 = partial_grad((normed0, grad_mixed0))
    else:
        grad_mid0, gain_two0, bias_two0 = norm_back(
            hidden0, norms_zero[1], norms_zero[3], grad_second0
        )
        grad_hidden0 = grad_result.astype(jnp.float32) + grad_mid0
        grad_cast0 = grad_hidden0.astype(jnp.bfloat16)
        grad_att0 = matmul_cols(grad_cast0, out_zero).astype(jnp.bfloat16)
        nothing = jnp.zeros_like(gain_two0)
        grad_norm0 = jnp.stack([nothing, gain_two0, nothing, bias_two0])
    out_part0 = partial_grad((attended0, grad_cast0))
    norm_pair = jnp.where(first, grad_norm0, grad_norm1) + pair(
        jnp.where(first, grad_norm1, grad_norm0)
    )
    rest = [dense_in_part, qkv_part1, out_part1]
    if kernel_fits:
        eight = jnp.zeros((8, width), jnp.float32)
        dense_out_sum, dense_in_sum, qkv_sum, out_sum, norm_sum, grad_tokens, grad_landed = tail_sums(
            experts,
            shards,
            [dense_in_part, dense_out_part, qkv_part1, out_part1, out_part0],
            (normed0, pair(normed0)),
            mixed0,
            grad_att0,
            qkv_zero,
            block_in,
            eight.at[0].set(norms_zero[0]),
            grad_hidden0,
            eight.at[:4].set(norm_pair),
        )
        size = width // (experts * shards)
        norm_sum = lax.dynamic_slice(norm_sum[:4], (0, (group * shards + shard) * size), (4, size))
        middle_landed = pair(grad_middle)
        act_grads = jnp.concatenate(
            [
                jnp.where(first, grad_tokens, middle_landed),
                jnp.where(first, grad_landed, grad_middle),
            ]
        )
    else:
        dense_out_sum = everyone_sum(*dense_out_part, 1, 2)
        dense_in_sum, qkv_one, out_one, qkv_zero, out_zero = [
            everyone_sum(*part, 2, 1).astype(jnp.bfloat16)
            for part in rest + [qkv_part0, out_part0]
        ]
        own_shared, other_shared = [
            jnp.where(first, *halves)
            for halves in (
                (
                    jnp.concatenate([qkv_zero, out_zero], axis=1),
                    jnp.concatenate([qkv_one, out_one], axis=1),
                ),
                (
                    jnp.concatenate([qkv_one, out_one], axis=1),
                    jnp.concatenate([qkv_zero, out_zero], axis=1),
                ),
            )
        ]
        other_shared = pair(other_shared)
        cut = qkv_zero.shape[1]
        qkv_sum = ordered(own_shared[:, :cut], other_shared[:, :cut], 1).astype(jnp.float32)
        out_sum = ordered(own_shared[:, cut:], other_shared[:, cut:], 1).astype(jnp.float32)
        dense_in_sum = dense_in_sum.astype(jnp.float32)
        norm_sum = lax.psum_scatter(
            norm_pair.T, ("experts", "dp"), scatter_dimension=0, tiled=True
        ).T
        act_grads = ordered(
            jnp.where(first, grad_tokens, grad_middle),
            pair(jnp.where(first, grad_middle, grad_tokens)),
            0,
        )

    acts = ordered(
        jnp.where(first, middle, final), pair(jnp.where(first, final, middle)), 0
    )
    return (
        acts[None],
        act_grads[None],
        qkv_sum[None],
        out_sum[None],
        norm_sum[:2][None],
        norm_sum[2:][None],
        dense_in_sum,
        dense_out_sum,
        expert_in_sum.T[None],
        expert_out_sum[None],
    )


def solution(mesh):
    placed = (
        P(("experts", "dp"), None),
        P(("experts", "dp"), None),
        P("section", None, None),
        P("section", None, None),
        P("section", None, None),
        P("section", None, None),
        P(),
        P(),
        P("experts", None, "dp"),
        P("experts", "dp", None),
        P(("experts", "dp"), None),
        P(("experts", "dp"), None),
    )
    return jax.shard_map(
        on_device,
        mesh=mesh,
        in_specs=placed,
        out_specs=(
            P("section", ("experts", "dp"), None),
            P("section", ("experts", "dp"), None),
            P("section", ("experts", "dp"), None),
            P("section", ("experts", "dp"), None),
            P("section", None, ("experts", "dp")),
            P("section", None, ("experts", "dp")),
            P(("experts", "dp"), "section"),
            P(("experts", "dp"), "section"),
            P("experts", "section", "dp"),
            P("experts", "dp", "section"),
        ),
        check_vma=False,
    )
```

```python
import functools

import jax
import jax.numpy as jnp
from jax import lax
from jax.experimental import pallas as pl
from jax.experimental.layout import Layout, with_layout_constraint
from jax.experimental.pallas import tpu as pltpu
from jax.sharding import PartitionSpec as P

HEADS = 12
HEAD_DIM = 64
SEQ = 197


eps = 1e-06


def pair(block):
    return lax.ppermute(block, "section", [(0, 1), (1, 0)])


def layer_norm(values, gain, bias):
    centred = values - jnp.mean(values, axis=-1, keepdims=True)
    spread = jnp.mean(centred * centred, axis=-1, keepdims=True)
    return centred * lax.rsqrt(spread + eps) * gain + bias


def norm_back(values, gain, bias, cotan):
    _, pull = jax.vjp(layer_norm, values, gain, bias)
    return pull(cotan)


def gelu_back(before, cotan):
    _, pull = jax.vjp(jax.nn.gelu, before)
    return pull(cotan)[0]


def matmul(left, right):
    return jnp.dot(left, right, preferred_element_type=jnp.float32)


def matmul_rows(left, right):
    return lax.dot_general(
        left, right, (((0,), (0,)), ((), ())), preferred_element_type=jnp.float32
    )


def matmul_cols(left, right):
    return lax.dot_general(
        left, right, (((1,), (1,)), ((), ())), preferred_element_type=jnp.float32
    )


def head_split(mixed):
    return mixed.reshape(-1, SEQ, 3, HEADS, HEAD_DIM)


def score_table(split):
    return jnp.einsum(
        "bqhd,bkhd->bhqk", split[:, :, 0], split[:, :, 1], preferred_element_type=jnp.float32
    ) * HEAD_DIM ** (-0.5)


def attend(normed, weight_qkv):
    mixed = matmul(normed, weight_qkv).astype(jnp.bfloat16)
    split = head_split(mixed)
    scores = score_table(split)
    top = jnp.max(scores, axis=-1, keepdims=True)
    logsum = top + jnp.log(jnp.sum(jnp.exp(scores - top), axis=-1, keepdims=True))
    probs = jnp.exp(scores - logsum).astype(jnp.bfloat16)
    attended = jnp.einsum(
        "bhqk,bkhd->bqhd", probs, split[:, :, 2], preferred_element_type=jnp.float32
    )
    return (mixed, logsum, attended.reshape(normed.shape[0], -1).astype(jnp.bfloat16))


def attend_back(normed, mixed, logsum, attended, grad_hidden, weight_qkv, weight_out):
    grad_cast = grad_hidden.astype(jnp.bfloat16)
    grad_att = matmul_cols(grad_cast, weight_out).astype(jnp.bfloat16)
    split = head_split(mixed)
    probs_full = jnp.exp(score_table(split) - logsum)
    probs = probs_full.astype(jnp.bfloat16)
    grad_heads = grad_att.reshape(-1, SEQ, HEADS, HEAD_DIM)
    grad_probs = jnp.einsum(
        "bqhd,bkhd->bhqk", grad_heads, split[:, :, 2], preferred_element_type=jnp.float32
    )
    grad_value = jnp.einsum(
        "bhqk,bqhd->bkhd", probs, grad_heads, preferred_element_type=jnp.float32
    )
    inner = jnp.sum(probs_full * grad_probs, axis=-1, keepdims=True)
    grad_scores = (probs_full * (grad_probs - inner) * HEAD_DIM ** (-0.5)).astype(jnp.bfloat16)
    grad_query = jnp.einsum(
        "bhqk,bkhd->bqhd", grad_scores, split[:, :, 1], preferred_element_type=jnp.float32
    )
    grad_key = jnp.einsum(
        "bhqk,bqhd->bkhd", grad_scores, split[:, :, 0], preferred_element_type=jnp.float32
    )
    grad_mixed = (
        jnp.stack([grad_query, grad_key, grad_value], axis=2)
        .reshape(normed.shape[0], -1)
        .astype(jnp.bfloat16)
    )
    return (matmul_cols(grad_mixed, weight_qkv), grad_mixed, grad_cast)


def front_half(block_in, gains, biases, weight_qkv, weight_out):
    start = block_in.astype(jnp.float32)
    normed = layer_norm(start, gains[0], biases[0]).astype(jnp.bfloat16)
    mixed, logsum, attended = attend(normed, weight_qkv)
    hidden = start + matmul(attended, weight_out)
    second = layer_norm(hidden, gains[1], biases[1]).astype(jnp.bfloat16)
    return (normed, mixed, logsum, attended, hidden, second)


def front_back(block_in, saved, grad_top, grad_second, gains, biases, weight_qkv, weight_out):
    normed, mixed, logsum, attended, hidden = saved
    grad_mid, gain_two, bias_two = norm_back(hidden, gains[1], biases[1], grad_second)
    grad_hidden = grad_top + grad_mid
    grad_normed, grad_mixed, grad_cast = attend_back(
        normed, mixed, logsum, attended, grad_hidden, weight_qkv, weight_out
    )
    grad_start, gain_one, bias_one = norm_back(
        block_in.astype(jnp.float32), gains[0], biases[0], grad_normed
    )
    return (
        grad_start + grad_hidden,
        jnp.stack([gain_one, gain_two, bias_one, bias_two]),
        grad_mixed,
        grad_cast,
    )


def rounded(values):
    return lax.reduce_precision(values, exponent_bits=8, mantissa_bits=7).astype(jnp.bfloat16)


TILE = 384
MESH = pl.DeviceIdType.MESH


def group_chunks(tiles):
    return [(at, 1) for at in range(tiles)]


def tail_kernel(
    experts,
    places,
    *refs,
):
    lefts, rights = [refs[0:6], refs[6:12]], [refs[12:17], refs[17:22]]
    count = 22
    mixed_in, grad_att_in, weight, block_in, gain, grad_hidden, norm_in = refs[count : count + 7]
    dense_out_sum, dense_in_sum, qkv_sum, out_sum, norm_out, grad_own, grad_other = refs[
        count + 7 : count + 14
    ]
    (
        near_in,
        far_out,
        far_in,
        group_out,
        group_in,
        norm_near,
        norm_mid,
        norm_far,
        near_send,
        near_recv,
        far_send,
        far_recv,
        group_send,
        group_recv,
        norm_send,
        norm_recv,
        norm_group_send,
        norm_group_recv,
        swap_out,
        swap_in,
        swap_send,
        swap_recv,
        right_own,
        grad_mixed,
        late,
        norm_own,
        norm_pair,
        pair_send,
        pair_recv,
        mixed,
        grad_att,
        grad_normed,
    ) = refs[count + 14 :]
    shard = lax.axis_index("dp")
    group = lax.axis_index("experts")
    section = lax.axis_index("section")
    low = shard % 2
    high = shard // 2
    peers = {0: shard, 1: shard + 1 - 2 * low, 2: shard + 2 - 4 * high, 3: 3 - shard}
    groups = [(group + step) % experts for step in range(experts)]
    tiles = len(places)
    batch = 4
    chunks = group_chunks(tiles)

    barrier = pltpu.get_barrier_semaphore()
    for mask in (1, 2, 3):
        pl.semaphore_signal(barrier, 1, device_id={"dp": peers[mask]}, device_id_type=MESH)
    for step in range(1, experts):
        pl.semaphore_signal(barrier, 1, device_id={"experts": groups[step]}, device_id_type=MESH)

    pl.semaphore_signal(barrier, 1, device_id={"section": 1 - section}, device_id_type=MESH)

    def block(tile, mask):
        return late.at[tile, :, peers[mask], :, :]

    def order(tile):
        return (1, 2) if tile % 2 == 0 else (2, 1)

    def near_copy(tile, part):
        near = order(tile)[0]
        return pltpu.make_async_remote_copy(
            block(tile, (3, near)[part]),
            near_in.at[tile, part],
            near_send.at[2 * tile + part],
            near_recv.at[2 * tile + part],
            device_id={"dp": peers[near]},
            device_id_type=MESH,
        )

    def far_copy(tile):
        return pltpu.make_async_remote_copy(
            far_out.at[tile],
            far_in.at[tile],
            far_send.at[tile],
            far_recv.at[tile],
            device_id={"dp": peers[order(tile)[1]]},
            device_id_type=MESH,
        )

    def group_copy(chunk, step):
        span = pl.ds(*chunks[chunk])
        return pltpu.make_async_remote_copy(
            group_out.at[groups[step], span],
            group_in.at[step - 1, span],
            group_send.at[chunk * (experts - 1) + step - 1],
            group_recv.at[chunk * (experts - 1) + step - 1],
            device_id={"experts": groups[step]},
            device_id_type=MESH,
        )

    def norm_copy(mask):
        return pltpu.make_async_remote_copy(
            norm_own,
            norm_near.at[mask - 1],
            norm_send.at[mask - 1],
            norm_recv.at[mask - 1],
            device_id={"dp": peers[mask]},
            device_id_type=MESH,
        )

    def norm_group_copy(step):
        return pltpu.make_async_remote_copy(
            norm_mid,
            norm_far.at[step - 1],
            norm_group_send.at[step - 1],
            norm_group_recv.at[step - 1],
            device_id={"experts": groups[step]},
            device_id_type=MESH,
        )

    def wide(value):
        return value.astype(jnp.float32)

    pl.semaphore_wait(barrier, 4 + experts - 1)

    def start(tile):
        near_copy(tile, 0).start()
        near_copy(tile, 1).start()

    def turn(tile):
        near_copy(tile, 0).wait_recv()
        far = peers[order(tile)[1]]

        @pl.loop(0, experts)
        def _(at):
            far_out[tile, at] = (wide(late[tile, at, far]) + wide(near_in[tile, 0, at])).astype(
                jnp.bfloat16
            )

        far_copy(tile).start()

    def finish(tile):
        near_copy(tile, 1).wait_recv()
        far_copy(tile).wait_recv()

        @pl.loop(0, experts)
        def _(at):
            group_out[at, tile] = (
                wide(late[tile, at, shard]) + wide(near_in[tile, 1, at]) + wide(far_in[tile, at])
            ).astype(jnp.bfloat16)

        for chunk, (begin, count) in enumerate(chunks):
            if tile == begin + count - 1:
                for step in range(1, experts):
                    group_copy(chunk, step).start()

    def pair_copy(index, source, target):
        return pltpu.make_async_remote_copy(
            source,
            target,
            pair_send.at[index],
            pair_recv.at[index],
            device_id={"section": 1 - section},
            device_id_type=MESH,
        )

    width = grad_att.shape[1]
    spaced = grad_att.shape[0]
    scale = HEAD_DIM ** (-0.5)
    valid = lax.broadcasted_iota(jnp.int32, (spaced, spaced), 1) < SEQ

    def dot(one, other, dims):
        return lax.dot_general(one, other, ((dims[:1], dims[1:]), ((), ())), preferred_element_type=jnp.float32)

    parts = width // TILE
    each = experts // parts

    def make(tile):
        which, span = places[tile]

        def right(side):
            columns = slice(span, span + TILE)
            if which < 5:
                return rights[side][which][:, columns]
            return right_own[side * spaced : side * spaced + SEQ, columns]

        @pl.loop(0, parts)
        def _(at):
            rows = pl.ds(pl.multiple_of(at * TILE, TILE), TILE)
            product = dot(lefts[0][which][:, rows], right(0), (0, 0)) + dot(
                lefts[1][which][:, rows], right(1), (0, 0)
            )
            product = product.astype(jnp.bfloat16).reshape((each,) + late.shape[2:])
            for inner in range(each):
                late[tile, at * each + inner] = product[inner]

    def make_folded():
        shards = late.shape[2]
        step = TILE // (batch * late.shape[3])

        @pl.loop(0, experts * shards // step)
        def _(at):
            rows = pl.ds(pl.multiple_of(at * TILE, TILE), TILE)
            product = dot(lefts[0][1][:, rows], rights[0][1][...], (0, 0)) + dot(
                lefts[1][1][:, rows], rights[1][1][...], (0, 0)
            )
            product = product.astype(jnp.bfloat16).reshape((step, batch) + late.shape[3:])
            place = at * step
            for inner in range(step):
                for fold in range(batch):
                    late[batch + fold, place // shards, place % shards + inner] = product[
                        inner, fold
                    ]

    done = []

    def pump(amount):
        for _ in range(amount):
            step = len(done)
            done.append(step)
            if step == batch:
                make_folded()
            if step < tiles:
                if places[step][0] != 1:
                    make(step)
                start(step)
            if 0 <= step - 2 < tiles:
                turn(step - 2)
            if 0 <= step - 3 < tiles:
                finish(step - 3)

    pump(2)
    mixed[...] = jnp.zeros_like(mixed)
    grad_att[...] = jnp.zeros_like(grad_att)
    mixed[0:SEQ] = mixed_in[...]
    grad_att[0:SEQ] = grad_att_in[...]

    def head_pair(at):
        def columns(part):
            return pl.ds(pl.multiple_of(part * width + at * 2 * HEAD_DIM, 2 * HEAD_DIM), 2 * HEAD_DIM)

        queries, keys, values = [mixed[:, columns(part)] for part in range(3)]
        grads = grad_att[:, columns(0)]
        made = []
        for half in range(2):
            span = slice(half * HEAD_DIM, (half + 1) * HEAD_DIM)
            query, key, value, grad = queries[:, span], keys[:, span], values[:, span], grads[:, span]
            scores = dot(query, key, (1, 1)) * scale
            top = jnp.max(jnp.where(valid, scores, -jnp.inf), axis=1, keepdims=True)
            raised = jnp.where(valid, jnp.exp(scores - top), 0.0)
            full = raised / jnp.sum(raised, axis=1, keepdims=True)
            probs = full.astype(jnp.bfloat16)
            grad_probs = dot(grad, value, (1, 1))
            inner = jnp.sum(full * grad_probs, axis=1, keepdims=True)
            grad_scores = (full * (grad_probs - inner) * scale).astype(jnp.bfloat16)
            made.append(
                (
                    dot(grad_scores, key, (1, 0)),
                    dot(grad_scores, query, (0, 0)),
                    dot(probs, grad, (0, 0)),
                )
            )
        for part in range(3):
            grad_mixed[:, columns(part)] = jnp.concatenate(
                [made[0][part], made[1][part]], axis=1
            ).astype(jnp.bfloat16)

    pairs = HEADS // 2
    for turn_at in range(pairs):
        pl.loop(turn_at, turn_at + 1)(head_pair)
        pump(1)

    cut = grad_mixed.shape[1] // 2
    kept = pl.ds(pl.multiple_of(section * cut, 128), cut)
    sent = pl.ds(pl.multiple_of((1 - section) * cut, 128), cut)
    mixed_copy = pair_copy(0, grad_mixed.at[:, sent], right_own.at[pl.ds(spaced, spaced)])
    mixed_copy.start()
    right_own[0:spaced] = grad_mixed[:, kept]

    rows_at = 256

    pump(1)

    @pl.loop(0, width // rows_at)
    def _(at):
        span = pl.ds(pl.multiple_of(at * rows_at, rows_at), rows_at)
        grad_normed[:, span] = dot(grad_mixed[...], weight[span, :], (1, 1))

    pump(1)
    mixed_copy.wait()
    pump(1)
    start_values = wide(block_in[...])
    centred = start_values - jnp.mean(start_values, axis=1, keepdims=True)
    root = lax.rsqrt(jnp.mean(centred * centred, axis=1, keepdims=True) + eps)
    unit = centred * root
    cotan = grad_normed[0:SEQ]
    norm_pair[0, 0:1, :] = jnp.sum(cotan * unit, axis=0, keepdims=True)
    norm_pair[0, 1:2, :] = jnp.sum(cotan, axis=0, keepdims=True)
    norm_copy_pair = pair_copy(1, norm_pair.at[0], norm_pair.at[1])
    norm_copy_pair.start()
    scaled = cotan * gain[0:1, :]
    grad_own[0:SEQ] = grad_hidden[...] + root * (
        scaled
        - jnp.mean(scaled, axis=1, keepdims=True)
        - unit * jnp.mean(scaled * unit, axis=1, keepdims=True)
    )
    grad_copy = pair_copy(2, grad_own, grad_other)
    grad_copy.start()
    norm_copy_pair.wait()
    chosen = jnp.where(section == 0, 1.0, 0.0)
    norm_own[...] = norm_in[...]
    norm_own[0:1, :] = norm_in[0:1, :] + chosen * (norm_pair[0, 0:1, :] + norm_pair[1, 0:1, :])
    norm_own[2:3, :] = norm_in[2:3, :] + chosen * (norm_pair[0, 1:2, :] + norm_pair[1, 1:2, :])
    for mask in (1, 2, 3):
        norm_copy(mask).start()

    pump(4)
    for mask in (1, 2, 3):
        norm_copy(mask).wait()
    norm_mid[...] = (norm_own[...] + norm_near[0]) + (norm_near[1] + norm_near[2])
    for other in range(1, experts):
        norm_group_copy(other).start()
    pump(tiles + 3 - len(done))

    grad_copy.wait()
    norm_total = norm_mid[...]
    for step in range(1, experts):
        norm_group_copy(step).wait()
        norm_total = norm_total + norm_far[step - 1]
    norm_out[...] = norm_total

    def total_of(tile):
        total = wide(group_out[group, tile])
        for step in range(1, experts):
            total = total + wide(group_in[step - 1, tile])
        return total

    size = dense_in_sum.shape[0]
    for chunk, (begin, length) in enumerate(chunks):
        for step in range(1, experts):
            group_copy(chunk, step).wait_recv()
        for tile in range(begin, begin + length):
            total = total_of(tile)
            which, at = tile // batch, tile % batch
            if which == 1:
                dense_out_sum[at * size : (at + 1) * size] = total
            elif which == 0:
                dense_in_sum[:, at * TILE : (at + 1) * TILE] = total
            else:
                swap_out[which - 2, at] = total

    swap = pltpu.make_async_remote_copy(
        swap_out.at[section],
        swap_in,
        swap_send,
        swap_recv,
        device_id={"section": 1 - section},
        device_id_type=MESH,
    )
    swap.start()

    def place(half, parts):
        cut = qkv_sum.shape[1] // 2
        for at in range(batch - 1):
            start_at = pl.multiple_of(half * cut + at * TILE, 128)
            qkv_sum[:, pl.ds(start_at, TILE)] = parts[at + 1]
        out_sum[:, pl.ds(pl.multiple_of(half * TILE, 128), TILE)] = parts[0]

    place(section, swap_out[1 - section])
    swap.wait()
    place(1 - section, swap_in[...])

    for tile in range(tiles):
        near_copy(tile, 0).wait_send()
        near_copy(tile, 1).wait_send()
        far_copy(tile).wait_send()
    for chunk in range(len(chunks)):
        for step in range(1, experts):
            group_copy(chunk, step).wait_send()


def tail_sums(experts, shards, sides, left, mixed, grad_att, weight, block_in, gain, grad_hidden, norms):
    width = grad_att.shape[1]
    size = width // (experts * shards)
    places = [(0, at * TILE) for at in range(4)] + [(1, 0)] * 4
    places += [(3, 0)] + [(2, at * TILE) for at in range(3)]
    places += [(4, 0)] + [(5, at * TILE) for at in range(3)]
    tiles = len(places)
    lefts = [side[0] for side in sides] + [left]
    rights = [side[1] for side in sides]
    inputs = [array[side] for arrays in (lefts, rights) for side in (0, 1) for array in arrays]
    assert [array[0].shape[1] // TILE for array in rights] == [4, 1, 3, 1, 1]
    spaced = -(-mixed.shape[0] // 256) * 256
    folds = 4
    full = (tiles, experts, size, TILE)
    dma = pltpu.SemaphoreType.DMA
    half = jnp.bfloat16
    return pl.pallas_call(
        functools.partial(tail_kernel, experts, places),
        out_shape=(
            jax.ShapeDtypeStruct((folds * size, TILE), jnp.float32),
            jax.ShapeDtypeStruct((size, 4 * TILE), jnp.float32),
            jax.ShapeDtypeStruct((size, 6 * TILE), jnp.float32),
            jax.ShapeDtypeStruct((size, 2 * TILE), jnp.float32),
            jax.ShapeDtypeStruct(norms.shape, jnp.float32),
            jax.ShapeDtypeStruct(block_in.shape, jnp.float32),
            jax.ShapeDtypeStruct(block_in.shape, jnp.float32),
        ),
        in_specs=[pl.BlockSpec(memory_space=pltpu.VMEM)] * (len(inputs) + 7),
        out_specs=(pl.BlockSpec(memory_space=pltpu.VMEM),) * 7,
        scratch_shapes=[
            pltpu.VMEM((tiles, 2) + full[1:], half),
            pltpu.VMEM(full, half),
            pltpu.VMEM(full, half),
            pltpu.VMEM((experts, tiles, size, TILE), half),
            pltpu.VMEM((experts - 1, tiles, size, TILE), half),
            pltpu.VMEM((shards - 1,) + norms.shape, jnp.float32),
            pltpu.VMEM(norms.shape, jnp.float32),
            pltpu.VMEM((experts - 1,) + norms.shape, jnp.float32),
            dma((2 * tiles,)),
            dma((2 * tiles,)),
            dma((tiles,)),
            dma((tiles,)),
            dma((len(group_chunks(tiles)) * (experts - 1),)),
            dma((len(group_chunks(tiles)) * (experts - 1),)),
            dma((shards - 1,)),
            dma((shards - 1,)),
            dma((experts - 1,)),
            dma((experts - 1,)),
            pltpu.VMEM((2, 4, size, TILE), jnp.float32),
            pltpu.VMEM((4, size, TILE), jnp.float32),
            dma,
            dma,
            pltpu.VMEM((2 * spaced, mixed.shape[1] // 2), half),
            pltpu.VMEM((spaced, mixed.shape[1]), half),
            pltpu.VMEM((tiles, experts, shards, size, TILE), half),
            pltpu.VMEM(norms.shape, jnp.float32),
            pltpu.VMEM((2,) + norms.shape, jnp.float32),
            dma((3,)),
            dma((3,)),
            pltpu.VMEM((spaced, mixed.shape[1]), half),
            pltpu.VMEM((spaced, width), half),
            pltpu.VMEM((spaced, width), jnp.float32),
        ],
        compiler_params=pltpu.CompilerParams(
            collective_id=0, has_side_effects=True, vmem_limit_bytes=58 * 2**20
        ),
        cost_estimate=pl.CostEstimate(
            flops=10**7, bytes_accessed=10**7, transcendentals=0
        ),
    )(*inputs, mixed, grad_att, weight, block_in, gain, grad_hidden, norms)


def on_device(
    tokens,
    cotangent,
    norm_gains,
    norm_biases,
    qkv_weight,
    out_weight,
    dense_in,
    dense_out,
    expert_in,
    expert_out,
    routes,
    gates,
):
    rows = SEQ
    width = tokens.shape[1]
    experts = lax.axis_size("experts")
    shards = lax.axis_size("dp")
    capacity = 2 * rows // experts
    padded = -(-capacity // 8) * 8
    slots = experts * padded
    section = lax.axis_index("section")
    group = lax.axis_index("experts")
    shard = lax.axis_index("dp")
    first = section == 0

    def ordered(mine, other, axis):
        return jnp.concatenate(
            [jnp.where(first, mine, other), jnp.where(first, other, mine)], axis=axis
        )

    def kept_half(array, axis):
        low, high = jnp.split(array, 2, axis=axis)
        return jnp.where(first, low, high)

    def sent_half(array, axis):
        low, high = jnp.split(array, 2, axis=axis)
        return jnp.where(first, high, low)

    def both(own):
        other = pair(own)
        return (jnp.where(first, own, other), jnp.where(first, other, own))

    def across(array, mask):
        return lax.ppermute(array, "dp", [(i, i ^ mask) for i in range(shards)])

    def shifted(array, step):
        return lax.ppermute(
            array, "experts", [(i, (i + step) % experts) for i in range(experts)]
        )

    def wide(array):
        return array.astype(jnp.float32)

    def shard_sum(block, near, far):
        passed = across(block(3).astype(jnp.bfloat16), near)
        direct = across(block(near).astype(jnp.bfloat16), near)
        turned = across((block(far) + wide(passed)).astype(jnp.bfloat16), far)
        return block(0) + wide(direct) + wide(turned)

    def group_sum(array):
        own = lax.dynamic_index_in_dim(array, group, 0, False)
        total = wide(own)
        for step in range(1, experts):
            target = lax.rem(group + step, experts)
            total = total + wide(
                shifted(lax.dynamic_index_in_dim(array, target, 0, False), step)
            )
        return total

    def everyone_sum(left, right, near, far):
        blocks = left.reshape(experts, shards, -1, left.shape[1])

        def block(mask):
            part = lax.dynamic_index_in_dim(blocks, shard ^ mask, 1, False)
            return matmul(part.reshape(-1, left.shape[1]), right)

        total = shard_sum(block, near, far).astype(jnp.bfloat16)
        return group_sum(total.reshape(experts, -1, right.shape[1]))

    def padded_rows(array):
        return jnp.pad(array, ((0, -array.shape[0] % 256), (0, 0)))

    def joined(own, other):
        return jnp.concatenate([padded_rows(own), padded_rows(other)], axis=0)

    kernel_fits = experts == 4 and shards == 4

    def partial_grad(both_sides):
        left, right = both_sides
        if kernel_fits:
            return ((left, pair(left)), (kept_half(right, 1), pair(sent_half(right, 1))))
        left = joined(left, pair(left))
        right = joined(kept_half(right, 1), pair(sent_half(right, 1)))
        return (left.T, right)

    qkv_zero, qkv_one = both(qkv_weight[0])
    norms_zero, norms_one = both(jnp.concatenate([norm_gains[0], norm_biases[0]], axis=0))
    out_zero, out_one = both(out_weight[0])

    def own_block(array):
        return lax.dynamic_slice_in_dim(array, section * rows, rows, 0)

    block_in = own_block(tokens)
    grad_top = own_block(cotangent).astype(jnp.float32)
    chosen = own_block(routes)
    gate_pair = own_block(gates)

    flat = jnp.concatenate([chosen[:, 0], chosen[:, 1]])
    order = jnp.arange(2 * rows, dtype=jnp.int32)
    place = jnp.sum(
        ((flat[:, None] == flat[None, :]) & (order[None, :] < order[:, None])).astype(jnp.int32),
        axis=1,
        dtype=jnp.int32,
    )
    step_of = lax.rem(flat - group + experts, experts)
    slot = jnp.where(place < capacity, step_of * padded + place, slots)
    gate_flat = jnp.concatenate([gate_pair[:, 0], gate_pair[:, 1]])
    spread = (jnp.arange(slots, dtype=jnp.int32)[:, None] == slot[None, :]).astype(jnp.bfloat16)
    spread_both = spread[:, :rows] + spread[:, rows:]

    def sent_out(array):
        parts = [array[k * padded : (k + 1) * padded] for k in range(experts)]
        return jnp.concatenate([parts[0]] + [shifted(parts[k], k) for k in range(1, experts)])

    def sent_home(array):
        parts = [array[k * padded : (k + 1) * padded] for k in range(experts)]
        return jnp.concatenate(
            [parts[0]] + [shifted(parts[k], experts - k) for k in range(1, experts)]
        )

    doubled = (jnp.concatenate([grad_top, grad_top]) * gate_flat[:, None]).astype(jnp.bfloat16)
    grad_outgoing = matmul(spread, doubled).astype(jnp.bfloat16)

    piece_in = kept_half(expert_in[0], 1)
    piece_back = kept_half(expert_out[0], 0)
    near = lax.all_gather(jnp.concatenate([piece_in.T, piece_back], axis=0), "dp", axis=0)

    normed0, mixed0, logsum0, attended0, hidden0, second0 = front_half(
        block_in, norms_zero[:2], norms_zero[2:], qkv_zero, out_zero
    )
    grad_outgoing, second0 = lax.optimization_barrier((grad_outgoing, second0))
    grad_pieces = [grad_outgoing[k * padded : (k + 1) * padded] for k in range(experts)]
    grad_pieces = grad_pieces[:1] + [shifted(grad_pieces[k], k) for k in range(1, experts)]
    before0 = matmul(second0, dense_in)
    active0 = jax.nn.gelu(before0).astype(jnp.bfloat16)
    middle = rounded(hidden0 + matmul(active0, dense_out))
    middle, grad_pieces[1] = lax.optimization_barrier((middle, grad_pieces[1]))

    normed1, mixed1, logsum1, attended1, hidden1, second1 = front_half(
        middle, norms_one[:2], norms_one[2:], qkv_one, out_one
    )
    second1, grad_pieces = lax.optimization_barrier((second1, grad_pieces))
    grad_rows = jnp.concatenate(grad_pieces)
    rows_in = sent_out(matmul(spread_both, second1).astype(jnp.bfloat16))

    near, rows_in = lax.optimization_barrier((near, rows_in))
    gathered = (near, pair(near))
    hidden_share = piece_back.shape[0]
    weights_in = [both[:, :hidden_share].reshape(-1, width) for both in gathered]
    weights_back = [both[:, hidden_share:].reshape(-1, width) for both in gathered]
    before1 = [matmul_cols(rows_in, weight) for weight in weights_in]
    active1 = [jax.nn.gelu(before).astype(jnp.bfloat16) for before in before1]
    grad_before1 = [
        gelu_back(before, matmul_cols(grad_rows, weight)).astype(jnp.bfloat16)
        for before, weight in zip(before1, weights_back)
    ]
    grad_arrived = (
        matmul(grad_before1[0], weights_in[0]) + matmul(grad_before1[1], weights_in[1])
    ).astype(jnp.bfloat16)
    grad_home = sent_home(grad_arrived)
    returned = (
        matmul(active1[0], weights_back[0]) + matmul(active1[1], weights_back[1])
    ).astype(jnp.bfloat16)
    returned_home = sent_home(returned)

    def expert_parts(halves, right):
        landed = [pair(half) for half in halves]
        lefts = [
            jnp.concatenate([halves[0], landed[1]], axis=0),
            jnp.concatenate([halves[1], landed[0]], axis=0),
        ]
        right = jnp.concatenate([kept_half(right, 1), pair(sent_half(right, 1))], axis=0)
        return [
            with_layout_constraint(
                matmul_rows(left, right).astype(jnp.bfloat16), Layout(major_to_minor=(0, 1))
            )
            for left in lefts
        ]

    expert_in_parts = expert_parts(grad_before1, rows_in)
    expert_out_parts = expert_parts(active1, grad_rows)
    expert_stack = jnp.concatenate(expert_in_parts + expert_out_parts, axis=1)
    grad_home, expert_stack = lax.optimization_barrier((grad_home, expert_stack))
    expert_shard = lax.psum_scatter(expert_stack, "dp", scatter_dimension=0, tiled=True)
    parts = jnp.split(expert_shard, 4, axis=1)
    expert_in_sum = ordered(parts[0], parts[1], 0).astype(jnp.float32)
    expert_out_sum = ordered(parts[2], parts[3], 0).astype(jnp.float32)

    picked = matmul_rows(spread, returned_home) * gate_flat[:, None]
    final = (hidden1 + (picked[:rows] + picked[rows:])).astype(jnp.bfloat16)
    grad_second1 = matmul_rows(spread_both, grad_home)
    grad_middle, grad_norm1, grad_mixed1, grad_cast1 = front_back(
        middle,
        (normed1, mixed1, logsum1, attended1, hidden1),
        grad_top,
        grad_second1,
        norms_one[:2],
        norms_one[2:],
        qkv_one,
        out_one,
    )

    grad_result = rounded(grad_middle)
    grad_before0 = gelu_back(before0, matmul_cols(grad_result, dense_out)).astype(jnp.bfloat16)
    dense_out_part = partial_grad((active0, grad_result))
    dense_in_part = partial_grad((second0, grad_before0))
    qkv_part1 = partial_grad((normed1, grad_mixed1))
    out_part1 = partial_grad((attended1, grad_cast1))
    grad_second0 = matmul_cols(grad_before0, dense_in)
    saved0 = (normed0, mixed0, logsum0, attended0, hidden0)
    if not kernel_fits:
        grad_tokens, grad_norm0, grad_mixed0, grad_cast0 = front_back(
            block_in,
            saved0,
            grad_result.astype(jnp.float32),
            grad_second0,
            norms_zero[:2],
            norms_zero[2:],
            qkv_zero,
            out_zero,
        )
        qkv_part0 = partial_grad((normed0, grad_mixed0))
    else:
        grad_mid0, gain_two0, bias_two0 = norm_back(
            hidden0, norms_zero[1], norms_zero[3], grad_second0
        )
        grad_hidden0 = grad_result.astype(jnp.float32) + grad_mid0
        grad_cast0 = grad_hidden0.astype(jnp.bfloat16)
        grad_att0 = matmul_cols(grad_cast0, out_zero).astype(jnp.bfloat16)
        nothing = jnp.zeros_like(gain_two0)
        grad_norm0 = jnp.stack([nothing, gain_two0, nothing, bias_two0])
    out_part0 = partial_grad((attended0, grad_cast0))
    norm_pair = jnp.where(first, grad_norm0, grad_norm1) + pair(
        jnp.where(first, grad_norm1, grad_norm0)
    )
    rest = [dense_in_part, qkv_part1, out_part1]
    if kernel_fits:
        eight = jnp.zeros((8, width), jnp.float32)
        dense_out_sum, dense_in_sum, qkv_sum, out_sum, norm_sum, grad_tokens, grad_landed = tail_sums(
            experts,
            shards,
            [dense_in_part, dense_out_part, qkv_part1, out_part1, out_part0],
            (normed0, pair(normed0)),
            mixed0,
            grad_att0,
            qkv_zero,
            block_in,
            eight.at[0].set(norms_zero[0]),
            grad_hidden0,
            eight.at[:4].set(norm_pair),
        )
        size = width // (experts * shards)
        norm_sum = lax.dynamic_slice(norm_sum[:4], (0, (group * shards + shard) * size), (4, size))
        middle_landed = pair(grad_middle)
        act_grads = jnp.concatenate(
            [
                jnp.where(first, grad_tokens, middle_landed),
                jnp.where(first, grad_landed, grad_middle),
            ]
        )
    else:
        dense_out_sum = everyone_sum(*dense_out_part, 1, 2)
        dense_in_sum, qkv_one, out_one, qkv_zero, out_zero = [
            everyone_sum(*part, 2, 1).astype(jnp.bfloat16)
            for part in rest + [qkv_part0, out_part0]
        ]
        own_shared, other_shared = [
            jnp.where(first, *halves)
            for halves in (
                (
                    jnp.concatenate([qkv_zero, out_zero], axis=1),
                    jnp.concatenate([qkv_one, out_one], axis=1),
                ),
                (
                    jnp.concatenate([qkv_one, out_one], axis=1),
                    jnp.concatenate([qkv_zero, out_zero], axis=1),
                ),
            )
        ]
        other_shared = pair(other_shared)
        cut = qkv_zero.shape[1]
        qkv_sum = ordered(own_shared[:, :cut], other_shared[:, :cut], 1).astype(jnp.float32)
        out_sum = ordered(own_shared[:, cut:], other_shared[:, cut:], 1).astype(jnp.float32)
        dense_in_sum = dense_in_sum.astype(jnp.float32)
        norm_sum = lax.psum_scatter(
            norm_pair.T, ("experts", "dp"), scatter_dimension=0, tiled=True
        ).T
        act_grads = ordered(
            jnp.where(first, grad_tokens, grad_middle),
            pair(jnp.where(first, grad_middle, grad_tokens)),
            0,
        )

    acts = ordered(
        jnp.where(first, middle, final), pair(jnp.where(first, final, middle)), 0
    )
    return (
        acts[None],
        act_grads[None],
        qkv_sum[None],
        out_sum[None],
        norm_sum[:2][None],
        norm_sum[2:][None],
        dense_in_sum,
        dense_out_sum,
        expert_in_sum.T[None],
        expert_out_sum[None],
    )


def solution(mesh):
    placed = (
        P(("experts", "dp"), None),
        P(("experts", "dp"), None),
        P("section", None, None),
        P("section", None, None),
        P("section", None, None),
        P("section", None, None),
        P(),
        P(),
        P("experts", None, "dp"),
        P("experts", "dp", None),
        P(("experts", "dp"), None),
        P(("experts", "dp"), None),
    )
    return jax.shard_map(
        on_device,
        mesh=mesh,
        in_specs=placed,
        out_specs=(
            P("section", ("experts", "dp"), None),
            P("section", ("experts", "dp"), None),
            P("section", ("experts", "dp"), None),
            P("section", ("experts", "dp"), None),
            P("section", None, ("experts", "dp")),
            P("section", None, ("experts", "dp")),
            P(("experts", "dp"), "section"),
            P(("experts", "dp"), "section"),
            P("experts", "section", "dp"),
            P("experts", "dp", "section"),
        ),
        check_vma=False,
    )
```
